256 devices in a mesh: row: 32 (over z, y_lo, core), col: 8 (over y_hi, x).
Axes of the slice: x: 4, y: 4 (y_hi: 2, y_lo: 2; y = y_hi * 2 + y_lo), z: 8, core: 2. Of those that a mesh axis runs over, the one named last changes fastest.
Arguments:
- source: float32 [8192, 8192], P('row', 'col'), may hold values from 0.25 to 4
- boxes_a: float32 [32, 32, 512, 512], P('row', 'col'), may hold values from 0.25 to 4
- shifts_a: int32 [32, 32, 2], P('row', 'col'), may hold values from -128 to -1
- widths_a: int32 [32, 32, 2], P('row', 'col'), may hold values from 256 to 512
- boxes_b: float32 [32, 32, 512, 512], P('row', 'col'), may hold values from 0.25 to 4
- shifts_b: int32 [32, 32, 2], P('row', 'col'), may hold values from -128 to -1
- widths_b: int32 [32, 32, 2], P('row', 'col'), may hold values from 256 to 512
Outputs:
- smoothed: float32 [8192, 8192], P('row', 'col')
The draws below stay inside these ranges and needn't reach their ends.
Inputs may be any that keep to these rules, and one draw needn't show every extreme that they name: `shifts_a`: first entry: rows, second: columns. `widths_a`: first entry: rows, second: columns. `shifts_b`: first entry: rows, second: columns. `widths_b`: first entry: rows, second: columns.
All inputs are finite; a program needn't handle non-finite values.
Results may differ from the reference program's by a relative error of at most 0.0003.
Values sent between devices are 32-bit elements; how exact they have to be, the bound alone decides.
No kernel may reach another device: no remote copies, remote signals or barrier semaphores. Data moves between devices by JAX's collectives and lax.ppermute only.
A program may use at most 64 MiB of HBM per device.

```python
import math
import jax
import jax.numpy as jnp
from jax import lax

S = 256
BOX = 512
ITERS = 3
RADIUS = 8
CELL_ROWS = 32
CELL_COLS = 32
NR = 8192
NC = 8192


def place_ends(array, stream_key, least, largest):
    index_at = [jax.random.randint(jax.random.fold_in(stream_key, axis), (), 0, length) for axis, length in enumerate(array.shape)]
    widest = array.shape.index(max(array.shape))
    neighbour = index_at[:widest] + [(index_at[widest] + 1) % array.shape[widest]] + index_at[widest + 1:]
    return array.at[tuple(index_at)].set(least).at[tuple(neighbour)].set(largest)


def steps_of(stream_key, extent, pieces, least, largest):
    level, own = 1.0, jax.random.fold_in(stream_key, 6)
    for dim, parts in pieces:
        steps = jnp.exp(jax.random.uniform(jax.random.fold_in(own, dim), (parts,), jnp.float32, least / len(pieces), largest / len(pieces)))
        level = level * jnp.repeat(steps, extent[dim] // parts).reshape([-1 if axis == dim else 1 for axis in range(len(extent))])
    return level


def setup_inputs(seed: int = 0) -> dict:
    arg_keys = jax.random.split(jax.random.key(seed), 8)
    return {
        "source": jnp.clip(jnp.exp(math.log(4.0) - 2.7725887 * jax.random.uniform(arg_keys[0], (NR, NC), jnp.float32) ** steps_of(arg_keys[0], (NR, NC), ((0, 32), (1, 8)), -0.2, 0.2)), 0.25, 4.0),
        "boxes_a": jnp.clip(jnp.exp(math.log(4.0) - 2.7725887 * jax.random.uniform(arg_keys[1], (CELL_ROWS, CELL_COLS, BOX, BOX), jnp.float32) ** steps_of(arg_keys[1], (CELL_ROWS, CELL_COLS, BOX, BOX), ((0, 32), (1, 8)), -0.2, 0.2)), 0.25, 4.0),
        "shifts_a": place_ends(jax.random.randint(arg_keys[2], (CELL_ROWS, CELL_COLS, 2), 0 - S // 2, 0), jax.random.fold_in(arg_keys[2], 1), 0 - S // 2, -1).astype(jnp.int32),
        "widths_a": place_ends(jax.random.randint(arg_keys[3], (CELL_ROWS, CELL_COLS, 2), S, 2 * S + 1), jax.random.fold_in(arg_keys[3], 1), S, 2 * S).astype(jnp.int32),
        "boxes_b": jnp.clip(jnp.exp(math.log(4.0) - 2.7725887 * jax.random.uniform(arg_keys[4], (CELL_ROWS, CELL_COLS, BOX, BOX), jnp.float32) ** steps_of(arg_keys[4], (CELL_ROWS, CELL_COLS, BOX, BOX), ((0, 32), (1, 8)), -0.2, 0.2)), 0.25, 4.0),
        "shifts_b": place_ends(jax.random.randint(arg_keys[5], (CELL_ROWS, CELL_COLS, 2), 0 - S // 2, 0), jax.random.fold_in(arg_keys[5], 1), 0 - S // 2, -1).astype(jnp.int32),
        "widths_b": place_ends(jax.random.randint(arg_keys[6], (CELL_ROWS, CELL_COLS, 2), S, 2 * S + 1), jax.random.fold_in(arg_keys[6], 1), S, 2 * S).astype(jnp.int32),
    }


kernel_eps = 0.05
blur_sigma = 2.0


def table(patch_displacement):
    rows = jnp.arange(S, dtype=jnp.int32)
    cols = jnp.arange(BOX, dtype=jnp.int32)
    dist = (patch_displacement + cols[None, :] - rows[:, None]).astype(jnp.float32) / S
    return jnp.exp(-dist * dist / kernel_eps).astype(jnp.bfloat16)


def masked(patch_rectangle, patch_extent):
    index = jnp.arange(BOX, dtype=jnp.int32)
    keep_rows = (index < patch_extent[0]).astype(jnp.float32)
    keep_cols = (index < patch_extent[1]).astype(jnp.float32)
    return patch_rectangle * keep_rows[:, None] * keep_cols[None, :]


def apply_back(horizontal_kernel_grid, vertical_kernel_grid, multiplier_array):
    inner = jnp.dot(horizontal_kernel_grid.T, multiplier_array.astype(jnp.bfloat16), preferred_element_type=jnp.float32)
    return jnp.dot(inner.astype(jnp.bfloat16), vertical_kernel_grid, preferred_element_type=jnp.float32)


def apply_fwd(horizontal_kernel_grid, vertical_kernel_grid, multiplier_array):
    inner = jnp.dot(horizontal_kernel_grid, multiplier_array.astype(jnp.bfloat16), preferred_element_type=jnp.float32)
    return jnp.dot(inner.astype(jnp.bfloat16), vertical_kernel_grid.T, preferred_element_type=jnp.float32)


def entropic_transport_iterate(probability_measure, patch_rectangle, patch_displacement, patch_extent, initial_corner_index):
    horizontal_kernel_grid = table(patch_displacement[0])
    vertical_kernel_grid = table(patch_displacement[1])
    target = masked(patch_rectangle, patch_extent)
    multiplier_array = initial_corner_index
    lagrange_multiplier_field = target
    for step in range(ITERS):
        lagrange_multiplier_field = target / apply_back(horizontal_kernel_grid, vertical_kernel_grid, multiplier_array)
        multiplier_array = probability_measure / apply_fwd(horizontal_kernel_grid, vertical_kernel_grid, lagrange_multiplier_field)
    return multiplier_array, lagrange_multiplier_field, horizontal_kernel_grid, vertical_kernel_grid


def section_first(probability_measure, patch_rectangle, patch_displacement, patch_extent):
    multiplier_array, lagrange_multiplier_field, horizontal_kernel_grid, vertical_kernel_grid = entropic_transport_iterate(probability_measure, patch_rectangle, patch_displacement, patch_extent, jnp.ones_like(probability_measure))
    return multiplier_array


def section_second(probability_measure, initial_corner_index, patch_rectangle, patch_displacement, patch_extent):
    multiplier_array, lagrange_multiplier_field, horizontal_kernel_grid, vertical_kernel_grid = entropic_transport_iterate(probability_measure, patch_rectangle, patch_displacement, patch_extent, initial_corner_index)
    return lagrange_multiplier_field * apply_back(horizontal_kernel_grid, vertical_kernel_grid, multiplier_array)


def blur_pairs():
    raw = [math.exp(-(step * step) / (2.0 * blur_sigma * blur_sigma)) for step in range(-RADIUS, RADIUS + 1)]
    total = sum(raw)
    return [(step, raw[step + RADIUS] / total) for step in range(-RADIUS, RADIUS + 1)]


def to_cells(field):
    return field.reshape(CELL_ROWS, S, CELL_COLS, S).transpose(0, 2, 1, 3)


def from_cells(cells):
    return cells.transpose(0, 2, 1, 3).reshape(NR, NC)


def reference(source, boxes_a, shifts_a, widths_a, boxes_b, shifts_b, widths_b):
    half = S // 2
    first = lax.map(lambda row: jax.vmap(section_first)(*row), (to_cells(source), boxes_a, shifts_a, widths_a))
    u_first = from_cells(first)
    u_moved = jnp.roll(u_first, (-half, -half), (0, 1))
    mass_moved = jnp.roll(source, (-half, -half), (0, 1))
    plans = lax.map(lambda row: jax.vmap(section_second)(*row),
                    (to_cells(mass_moved), to_cells(u_moved), boxes_b, shifts_b, widths_b))
    canvas = jnp.zeros((NR + 2 * S, NC + 2 * S), jnp.float32)

    def place(index, canvas):
        cell_row = index // CELL_COLS
        cell_col = index % CELL_COLS
        plan = plans[cell_row, cell_col]
        top = (cell_row * S + half + shifts_b[cell_row, cell_col, 0]).astype(jnp.int32)
        left = (cell_col * S + half + shifts_b[cell_row, cell_col, 1]).astype(jnp.int32)
        region = lax.dynamic_slice(canvas, (top, left), (BOX, BOX))
        return lax.dynamic_update_slice(canvas, region + plan, (top, left))

    canvas = lax.fori_loop(0, CELL_ROWS * CELL_COLS, place, canvas)
    folded = canvas[:NR].at[:2 * S].add(canvas[NR:])
    gathered = folded[:, :NC].at[:, :2 * S].add(folded[:, NC:])
    row_smooth = jnp.zeros_like(gathered)
    for step, weight in blur_pairs():
        row_smooth = row_smooth + weight * jnp.roll(gathered, -step, 0)
    smoothed = jnp.zeros_like(gathered)
    for step, weight in blur_pairs():
        smoothed = smoothed + weight * jnp.roll(row_smooth, -step, 1)
    return smoothed
```

```python
import functools
import math

import jax
import jax.numpy as jnp
from jax import lax
from jax.experimental import pallas as pl
from jax.experimental.pallas import tpu as pltpu
from jax.sharding import PartitionSpec as P

S = 256
HALF = 128
BOX = 512
ITERS = 3
RADIUS = 8
REACH = BOX + HALF
EPS = 0.05
SIGMA = 2.0
F32 = jnp.float32
BF16 = jnp.bfloat16


def dot(a, b):
    return jnp.dot(a, b, preferred_element_type=F32)


def gauss(shape, first):
    rows = lax.broadcasted_iota(jnp.int32, shape, 0)
    cols = lax.broadcasted_iota(jnp.int32, shape, 1)
    dist = (rows - cols + first).astype(F32) / S
    return jnp.exp(-dist * dist / EPS)


def fill_tables(tall_ref, wide_ref):
    tall_ref[REACH:] = jnp.zeros((8, S), F32)
    for c in range(0, REACH, HALF):
        tall_ref[c : c + HALF] = gauss((HALF, S), c - HALF)
    wide_ref[S + HALF :] = jnp.zeros((8, BOX), F32)
    for c in range(0, S + HALF, HALF):
        wide_ref[c : c + HALF] = gauss((HALF, BOX), c)


def window(ref, start, size):
    base = pl.multiple_of(start // 8 * 8, 8)
    rest = start - base
    width = ref.shape[1]
    tiles = ref[pl.ds(base, size + 8), :].reshape(size // 8 + 1, 8, width)
    turned = pltpu.roll(tiles, jnp.where(rest == 0, 0, 8 - rest), 1)
    row = lax.broadcasted_iota(jnp.int32, (size // 8, 8, width), 1)
    return jnp.where(row < 8 - rest, turned[:-1], turned[1:]).reshape(size, width)


def cell_tables(offsets, widths, tall_ref, wide_ref):
    o_r, o_c = offsets
    w_r, w_c = widths
    lane = lax.broadcasted_iota(jnp.int32, (S, BOX), 1)
    deep = lax.broadcasted_iota(jnp.int32, (BOX, S), 0)
    back_r = window(tall_ref, o_r + HALF, BOX).astype(BF16)
    back_c = window(wide_ref, -o_c, S).astype(BF16)
    fwd_r = jnp.where(lane < w_r, window(wide_ref, -o_r, S), 0.0).astype(BF16)
    fwd_c = jnp.where(deep < w_c, window(tall_ref, o_c + HALF, BOX), 0.0).astype(BF16)
    return back_r, back_c, fwd_r, fwd_c


def forward(mass, fwd_r, fwd_c, vb_ref):
    inner = dot(fwd_r, vb_ref[...]).astype(BF16)
    return mass / dot(inner, fwd_c)


def aligned_kernel(shifts, widths, source_ref, box_ref, top_ref, bot_ref, ltop_ref, lbot_ref,
                   tall_ref, wide_ref, vb_ref, tb):
    j = pl.program_id(0)

    @pl.when(j == 0)
    def _():
        fill_tables(tall_ref, wide_ref)

    back_r, back_c, fwd_r, fwd_c = cell_tables(
        (shifts[j, 0], shifts[j, 1]), (widths[j, 0], widths[j, 1]), tall_ref, wide_ref)
    br_ref, bc_ref, fr_ref, fc_ref = tb
    br_ref[...] = back_r
    bc_ref[...] = back_c
    fr_ref[...] = fwd_r
    fc_ref[...] = fwd_c
    mass = source_ref[...]
    down = 1.0 / dot(br_ref[...], jnp.ones((S, HALF), BF16)).astype(BF16).astype(F32)
    across = 1.0 / dot(jnp.ones((8, S), BF16), bc_ref[...])
    down = down[:, :1]
    across = across[:1]
    for c in range(0, BOX, HALF):
        vb_ref[c : c + HALF] = (box_ref[c : c + HALF] * down[c : c + HALF] * across).astype(BF16)
    u = forward(mass, fr_ref[...], fc_ref[...], vb_ref)
    for _ in range(ITERS - 1):
        inner = dot(br_ref[...], u.astype(BF16)).astype(BF16)
        den = dot(inner, bc_ref[...])
        vb_ref[...] = (box_ref[...] / den).astype(BF16)
        u = forward(mass, fr_ref[...], fc_ref[...], vb_ref)
    top_ref[...] = u[:HALF]
    bot_ref[...] = u[HALF:]

    @pl.when(j == 0)
    def _():
        ltop_ref[...] = u[:HALF, :HALF]
        lbot_ref[...] = u[HALF:, :HALF]


def aligned(source, boxes, shifts, widths):
    cells = boxes.shape[0]
    smem = pl.BlockSpec(memory_space=pltpu.SMEM)
    return pl.pallas_call(
        aligned_kernel,
        grid=(cells,),
        in_specs=[
            smem,
            smem,
            pl.BlockSpec((S, S), lambda j: (0, j)),
            pl.BlockSpec((None, BOX, BOX), lambda j: (j, 0, 0)),
        ],
        out_specs=[
            pl.BlockSpec((HALF, S), lambda j: (0, j)),
            pl.BlockSpec((HALF, S), lambda j: (0, j)),
            pl.BlockSpec((HALF, HALF), lambda j: (0, 0)),
            pl.BlockSpec((HALF, HALF), lambda j: (0, 0)),
        ],
        out_shape=[
            jax.ShapeDtypeStruct((HALF, cells * S), F32),
            jax.ShapeDtypeStruct((HALF, cells * S), F32),
            jax.ShapeDtypeStruct((HALF, HALF), F32),
            jax.ShapeDtypeStruct((HALF, HALF), F32),
        ],
        scratch_shapes=[
            pltpu.VMEM((REACH + 8, S), F32),
            pltpu.VMEM((S + HALF + 8, BOX), F32),
            pltpu.VMEM((BOX, BOX), BF16),
            [
                pltpu.VMEM((BOX, S), BF16),
                pltpu.VMEM((S, BOX), BF16),
                pltpu.VMEM((S, BOX), BF16),
                pltpu.VMEM((BOX, S), BF16),
            ],
        ],
        compiler_params=pltpu.CompilerParams(vmem_limit_bytes=48 << 20),
        name="aligned",
    )(shifts, widths, source, boxes)


REAR = RADIUS + S + RADIUS
SPILL = REACH - 2 * S + RADIUS
WIDE = HALF + S


def shifted_kernel(shifts, widths, ubot_ref, utop_ref, ueast_ref, udiag_ref, mbot_ref, mtop_ref,
                   meast_ref, mdiag_ref, box_ref, own_ref, next_ref, far_ref, back_ref,
                   tall_ref, wide_ref, vb_ref, v_ref, u_ref, mass_ref, canvas_ref, tb, sems):
    j = pl.program_id(0)
    cells = pl.num_programs(0)
    span = ubot_ref.shape[1]

    @pl.when(j == 0)
    def _():
        fill_tables(tall_ref, wide_ref)
        canvas_ref[...] = jnp.zeros_like(canvas_ref)
        for ref, bot, top, east, diag in (
            (u_ref, ubot_ref, utop_ref, ueast_ref, udiag_ref),
            (mass_ref, mbot_ref, mtop_ref, meast_ref, mdiag_ref),
        ):
            ref[:HALF, :span] = bot[...]
            ref[HALF:, :span] = top[...]
            ref[:HALF, span:] = east[...]
            ref[HALF:, span:] = diag[...]

    o_r, o_c = shifts[j, 0], shifts[j, 1]
    w_r, w_c = widths[j, 0], widths[j, 1]
    back_r, back_c, fwd_r, fwd_c = cell_tables((o_r, o_c), (w_r, w_c), tall_ref, wide_ref)
    br_ref, bc_ref, fr_ref, fc_ref = tb
    br_ref[...] = back_r
    bc_ref[...] = back_c
    fr_ref[...] = fwd_r
    fc_ref[...] = fwd_c
    here = pl.ds(pl.multiple_of(j * S + HALF, HALF), S)
    mass = mass_ref[:, here]
    u = u_ref[:, here]
    for step in range(ITERS):
        inner = dot(br_ref[...], u.astype(BF16)).astype(BF16)
        v = box_ref[...] / dot(inner, bc_ref[...])
        if step == ITERS - 1:
            v_ref[...] = v
        vb_ref[...] = v.astype(BF16)
        u = forward(mass, fr_ref[...], fc_ref[...], vb_ref)
    deep = lax.broadcasted_iota(jnp.int32, (BOX, S), 0)
    lane = lax.broadcasted_iota(jnp.int32, (S, BOX), 1)
    inner = jnp.where(deep < w_r, dot(br_ref[...], u.astype(BF16)), 0.0).astype(BF16)
    last_c = jnp.where(lane < w_c, bc_ref[...], jnp.zeros((), BF16))
    v_ref[...] = v_ref[...] * dot(inner, last_c)
    top = o_r + HALF
    left = o_c + HALF
    base = pl.multiple_of(top // 8 * 8, 8)
    rest = top - base
    for c in range(0, BOX, HALF):
        tiles = v_ref[c : c + HALF].reshape(HALF // 8, 8, BOX)
        turned = pltpu.roll(tiles, rest, 1)
        none = jnp.zeros((1, 8, BOX), F32)
        row = lax.broadcasted_iota(jnp.int32, (HALF // 8 + 1, 8, BOX), 1)
        rows = jnp.where(
            row < rest,
            jnp.concatenate([none, turned], 0),
            jnp.concatenate([turned, none], 0),
        ).reshape(HALF + 8, BOX)
        before = jnp.zeros((HALF + 8, HALF), F32)
        column = lax.broadcasted_iota(jnp.int32, (HALF + 8, HALF), 1)
        for k in range(BOX // HALF + 1):
            if k < BOX // HALF:
                now = pltpu.roll(rows[:, k * HALF : (k + 1) * HALF], left, 1)
            else:
                now = jnp.zeros((HALF + 8, HALF), F32)
            at = (pl.ds(base + c, HALF + 8), pl.ds(pl.multiple_of(j * S + k * HALF, HALF), HALF))
            canvas_ref[at] = canvas_ref[at] + jnp.where(column < left, before, now)
            before = now

    @pl.when(j == cells - 1)
    def _():
        copies = []
        for k, (ref, first) in enumerate(
            ((own_ref, 0), (next_ref, S - RADIUS), (far_ref, 2 * S - RADIUS), (back_ref, 0))
        ):
            copies.append(
                pltpu.make_async_copy(
                    canvas_ref.at[pl.ds(first, ref.shape[0])], ref, sems.at[k]))
        for copy in copies:
            copy.start()
        for copy in copies:
            copy.wait()


def shifted(boxes, shifts, widths, u, mass):
    cells = boxes.shape[0]
    span = cells * S
    reach = span + WIDE
    smem = pl.BlockSpec(memory_space=pltpu.SMEM)
    vmem = pl.BlockSpec(memory_space=pltpu.VMEM)
    half = pl.BlockSpec((HALF, span), lambda j: (1, 0))
    return pl.pallas_call(
        shifted_kernel,
        grid=(cells,),
        in_specs=[smem, smem] + [vmem] * 4 + [half] + [vmem] * 3
        + [pl.BlockSpec((None, BOX, BOX), lambda j: (j, 0, 0))],
        out_specs=[pl.BlockSpec(memory_space=pl.ANY)] * 4,
        out_shape=[
            jax.ShapeDtypeStruct((S + RADIUS, reach), F32),
            jax.ShapeDtypeStruct((REAR, reach), F32),
            jax.ShapeDtypeStruct((SPILL, reach), F32),
            jax.ShapeDtypeStruct((RADIUS, reach), F32),
        ],
        scratch_shapes=[
            pltpu.VMEM((REACH + 8, S), F32),
            pltpu.VMEM((S + HALF + 8, BOX), F32),
            pltpu.VMEM((BOX, BOX), BF16),
            pltpu.VMEM((BOX, BOX), F32),
            pltpu.VMEM((S, span + HALF), F32),
            pltpu.VMEM((S, span + HALF), F32),
            pltpu.VMEM((REACH + 8, reach), F32),
            [
                pltpu.VMEM((BOX, S), BF16),
                pltpu.VMEM((S, BOX), BF16),
                pltpu.VMEM((S, BOX), BF16),
                pltpu.VMEM((BOX, S), BF16),
            ],
            pltpu.SemaphoreType.DMA((4,)),
        ],
        compiler_params=pltpu.CompilerParams(vmem_limit_bytes=52 << 20),
        name="shifted",
    )(shifts, widths, *u, *mass, boxes)


def blur_weights():
    raw = [math.exp(-(d * d) / (2.0 * SIGMA * SIGMA)) for d in range(-RADIUS, RADIUS + 1)]
    total = sum(raw)
    return [w / total for w in raw]


def rows_kernel(own_ref, next_ref, far_ref, back_ref, main_ref, east_ref, west_ref, win_ref):
    span = main_ref.shape[1]
    win_ref[...] = next_ref[...]
    win_ref[RADIUS:] = win_ref[RADIUS:] + own_ref[...]
    win_ref[:SPILL] = win_ref[:SPILL] + far_ref[...]
    win_ref[REAR - RADIUS :] = win_ref[REAR - RADIUS :] + back_ref[...]
    weights = blur_weights()
    for c in range(0, win_ref.shape[1], HALF):
        col = win_ref[:, c : c + HALF]
        out = weights[RADIUS] * col[RADIUS : RADIUS + S]
        for d in range(1, RADIUS + 1):
            out = out + weights[RADIUS + d] * (
                col[RADIUS + d : RADIUS + d + S] + col[RADIUS - d : RADIUS - d + S])
        if c < span:
            main_ref[:, c : c + HALF] = out
        else:
            east_ref[:S, c - span : c - span + HALF] = out
        if c == 0:
            west_ref[...] = out.T[:RADIUS]
        if c == span - HALF:
            east_ref[S:, :S] = out.T[HALF - RADIUS :]
            east_ref[S:, S:] = jnp.zeros((RADIUS, HALF), F32)


def rows(own, after, far, back):
    span = own.shape[1] - WIDE
    vmem = pl.BlockSpec(memory_space=pltpu.VMEM)
    return pl.pallas_call(
        rows_kernel,
        in_specs=[vmem] * 4,
        out_specs=[vmem] * 3,
        out_shape=[
            jax.ShapeDtypeStruct((S, span), F32),
            jax.ShapeDtypeStruct((S + RADIUS, WIDE), F32),
            jax.ShapeDtypeStruct((RADIUS, S), F32),
        ],
        scratch_shapes=[pltpu.VMEM((REAR, own.shape[1]), F32)],
        compiler_params=pltpu.CompilerParams(vmem_limit_bytes=48 << 20),
        name="rows",
    )(own, after, far, back)


def columns_kernel(main_ref, spill_ref, east_ref, west_ref, out_ref, win_ref):
    span = main_ref.shape[1]
    none = jnp.zeros((HALF - RADIUS, S), F32)
    win_ref[:, :HALF] = jnp.concatenate([none, east_ref[S:, :S]], 0).T
    win_ref[:, HALF : HALF + WIDE] = main_ref[:, :WIDE] + east_ref[:S]
    win_ref[:, HALF + WIDE : HALF + span] = main_ref[:, WIDE:]
    win_ref[:, HALF + span :] = (
        spill_ref[...] + jnp.concatenate([west_ref[...], none], 0).T)
    weights = blur_weights()
    for c in range(0, span, HALF):
        strip = win_ref[:, c : c + 3 * HALF]
        out = weights[RADIUS] * strip[:, HALF : 2 * HALF]
        for d in range(1, RADIUS + 1):
            out = out + weights[RADIUS + d] * (
                strip[:, HALF + d : 2 * HALF + d] + strip[:, HALF - d : 2 * HALF - d])
        out_ref[:, c : c + HALF] = out


def columns(main, spill, east, west):
    vmem = pl.BlockSpec(memory_space=pltpu.VMEM)
    return pl.pallas_call(
        columns_kernel,
        grid=(1,),
        in_specs=[vmem, pl.BlockSpec((S, HALF), lambda j: (0, 0)), vmem, vmem],
        out_specs=vmem,
        out_shape=jax.ShapeDtypeStruct(main.shape, F32),
        scratch_shapes=[pltpu.VMEM((S, main.shape[1] + 2 * HALF), F32)],
        compiler_params=pltpu.CompilerParams(vmem_limit_bytes=48 << 20),
        name="columns",
    )(main, spill, east, west)


def moved(array, by_row, by_col):
    n_row, n_col = lax.axis_size("row"), lax.axis_size("col")
    if by_col == 0:
        return lax.ppermute(array, "row", [(i, (i + by_row) % n_row) for i in range(n_row)])
    if by_row == 0:
        return lax.ppermute(array, "col", [(i, (i + by_col) % n_col) for i in range(n_col)])
    pairs = [
        (r * n_col + c, (r + by_row) % n_row * n_col + (c + by_col) % n_col)
        for r in range(n_row)
        for c in range(n_col)
    ]
    return lax.ppermute(array, ("row", "col"), pairs)


def on_device(source, boxes_a, shifts_a, widths_a, boxes_b, shifts_b, widths_b):
    mtop = moved(source[:HALF], -1, 0)
    meast = moved(source[HALF:, :HALF], 0, -1)
    mdiag = moved(source[:HALF, :HALF], -1, -1)
    top, bot, left_top, left_bot = aligned(source, boxes_a[0], shifts_a[0], widths_a[0])
    utop = moved(top, -1, 0)
    ueast = moved(left_bot, 0, -1)
    udiag = moved(left_top, -1, -1)
    own, after, far, back = shifted(
        boxes_b[0], shifts_b[0], widths_b[0],
        (bot, utop, ueast, udiag), (source, mtop, meast, mdiag))
    main, east, west = rows(own, moved(after, 1, 0), moved(far, 2, 0), moved(back, -1, 0))
    return columns(main, east, moved(east, 0, 1), moved(west, 0, -1))


def solution(mesh):
    cells = P("row", "col", None)
    boxes = P("row", "col", None, None)
    return jax.shard_map(
        on_device,
        mesh=mesh,
        in_specs=(P("row", "col"), boxes, cells, cells, boxes, cells, cells),
        out_specs=P("row", "col"),
        check_vma=False,
    )
```

```python
import functools
import math

import jax
import jax.numpy as jnp
import numpy as np
from jax import lax
from jax.experimental import pallas as pl
from jax.experimental.pallas import tpu as pltpu
from jax.sharding import PartitionSpec as P

S = 256
HALF = 128
BOX = 512
ITERS = 3
RADIUS = 8
REACH = BOX + HALF
EPS = 0.05
SIGMA = 2.0
F32 = jnp.float32
BF16 = jnp.bfloat16
OWN = S + RADIUS
NEXT = S + 2 * RADIUS
FAR = REACH - 2 * S + RADIUS
BASE = 904
VMEM = pl.BlockSpec(memory_space=pltpu.VMEM)
SMEM = pl.BlockSpec(memory_space=pltpu.SMEM)
ANY = pl.BlockSpec(memory_space=pl.ANY)
HBM = pl.BlockSpec(memory_space=pltpu.HBM)
PARAMS = pltpu.CompilerParams(vmem_limit_bytes=40 << 20)


def dot(a, b):
    return jnp.dot(a, b, preferred_element_type=F32)


def fill_base(ref):
    for c in range(0, BASE, 8 * 28):
        n = min(8 * 28, BASE - c)
        rows = lax.broadcasted_iota(jnp.int32, (n, HALF), 0)
        cols = lax.broadcasted_iota(jnp.int32, (n, HALF), 1)
        dist = (rows - cols + (c - 384)).astype(F32) / S
        ref[c : c + n] = jnp.exp(-dist * dist / EPS)


def window(ref, start):
    base = pl.multiple_of(start // 8 * 8, 8)
    rest = start - base
    tiles = ref[pl.ds(base, REACH + 8), :].reshape(REACH // 8 + 1, 8, HALF)
    tiles = pltpu.roll(tiles, jnp.where(rest == 0, 0, 8 - rest), 1)
    row = lax.broadcasted_iota(jnp.int32, (REACH // 8, 8, HALF), 1)
    return jnp.where(row < 8 - rest, tiles[:-1], tiles[1:]).reshape(REACH, HALF).astype(BF16)


def fill_tables(o_r, o_c, w_r, w_c, base_ref, refs):
    back_r, back_c, fwd_r, fwd_c = refs
    tall_r = window(base_ref, o_r + S)
    tall_c = window(base_ref, o_c + S)
    wide_r = window(base_ref, -o_r)
    wide_c = window(base_ref, -o_c)
    none = jnp.zeros((), BF16)
    lane = lax.broadcasted_iota(jnp.int32, (S, HALF), 1)
    deep = lax.broadcasted_iota(jnp.int32, (BOX, HALF), 0)
    for k in range(BOX // HALF):
        at = slice(k * HALF, (k + 1) * HALF)
        rows = slice(384 - HALF * k, 640 - HALF * k)
        back_c[:, at] = wide_c[rows]
        fwd_r[:, at] = jnp.where(lane + k * HALF < w_r, wide_r[rows], none)
    for k in range(S // HALF):
        at = slice(k * HALF, (k + 1) * HALF)
        rows = slice(HALF - HALF * k, REACH - HALF * k)
        back_r[:, at] = tall_r[rows]
        fwd_c[:, at] = jnp.where(deep < w_c, tall_c[rows], none)


def table_scratch():
    return [
        pltpu.VMEM((BOX, S), BF16),
        pltpu.VMEM((S, BOX), BF16),
        pltpu.VMEM((S, BOX), BF16),
        pltpu.VMEM((BOX, S), BF16),
    ]


def forward(mass, tables, vb_ref):
    inner = dot(tables[2][...], vb_ref[...]).astype(BF16)
    return mass / dot(inner, tables[3][...])


def aligned_kernel(cells, shifts, widths, source, boxes, *refs):
    n = len(cells)
    outs, refs = refs[: 4 if 0 in cells else 2], refs[4 if 0 in cells else 2 :]
    base_ref, box_ref, mass_ref, vb_ref, tables, sems = refs
    copies = []
    for i, j in enumerate(cells):
        copies.append((
            pltpu.make_async_copy(boxes.at[0, j], box_ref.at[i], sems.at[i, 0]),
            pltpu.make_async_copy(
                source.at[:, pl.ds(j * S, S)], mass_ref.at[:, pl.ds(i * S, S)], sems.at[i, 1]),
        ))
    for pair in copies:
        for copy in pair:
            copy.start()
    fill_base(base_ref)
    for i, j in enumerate(cells):
        fill_tables(
            shifts[0, j, 0], shifts[0, j, 1], widths[0, j, 0], widths[0, j, 1], base_ref, tables[i])
    scales = []
    for i in range(n):
        down = dot(tables[i][0][...], jnp.ones((S, HALF), BF16)).astype(BF16).astype(F32)
        across = dot(jnp.ones((8, S), BF16), tables[i][1][...])
        scales.append(((1.0 / down)[:, :1], (1.0 / across)[:1]))
    u = [None] * n
    for step in range(ITERS):
        for i in range(n):
            if step == 0:
                for copy in copies[i]:
                    copy.wait()
                down, across = scales[i]
                for c in range(0, BOX, HALF):
                    v = box_ref[i, c : c + HALF] * down[c : c + HALF] * across
                    vb_ref[i, c : c + HALF] = v.astype(BF16)
            else:
                inner = dot(tables[i][0][...], u[i].astype(BF16)).astype(BF16)
                vb_ref[i] = (box_ref[i] / dot(inner, tables[i][1][...])).astype(BF16)
        for i in range(n):
            u[i] = forward(mass_ref[:, i * S : (i + 1) * S], tables[i], vb_ref.at[i])
    for i, j in enumerate(cells):
        outs[0][:, i * S : (i + 1) * S] = u[i][:HALF]
        outs[1][:, i * S : (i + 1) * S] = u[i][HALF:]
        if j == 0:
            for k in range(2):
                outs[2 + k][:HALF] = u[i][k * HALF : (k + 1) * HALF, :HALF]
                outs[2 + k][HALF:] = mass_ref[k * HALF : (k + 1) * HALF, i * S : i * S + HALF]


def cost(cells, applies):
    return pl.CostEstimate(
        flops=cells * applies * 804_000_000, bytes_accessed=cells << 20, transcendentals=0)


def aligned(cells, source, boxes, shifts, widths):
    n = len(cells)
    half = jax.ShapeDtypeStruct((HALF, n * S), F32)
    corner = jax.ShapeDtypeStruct((S, HALF), F32)
    shapes = [half, half] + ([corner, corner] if 0 in cells else [])
    return pl.pallas_call(
        functools.partial(aligned_kernel, cells),
        in_specs=[SMEM, SMEM, HBM, HBM],
        out_specs=[VMEM] * len(shapes),
        out_shape=shapes,
        scratch_shapes=[
            pltpu.VMEM((BASE, HALF), F32),
            pltpu.VMEM((n, BOX, BOX), F32),
            pltpu.VMEM((S, n * S), F32),
            pltpu.VMEM((n, BOX, BOX), BF16),
            [table_scratch() for _ in cells],
            pltpu.SemaphoreType.DMA((n, 2)),
        ],
        compiler_params=PARAMS,
        cost_estimate=cost(n, 5),
        name="aligned",
    )(shifts, widths, source, boxes)


def place(plan_ref, top, left, canvas_ref, first):
    base = pl.multiple_of(top // 8 * 8, 8)
    rest = top - base
    row = lax.broadcasted_iota(jnp.int32, (HALF // 8 + 1, 8, BOX), 1)
    column = lax.broadcasted_iota(jnp.int32, (HALF + 8, HALF), 1)
    none = jnp.zeros((1, 8, BOX), F32)
    for c in range(0, BOX, HALF):
        turned = pltpu.roll(plan_ref[c : c + HALF].reshape(HALF // 8, 8, BOX), rest, 1)
        rows = jnp.where(
            row < rest,
            jnp.concatenate([none, turned], 0),
            jnp.concatenate([turned, none], 0),
        ).reshape(HALF + 8, BOX)
        before = jnp.zeros((HALF + 8, HALF), F32)
        for k in range(BOX // HALF + 1):
            now = jnp.zeros((HALF + 8, HALF), F32)
            if k < BOX // HALF:
                now = pltpu.roll(rows[:, k * HALF : (k + 1) * HALF], left, 1)
            at = (pl.ds(base + c, HALF + 8), slice(first + k * HALF, first + (k + 1) * HALF))
            canvas_ref[at] = canvas_ref[at] + jnp.where(column < left, before, now)
            before = now


def shifted_kernel(cells, origin, carried, finals, kept, shifts, widths, boxes, *refs):
    n = len(cells)
    quads, refs = refs[: 8 * n], refs[8 * n :]
    upper_ref = None
    if carried:
        carry_ref, refs = refs[0], refs[1:]
        if kept:
            upper_ref, refs = refs[0], refs[1:]
    outs, refs = refs[:4], refs[4:]
    if kept:
        keep_ref, refs = refs[0], refs[1:]
    base_ref, box_ref, mass_ref, ub_ref, vb_ref, v_ref, canvas_ref, tables, sems, out_sems = refs
    copies = [
        pltpu.make_async_copy(boxes.at[0, j], box_ref.at[i], sems.at[i])
        for i, j in enumerate(cells)
    ]
    for copy in copies:
        copy.start()
    fill_base(base_ref)
    canvas_ref[...] = jnp.zeros_like(canvas_ref)
    if carried:
        first, last = carried[0] - origin, carried[1] - origin
        canvas_ref[:REACH, first:last] = carry_ref[...]
    for i, j in enumerate(cells):
        fill_tables(
            shifts[0, j, 0], shifts[0, j, 1], widths[0, j, 0], widths[0, j, 1], base_ref, tables[i])
        for k in range(4):
            rows = slice(k // 2 * HALF, (k // 2 + 1) * HALF)
            cols = slice(k % 2 * HALF, (k % 2 + 1) * HALF)
            ub_ref[i, rows, cols] = quads[8 * i + k][...].astype(BF16)
            mass_ref[i, rows, cols] = quads[8 * i + 4 + k][...]
    u = [ub_ref[i] for i in range(n)]
    for step in range(ITERS):
        for i in range(n):
            inner = dot(tables[i][0][...], u[i]).astype(BF16)
            den = dot(inner, tables[i][1][...])
            if step == 0:
                copies[i].wait()
            v = box_ref[i] / den
            if step == ITERS - 1:
                v_ref[i] = v
            vb_ref[i] = v.astype(BF16)
        for i in range(n):
            u[i] = forward(mass_ref[i], tables[i], vb_ref.at[i]).astype(BF16)
    deep = lax.broadcasted_iota(jnp.int32, (BOX, S), 0)
    lane = lax.broadcasted_iota(jnp.int32, (S, BOX), 1)
    for i, j in enumerate(cells):
        inner = jnp.where(deep < widths[0, j, 0], dot(tables[i][0][...], u[i]), 0.0).astype(BF16)
        used = jnp.where(lane < widths[0, j, 1], tables[i][1][...], jnp.zeros((), BF16))
        v_ref[i] = v_ref[i] * dot(inner, used)
    for i, j in enumerate(cells):
        place(v_ref.at[i], shifts[0, j, 0] + HALF, shifts[0, j, 1] + HALF, canvas_ref,
              j * S - origin)
    writes = []
    at = 0
    for first, last in finals:
        size = last - first
        for ref, row in zip(outs, (0, S - RADIUS, 2 * S - RADIUS, 0)):
            writes.append(pltpu.make_async_copy(
                canvas_ref.at[pl.ds(row, ref.shape[0]), pl.ds(first - origin, size)],
                ref.at[:, pl.ds(at, size)],
                out_sems.at[len(writes)]))
        at += size
    if upper_ref is not None:
        writes.append(pltpu.make_async_copy(
            upper_ref, outs[3].at[:, pl.ds(at, upper_ref.shape[1])], out_sems.at[len(writes)]))
    if kept:
        size = kept[1] - kept[0]
        writes.append(pltpu.make_async_copy(
            canvas_ref.at[pl.ds(0, REACH), pl.ds(kept[0] - origin, size)], keep_ref,
            out_sems.at[len(writes)]))
    for copy in writes:
        copy.start()
    for copy in writes:
        copy.wait()


def shifted(cells, boxes, shifts, widths, quads, carried=None, carry=None, finals=(), kept=None):
    n = len(cells)
    origin = min(j * S for j in cells)
    width = max(j * S + REACH for j in cells) - origin
    total = sum(last - first for first, last in finals)
    shapes = [jax.ShapeDtypeStruct((rows, total), F32) for rows in (OWN, NEXT, FAR, RADIUS)]
    if kept:
        shapes.append(jax.ShapeDtypeStruct((REACH, kept[1] - kept[0]), F32))
    blocks, arrays = [], []
    for j in cells:
        for array, at in quads[j]:
            arrays.append(array)
            blocks.append(pl.BlockSpec((HALF, HALF), lambda g, at=at: at))
    if carried:
        arrays += carry
        blocks += [VMEM] * len(carry)
        if kept:
            shapes[3] = jax.ShapeDtypeStruct((RADIUS, total + carry[1].shape[1]), F32)
    return pl.pallas_call(
        functools.partial(shifted_kernel, cells, origin, carried, finals, kept),
        grid=(1,),
        in_specs=[SMEM, SMEM, HBM] + blocks,
        out_specs=[ANY] * len(shapes),
        out_shape=shapes,
        scratch_shapes=[
            pltpu.VMEM((BASE, HALF), F32),
            pltpu.VMEM((n, BOX, BOX), F32),
            pltpu.VMEM((n, S, S), F32),
            pltpu.VMEM((n, S, S), BF16),
            pltpu.VMEM((n, BOX, BOX), BF16),
            pltpu.VMEM((n, BOX, BOX), F32),
            pltpu.VMEM((REACH + 8, width), F32),
            [table_scratch() for _ in cells],
            pltpu.SemaphoreType.DMA((n,)),
            pltpu.SemaphoreType.DMA((4 * len(finals) + 2,)),
        ],
        compiler_params=PARAMS,
        cost_estimate=cost(n, 7),
        name="shifted",
    )(shifts, widths, boxes, *arrays)


def blur_weights():
    raw = [math.exp(-(d * d) / (2.0 * SIGMA * SIGMA)) for d in range(-RADIUS, RADIUS + 1)]
    total = sum(raw)
    return [w / total for w in raw]


def blurred_rows(own_ref, next_ref, far_ref, back_ref, win_ref, width, put):
    win_ref[:, :width] = next_ref[...]
    win_ref[RADIUS:, :width] = win_ref[RADIUS:, :width] + own_ref[...]
    win_ref[:FAR, :width] = win_ref[:FAR, :width] + far_ref[...]
    win_ref[NEXT - RADIUS :, :width] = win_ref[NEXT - RADIUS :, :width] + back_ref[...]
    weights = blur_weights()
    for c in range(0, width, HALF):
        col = win_ref[:, c : c + HALF]
        out = weights[RADIUS] * col[RADIUS : RADIUS + S]
        for d in range(1, RADIUS + 1):
            out = out + weights[RADIUS + d] * (
                col[RADIUS + d : RADIUS + d + S] + col[RADIUS - d : RADIUS - d + S])
        put(c, out)


def edges_kernel(*refs):
    (own3, next3, far3, own2, next2, far2, back2, main_ref, right_ref, east_ref, west_ref,
     win_ref) = refs

    def outer(c, out):
        east_ref[:S, HALF + c : 2 * HALF + c] = out

    def inner(c, out):
        if c < 3 * HALF:
            main_ref[:, c : c + HALF] = out
        else:
            east_ref[:S, :HALF] = out
            right_ref[...] = out
        if c == 0:
            west_ref[...] = out.T[:RADIUS]
        if c == 2 * HALF:
            east_ref[S:, :S] = out.T[HALF - RADIUS :]
            east_ref[S:, S:] = jnp.zeros((RADIUS, HALF), F32)

    blurred_rows(own3, next3, far3, back2.at[:, 2 * S :], win_ref, S, outer)
    blurred_rows(own2, next2, far2, back2.at[:, : 2 * S], win_ref, 2 * S, inner)


def edges(*arrays):
    return pl.pallas_call(
        edges_kernel,
        in_specs=[VMEM] * 7,
        out_specs=[VMEM] * 4,
        out_shape=[
            jax.ShapeDtypeStruct((S, 3 * HALF), F32),
            jax.ShapeDtypeStruct((S, HALF), F32),
            jax.ShapeDtypeStruct((S + RADIUS, 3 * HALF), F32),
            jax.ShapeDtypeStruct((RADIUS, S), F32),
        ],
        scratch_shapes=[pltpu.VMEM((NEXT, 2 * S), F32)],
        compiler_params=PARAMS,
        name="edges",
    )(*arrays)


def band():
    full = np.zeros((2 * S, S), np.float64)
    for j in range(S):
        for d, w in zip(range(-RADIUS, RADIUS + 1), blur_weights()):
            full[j + HALF + d, j] = w
    high = full.astype(jnp.bfloat16)
    return high, (full - high.astype(np.float64)).astype(jnp.bfloat16)


def final_kernel(own1, next1, far1, back1, main_ref, right_ref, east_ref, west_ref, high_ref,
                 low_ref, out_ref, rows_ref, win_ref):
    span = out_ref.shape[1]
    none = jnp.zeros((HALF - RADIUS, S), F32)
    win_ref[:, :HALF] = jnp.concatenate([none, east_ref[S:, :S]], 0).T
    win_ref[:, HALF : HALF + S] = main_ref[:, :S] + east_ref[:S, :S]
    win_ref[:, HALF + 7 * HALF : HALF + span] = main_ref[:, S:]
    win_ref[:, HALF + span :] = right_ref[...] + jnp.concatenate([west_ref[...], none], 0).T

    def middle(c, out):
        if c == 0:
            out = out + east_ref[:S, S:]
        win_ref[:, HALF + S + c : 2 * HALF + S + c] = out

    blurred_rows(own1, next1, far1, back1, rows_ref, REACH, middle)
    for c in range(0, span, S):
        strip = win_ref[:, c : c + 2 * S]
        high = strip.astype(BF16)
        low = (strip - high.astype(F32)).astype(BF16)
        out_ref[:, c : c + S] = (
            dot(high, high_ref[...]) + dot(high, low_ref[...]) + dot(low, high_ref[...]))


def final(span, *arrays):
    high, low = band()
    return pl.pallas_call(
        final_kernel,
        in_specs=[VMEM] * 10,
        out_specs=VMEM,
        out_shape=jax.ShapeDtypeStruct((S, span), F32),
        scratch_shapes=[
            pltpu.VMEM((NEXT, REACH), F32),
            pltpu.VMEM((S, span + 2 * HALF), F32),
        ],
        compiler_params=PARAMS,
        name="final",
    )(*arrays, jnp.asarray(high), jnp.asarray(low))


def moved(array, by_row, by_col):
    n_row, n_col = lax.axis_size("row"), lax.axis_size("col")
    if by_col == 0:
        return lax.ppermute(array, "row", [(i, (i + by_row) % n_row) for i in range(n_row)])
    if by_row == 0:
        return lax.ppermute(array, "col", [(i, (i + by_col) % n_col) for i in range(n_col)])
    pairs = [
        (r * n_col + c, (r + by_row) % n_row * n_col + (c + by_col) % n_col)
        for r in range(n_row)
        for c in range(n_col)
    ]
    return lax.ppermute(array, ("row", "col"), pairs)


def spilled(parts):
    own, after, far, back = parts
    return own, moved(after, 1, 0), moved(far, 2, 0), moved(back, -1, 0)


def behind(array, *others):
    return lax.optimization_barrier((array, *others))[0]


def on_device(source, boxes_a, shifts_a, widths_a, boxes_b, shifts_b, widths_b):
    mtop = moved(source[:HALF], -1, 0)
    boxes_a = pltpu.with_memory_space_constraint(boxes_a, pltpu.HBM)
    boxes_b = pltpu.with_memory_space_constraint(boxes_b, pltpu.HBM)
    masses = pltpu.with_memory_space_constraint(source, pltpu.HBM)
    top03, bot03, left_top, left_bot = aligned((0, 3), masses, boxes_a, shifts_a, widths_a)
    rtop03 = moved(top03, -1, 0)
    east = moved(left_bot, 0, -1)
    diag = moved(left_top, -1, -1)
    top12, bot12 = aligned(
        (1, 2), masses, boxes_a, behind(shifts_a, bot03), widths_a)
    rtop12 = moved(top12, -1, 0)
    own = [(bot03, 0), (bot03, 1), (bot12, 0), (bot12, 1), (bot12, 2), (bot12, 3), (bot03, 2),
           (bot03, 3), (east, 0)]
    below = [(rtop03, 0), (rtop03, 1), (rtop12, 0), (rtop12, 1), (rtop12, 2), (rtop12, 3),
             (rtop03, 2), (rtop03, 3), (diag, 0)]
    quads = {}
    for j in range(4):
        a, b = 2 * j + 1, 2 * j + 2
        quads[j] = [(array, (0, at)) for array, at in (own[a], own[b], below[a], below[b])]
        quads[j] += [
            (source, (1, a)),
            (source, (1, b)) if j < 3 else (east, (1, 0)),
            (mtop, (0, a)),
            (mtop, (0, b)) if j < 3 else (diag, (1, 0)),
        ]
    own3, next3, far3, back3, carry = shifted(
        (3,), boxes_b, behind(shifts_b, bot12), widths_b, quads,
        finals=((1152, 1408),), kept=(768, 1152))
    next3 = moved(next3, 1, 0)
    far3 = moved(far3, 2, 0)
    own2, next2, far2, back2, carry = shifted(
        (0, 2), boxes_b, shifts_b, widths_b, quads,
        carried=(768, 1152), carry=(carry, back3), finals=((0, 256), (896, 1152)),
        kept=(256, 896))
    next2 = moved(next2, 1, 0)
    far2 = moved(far2, 2, 0)
    rback2 = moved(back2, -1, 0)
    own1, next1, far1, back1 = shifted(
        (1,), boxes_b, shifts_b, widths_b, quads,
        carried=(256, 896), carry=(behind(carry, next3, far3),),
        finals=((256, 896),))
    next1 = moved(behind(next1, next2, far2, rback2), 1, 0)
    far1 = moved(behind(far1, next2, far2, rback2), 2, 0)
    back1 = moved(behind(back1, next2, far2, rback2), -1, 0)
    main, right, east, west = edges(own3, next3, far3, own2, next2, far2, rback2)
    return final(
        source.shape[1], own1, next1, far1, back1, main, right, moved(east, 0, 1),
        moved(west, 0, -1))


def solution(mesh):
    cells = P("row", "col", None)
    boxes = P("row", "col", None, None)
    return jax.shard_map(
        on_device,
        mesh=mesh,
        in_specs=(P("row", "col"), boxes, cells, cells, boxes, cells, cells),
        out_specs=P("row", "col"),
        check_vma=False,
    )
```

```python
import functools
import math

import jax
import jax.numpy as jnp
import numpy as np
from jax import lax
from jax.experimental import pallas as pl
from jax.experimental.pallas import tpu as pltpu
from jax.sharding import PartitionSpec as P

S = 256
HALF = 128
BOX = 512
ITERS = 3
RADIUS = 8
REACH = BOX + HALF
EPS = 0.05
SIGMA = 2.0
F32 = jnp.float32
BF16 = jnp.bfloat16
OWN = S + RADIUS
NEXT = S + 2 * RADIUS
FAR = REACH - 2 * S + RADIUS
BASE = 904
VMEM = pl.BlockSpec(memory_space=pltpu.VMEM)
SMEM = pl.BlockSpec(memory_space=pltpu.SMEM)
ANY = pl.BlockSpec(memory_space=pl.ANY)
HBM = pl.BlockSpec(memory_space=pltpu.HBM)
PARAMS = pltpu.CompilerParams(vmem_limit_bytes=24 << 20)


def dot(a, b):
    return jnp.dot(a, b, preferred_element_type=F32)


def fill_base(ref):
    for c in range(0, BASE, 8 * 28):
        n = min(8 * 28, BASE - c)
        rows = lax.broadcasted_iota(jnp.int32, (n, HALF), 0)
        cols = lax.broadcasted_iota(jnp.int32, (n, HALF), 1)
        dist = (rows - cols + (c - 384)).astype(F32) / S
        ref[c : c + n] = jnp.exp(-dist * dist / EPS)


def window(ref, start):
    base = pl.multiple_of(start // 8 * 8, 8)
    rest = start - base
    tiles = ref[pl.ds(base, REACH + 8), :].reshape(REACH // 8 + 1, 8, HALF)
    tiles = pltpu.roll(tiles, jnp.where(rest == 0, 0, 8 - rest), 1)
    row = lax.broadcasted_iota(jnp.int32, (REACH // 8, 8, HALF), 1)
    return jnp.where(row < 8 - rest, tiles[:-1], tiles[1:]).reshape(REACH, HALF).astype(BF16)


def fill_tables(o_r, o_c, w_r, w_c, base_ref, refs):
    back_r, back_c, fwd_r, fwd_c = refs
    tall_r = window(base_ref, o_r + S)
    tall_c = window(base_ref, o_c + S)
    wide_r = window(base_ref, -o_r)
    wide_c = window(base_ref, -o_c)
    none = jnp.zeros((), BF16)
    lane = lax.broadcasted_iota(jnp.int32, (S, HALF), 1)
    deep = lax.broadcasted_iota(jnp.int32, (BOX, HALF), 0)
    for k in range(BOX // HALF):
        at = slice(k * HALF, (k + 1) * HALF)
        rows = slice(384 - HALF * k, 640 - HALF * k)
        back_c[:, at] = wide_c[rows]
        fwd_r[:, at] = jnp.where(lane + k * HALF < w_r, wide_r[rows], none)
    for k in range(S // HALF):
        at = slice(k * HALF, (k + 1) * HALF)
        rows = slice(HALF - HALF * k, REACH - HALF * k)
        back_r[:, at] = tall_r[rows]
        fwd_c[:, at] = jnp.where(deep < w_c, tall_c[rows], none)


def table_scratch():
    return [
        pltpu.VMEM((BOX, S), BF16),
        pltpu.VMEM((S, BOX), BF16),
        pltpu.VMEM((S, BOX), BF16),
        pltpu.VMEM((BOX, S), BF16),
    ]


def forward(mass, tables, vb_ref):
    inner = dot(tables[2][...], vb_ref[...]).astype(BF16)
    return mass / dot(inner, tables[3][...])


def aligned_kernel(cells, shifts, widths, source, boxes, *refs):
    n = len(cells)
    if 0 in cells:
        outs, base_ref, refs = refs[:4], refs[4], refs[5:]
    else:
        base_ref, outs, refs = refs[0], refs[1:3], refs[3:]
    box_ref, mass_ref, vb_ref, tables, sems = refs
    copies = []
    for i, j in enumerate(cells):
        copies.append((
            pltpu.make_async_copy(boxes.at[0, j], box_ref.at[i], sems.at[i, 0]),
            pltpu.make_async_copy(
                source.at[:, pl.ds(j * S, S)], mass_ref.at[:, pl.ds(i * S, S)], sems.at[i, 1]),
        ))
    for pair in copies:
        for copy in pair:
            copy.start()
    if 0 in cells:
        fill_base(base_ref)
    for i, j in enumerate(cells):
        fill_tables(
            shifts[0, 0, j], shifts[0, 1, j], widths[0, 0, j], widths[0, 1, j], base_ref, tables[i])
    scales = []
    for i in range(n):
        down = dot(tables[i][0][...], jnp.ones((S, HALF), BF16)).astype(BF16).astype(F32)
        across = dot(jnp.ones((8, S), BF16), tables[i][1][...])
        scales.append(((1.0 / down)[:, :1], (1.0 / across)[:1]))
    u = [None] * n
    for step in range(ITERS):
        for i in range(n):
            if step == 0:
                for copy in copies[i]:
                    copy.wait()
                down, across = scales[i]
                for c in range(0, BOX, HALF):
                    v = box_ref[i, c : c + HALF] * down[c : c + HALF] * across
                    vb_ref[i, c : c + HALF] = v.astype(BF16)
            else:
                inner = dot(tables[i][0][...], u[i].astype(BF16)).astype(BF16)
                vb_ref[i] = (box_ref[i] / dot(inner, tables[i][1][...])).astype(BF16)
        for i in range(n):
            u[i] = forward(mass_ref[:, i * S : (i + 1) * S], tables[i], vb_ref.at[i])
    for i, j in enumerate(cells):
        outs[0][:HALF, i * S : (i + 1) * S] = u[i][:HALF]
        outs[0][HALF:, i * S : (i + 1) * S] = mass_ref[:HALF, i * S : (i + 1) * S]
        outs[1][:, i * S : (i + 1) * S] = u[i][HALF:]
        if j == 0:
            for k in range(2):
                outs[2 + k][:HALF] = u[i][k * HALF : (k + 1) * HALF, :HALF]
                outs[2 + k][HALF:] = mass_ref[k * HALF : (k + 1) * HALF, i * S : i * S + HALF]


def cost(cells, applies):
    return pl.CostEstimate(
        flops=cells * applies * 804_000_000, bytes_accessed=cells << 20, transcendentals=0)


def aligned(cells, source, boxes, shifts, widths, *base):
    n = len(cells)
    corner = jax.ShapeDtypeStruct((S, HALF), F32)
    shapes = [jax.ShapeDtypeStruct((S, n * S), F32), jax.ShapeDtypeStruct((HALF, n * S), F32)]
    if 0 in cells:
        shapes += [corner, corner, jax.ShapeDtypeStruct((BASE, HALF), F32)]
    return pl.pallas_call(
        functools.partial(aligned_kernel, cells),
        in_specs=[SMEM, SMEM, HBM, HBM] + [VMEM] * len(base),
        out_specs=[VMEM] * len(shapes),
        out_shape=shapes,
        scratch_shapes=[
            pltpu.VMEM((n, BOX, BOX), F32),
            pltpu.VMEM((S, n * S), F32),
            pltpu.VMEM((n, BOX, BOX), BF16),
            [table_scratch() for _ in cells],
            pltpu.SemaphoreType.DMA((n, 2)),
        ],
        compiler_params=PARAMS,
        cost_estimate=cost(n, 5),
        name="aligned",
    )(shifts, widths, source, boxes, *base)


def place(plan_ref, top, left, canvas_ref, first):
    base = pl.multiple_of(top // 8 * 8, 8)
    rest = top - base
    row = lax.broadcasted_iota(jnp.int32, (HALF // 8 + 1, 8, BOX), 1)
    column = lax.broadcasted_iota(jnp.int32, (HALF + 8, HALF), 1)
    none = jnp.zeros((1, 8, BOX), F32)
    for c in range(0, BOX, HALF):
        turned = pltpu.roll(plan_ref[c : c + HALF].reshape(HALF // 8, 8, BOX), rest, 1)
        rows = jnp.where(
            row < rest,
            jnp.concatenate([none, turned], 0),
            jnp.concatenate([turned, none], 0),
        ).reshape(HALF + 8, BOX)
        before = jnp.zeros((HALF + 8, HALF), F32)
        for k in range(BOX // HALF + 1):
            now = jnp.zeros((HALF + 8, HALF), F32)
            if k < BOX // HALF:
                now = pltpu.roll(rows[:, k * HALF : (k + 1) * HALF], left, 1)
            at = (pl.ds(base + c, HALF + 8), slice(first + k * HALF, first + (k + 1) * HALF))
            canvas_ref[at] = canvas_ref[at] + jnp.where(column < left, before, now)
            before = now


def shifted_kernel(cells, origin, carried, finals, kept, shifts, widths, boxes, base_ref, *refs):
    n = len(cells)
    quads, refs = refs[: 8 * n], refs[8 * n :]
    upper_ref = None
    if carried:
        carry_ref, refs = refs[0], refs[1:]
        if kept:
            upper_ref, refs = refs[0], refs[1:]
    outs, refs = refs[:4], refs[4:]
    if kept:
        keep_ref, refs = refs[0], refs[1:]
    box_ref, mass_ref, ub_ref, vb_ref, v_ref, canvas_ref, tables, sems, out_sems = refs
    copies = [
        pltpu.make_async_copy(boxes.at[0, j], box_ref.at[i], sems.at[i])
        for i, j in enumerate(cells)
    ]
    for copy in copies:
        copy.start()
    canvas_ref[...] = jnp.zeros_like(canvas_ref)
    if carried:
        first, last = carried[0] - origin, carried[1] - origin
        canvas_ref[:REACH, first:last] = carry_ref[...]
    for i, j in enumerate(cells):
        fill_tables(
            shifts[0, 0, j], shifts[0, 1, j], widths[0, 0, j], widths[0, 1, j], base_ref, tables[i])
        for k in range(4):
            rows = slice(k // 2 * HALF, (k // 2 + 1) * HALF)
            cols = slice(k % 2 * HALF, (k % 2 + 1) * HALF)
            ub_ref[i, rows, cols] = quads[8 * i + k][...].astype(BF16)
            mass_ref[i, rows, cols] = quads[8 * i + 4 + k][...]
    u = [ub_ref[i] for i in range(n)]
    for step in range(ITERS):
        for i in range(n):
            inner = dot(tables[i][0][...], u[i]).astype(BF16)
            den = dot(inner, tables[i][1][...])
            if step == 0:
                copies[i].wait()
            v = box_ref[i] / den
            if step == ITERS - 1:
                v_ref[i] = v
            vb_ref[i] = v.astype(BF16)
        for i in range(n):
            u[i] = forward(mass_ref[i], tables[i], vb_ref.at[i]).astype(BF16)
    deep = lax.broadcasted_iota(jnp.int32, (BOX, S), 0)
    lane = lax.broadcasted_iota(jnp.int32, (S, BOX), 1)
    for i, j in enumerate(cells):
        inner = jnp.where(deep < widths[0, 0, j], dot(tables[i][0][...], u[i]), 0.0).astype(BF16)
        used = jnp.where(lane < widths[0, 1, j], tables[i][1][...], jnp.zeros((), BF16))
        v_ref[i] = v_ref[i] * dot(inner, used)
    for i, j in enumerate(cells):
        place(v_ref.at[i], shifts[0, 0, j] + HALF, shifts[0, 1, j] + HALF, canvas_ref,
              j * S - origin)
    writes = []
    at = 0
    for first, last in finals:
        size = last - first
        for ref, row in zip(outs, (0, S - RADIUS, 2 * S - RADIUS, 0)):
            writes.append(pltpu.make_async_copy(
                canvas_ref.at[pl.ds(row, ref.shape[0]), pl.ds(first - origin, size)],
                ref.at[:, pl.ds(at, size)],
                out_sems.at[len(writes)]))
        at += size
    if upper_ref is not None:
        writes.append(pltpu.make_async_copy(
            upper_ref, outs[3].at[:, pl.ds(at, upper_ref.shape[1])], out_sems.at[len(writes)]))
    if kept:
        size = kept[1] - kept[0]
        writes.append(pltpu.make_async_copy(
            canvas_ref.at[pl.ds(0, REACH), pl.ds(kept[0] - origin, size)], keep_ref,
            out_sems.at[len(writes)]))
    for copy in writes:
        copy.start()
    for copy in writes:
        copy.wait()


def shifted(cells, boxes, shifts, widths, base, quads, carried=None, carry=None, finals=(), kept=None):
    n = len(cells)
    origin = min(j * S for j in cells)
    width = max(j * S + REACH for j in cells) - origin
    total = sum(last - first for first, last in finals)
    shapes = [jax.ShapeDtypeStruct((rows, total), F32) for rows in (OWN, NEXT, FAR, RADIUS)]
    if kept:
        shapes.append(jax.ShapeDtypeStruct((REACH, kept[1] - kept[0]), F32))
    blocks, arrays = [], []
    for j in cells:
        for array, at in quads[j]:
            arrays.append(array)
            blocks.append(pl.BlockSpec((HALF, HALF), lambda g, at=at: at))
    if carried:
        arrays += carry
        blocks += [VMEM] * len(carry)
        if kept:
            shapes[3] = jax.ShapeDtypeStruct((RADIUS, total + carry[1].shape[1]), F32)
    return pl.pallas_call(
        functools.partial(shifted_kernel, cells, origin, carried, finals, kept),
        grid=(1,),
        in_specs=[SMEM, SMEM, HBM, VMEM] + blocks,
        out_specs=[ANY] * len(shapes),
        out_shape=shapes,
        scratch_shapes=[
            pltpu.VMEM((n, BOX, BOX), F32),
            pltpu.VMEM((n, S, S), F32),
            pltpu.VMEM((n, S, S), BF16),
            pltpu.VMEM((n, BOX, BOX), BF16),
            pltpu.VMEM((n, BOX, BOX), F32),
            pltpu.VMEM((REACH + 8, width), F32),
            [table_scratch() for _ in cells],
            pltpu.SemaphoreType.DMA((n,)),
            pltpu.SemaphoreType.DMA((4 * len(finals) + 2,)),
        ],
        compiler_params=PARAMS,
        cost_estimate=cost(n, 7),
        name="shifted",
    )(shifts, widths, boxes, base, *arrays)


def blur_weights():
    raw = [math.exp(-(d * d) / (2.0 * SIGMA * SIGMA)) for d in range(-RADIUS, RADIUS + 1)]
    total = sum(raw)
    return [w / total for w in raw]


def blurred_rows(own_ref, next_ref, far_ref, back_ref, win_ref, width, put):
    win_ref[:, :width] = next_ref[...]
    win_ref[RADIUS:, :width] = win_ref[RADIUS:, :width] + own_ref[...]
    win_ref[:FAR, :width] = win_ref[:FAR, :width] + far_ref[...]
    win_ref[NEXT - RADIUS :, :width] = win_ref[NEXT - RADIUS :, :width] + back_ref[...]
    weights = blur_weights()
    for c in range(0, width, HALF):
        col = win_ref[:, c : c + HALF]
        out = weights[RADIUS] * col[RADIUS : RADIUS + S]
        for d in range(1, RADIUS + 1):
            out = out + weights[RADIUS + d] * (
                col[RADIUS + d : RADIUS + d + S] + col[RADIUS - d : RADIUS - d + S])
        put(c, out)


def edges_kernel(*refs):
    (own3, next3, far3, own2, next2, far2, back2, next1, joined, main_ref, right_ref, east_ref,
     west_ref, sum_ref, win_ref) = refs
    sum_ref[:FAR] = next1[:FAR] + joined[...]
    sum_ref[FAR:] = next1[FAR:]

    def outer(c, out):
        east_ref[:S, HALF + c : 2 * HALF + c] = out

    def inner(c, out):
        if c < 3 * HALF:
            main_ref[:, c : c + HALF] = out
        else:
            east_ref[:S, :HALF] = out
            right_ref[...] = out
        if c == 0:
            west_ref[...] = out.T[:RADIUS]
        if c == 2 * HALF:
            east_ref[S:, :S] = out.T[HALF - RADIUS :]
            east_ref[S:, S:] = jnp.zeros((RADIUS, HALF), F32)

    blurred_rows(own3, next3, far3, back2.at[:, 2 * S :], win_ref, S, outer)
    blurred_rows(own2, next2, far2, back2.at[:, : 2 * S], win_ref, 2 * S, inner)


def edges(*arrays):
    return pl.pallas_call(
        edges_kernel,
        in_specs=[VMEM] * 9,
        out_specs=[VMEM] * 5,
        out_shape=[
            jax.ShapeDtypeStruct((S, 3 * HALF), F32),
            jax.ShapeDtypeStruct((S, HALF), F32),
            jax.ShapeDtypeStruct((S + RADIUS, 3 * HALF), F32),
            jax.ShapeDtypeStruct((RADIUS, S), F32),
            jax.ShapeDtypeStruct((NEXT, REACH), F32),
        ],
        scratch_shapes=[pltpu.VMEM((NEXT, 2 * S), F32)],
        compiler_params=PARAMS,
        name="edges",
    )(*arrays)


def band():
    full = np.zeros((2 * S, S), np.float64)
    for j in range(S):
        for d, w in zip(range(-RADIUS, RADIUS + 1), blur_weights()):
            full[j + HALF + d, j] = w
    high = full.astype(jnp.bfloat16)
    return high, (full - high.astype(np.float64)).astype(jnp.bfloat16)


def final_kernel(own1, next1, far1, back1, main_ref, right_ref, east_ref, west_ref, high_ref,
                 low_ref, out_ref, rows_ref, win_ref):
    span = out_ref.shape[1]
    none = jnp.zeros((HALF - RADIUS, S), F32)
    win_ref[:, :HALF] = jnp.concatenate([none, east_ref[S:, :S]], 0).T
    win_ref[:, HALF : HALF + S] = main_ref[:, :S] + east_ref[:S, :S]
    win_ref[:, HALF + 7 * HALF : HALF + span] = main_ref[:, S:]
    win_ref[:, HALF + span :] = right_ref[...] + jnp.concatenate([west_ref[...], none], 0).T

    def middle(c, out):
        if c == 0:
            out = out + east_ref[:S, S:]
        win_ref[:, HALF + S + c : 2 * HALF + S + c] = out

    blurred_rows(own1, next1, far1, back1, rows_ref, REACH, middle)
    for c in range(0, span, S):
        strip = win_ref[:, c : c + 2 * S]
        high = strip.astype(BF16)
        low = (strip - high.astype(F32)).astype(BF16)
        out_ref[:, c : c + S] = (
            dot(high, high_ref[...]) + dot(high, low_ref[...]) + dot(low, high_ref[...]))


def final(span, *arrays):
    high, low = band()
    return pl.pallas_call(
        final_kernel,
        in_specs=[VMEM] * 10,
        out_specs=VMEM,
        out_shape=jax.ShapeDtypeStruct((S, span), F32),
        scratch_shapes=[
            pltpu.VMEM((NEXT, REACH), F32),
            pltpu.VMEM((S, span + 2 * HALF), F32),
        ],
        compiler_params=PARAMS,
        name="final",
    )(*arrays, jnp.asarray(high), jnp.asarray(low))


def moved(array, by_row, by_col):
    n_row, n_col = lax.axis_size("row"), lax.axis_size("col")
    if by_col == 0:
        return lax.ppermute(array, "row", [(i, (i + by_row) % n_row) for i in range(n_row)])
    if by_row == 0:
        return lax.ppermute(array, "col", [(i, (i + by_col) % n_col) for i in range(n_col)])
    pairs = [
        (r * n_col + c, (r + by_row) % n_row * n_col + (c + by_col) % n_col)
        for r in range(n_row)
        for c in range(n_col)
    ]
    return lax.ppermute(array, ("row", "col"), pairs)


def spilled(parts):
    own, after, far, back = parts
    return own, moved(after, 1, 0), moved(far, 2, 0), moved(back, -1, 0)


def behind(array, *others):
    return lax.optimization_barrier((array, *others))[0]


def on_device(source, boxes_a, shifts_a, widths_a, boxes_b, shifts_b, widths_b):
    shifts_a, widths_a, shifts_b, widths_b = (
        jnp.swapaxes(array, 1, 2) for array in (shifts_a, widths_a, shifts_b, widths_b))
    boxes_a = pltpu.with_memory_space_constraint(boxes_a, pltpu.HBM)
    boxes_b = pltpu.with_memory_space_constraint(boxes_b, pltpu.HBM)
    masses = pltpu.with_memory_space_constraint(source, pltpu.HBM)
    top03, bot03, left_top, left_bot, base = aligned(
        (0, 3), masses, boxes_a, shifts_a, widths_a)
    rtop03 = moved(top03, -1, 0)
    east = moved(left_bot, 0, -1)
    diag = moved(left_top, -1, -1)
    top12, bot12 = aligned(
        (1, 2), masses, boxes_a, shifts_a, widths_a, behind(base, bot03))
    rtop12 = moved(top12, -1, 0)
    own = [(bot03, 0), (bot03, 1), (bot12, 0), (bot12, 1), (bot12, 2), (bot12, 3), (bot03, 2),
           (bot03, 3), (east, 0)]
    below = [(rtop03, 0), (rtop03, 1), (rtop12, 0), (rtop12, 1), (rtop12, 2), (rtop12, 3),
             (rtop03, 2), (rtop03, 3), (diag, 0)]
    quads = {}
    for j in range(4):
        a, b = 2 * j + 1, 2 * j + 2
        quads[j] = [(array, (0, at)) for array, at in (own[a], own[b], below[a], below[b])]
        quads[j] += [
            (source, (1, a)),
            (source, (1, b)) if j < 3 else (east, (1, 0)),
        ]
        quads[j] += [(array, (1, at)) for array, at in (below[a], below[b])]
    own3, next3, far3, back3, carry = shifted(
        (3,), boxes_b, shifts_b, widths_b, behind(base, bot12), quads,
        finals=((1152, 1408),), kept=(768, 1152))
    next3 = moved(next3, 1, 0)
    far3 = moved(far3, 2, 0)
    own2, next2, far2, back2, carry = shifted(
        (0, 2), boxes_b, shifts_b, widths_b, base, quads,
        carried=(768, 1152), carry=(carry, back3), finals=((0, 256), (896, 1152)),
        kept=(256, 896))
    next2 = moved(next2, 1, 0)
    far2 = moved(far2, 2, 0)
    rback2 = moved(back2, -1, 0)
    own1, next1, far1, back1 = shifted(
        (1,), boxes_b, shifts_b, widths_b, base, quads,
        carried=(256, 896), carry=(behind(carry, next3, far3),),
        finals=((256, 896),))
    n_row = lax.axis_size("row")
    joined = lax.ppermute(
        behind(far1, far2, rback2), "row", [(i, i + 1) for i in range(0, n_row, 2)])
    far1 = lax.ppermute(far1, "row", [(i, (i + 2) % n_row) for i in range(1, n_row, 2)])
    back1 = moved(back1, -1, 0)
    main, right, east, west, next1 = edges(
        own3, next3, far3, own2, next2, far2, rback2, next1, joined)
    next1 = moved(next1, 1, 0)
    return final(
        source.shape[1], own1, next1, far1, back1, main, right, moved(east, 0, 1),
        moved(west, 0, -1))


def solution(mesh):
    cells = P("row", "col", None)
    boxes = P("row", "col", None, None)
    return jax.shard_map(
        on_device,
        mesh=mesh,
        in_specs=(P("row", "col"), boxes, cells, cells, boxes, cells, cells),
        out_specs=P("row", "col"),
        check_vma=False,
    )
```

```python
import functools
import math

import jax
import jax.numpy as jnp
import numpy as np
from jax import lax
from jax.experimental import pallas as pl
from jax.experimental.pallas import tpu as pltpu
from jax.sharding import PartitionSpec as P

S = 256
HALF = 128
BOX = 512
ITERS = 3
RADIUS = 8
REACH = BOX + HALF
EPS = 0.05
SIGMA = 2.0
F32 = jnp.float32
BF16 = jnp.bfloat16
OWN = S + RADIUS
NEXT = S + 2 * RADIUS
FAR = REACH - 2 * S + RADIUS
BASE = 904
VMEM = pl.BlockSpec(memory_space=pltpu.VMEM)
SMEM = pl.BlockSpec(memory_space=pltpu.SMEM)
ANY = pl.BlockSpec(memory_space=pl.ANY)
HBM = pl.BlockSpec(memory_space=pltpu.HBM)
PARAMS = pltpu.CompilerParams(vmem_limit_bytes=24 << 20)


def dot(a, b):
    return jnp.dot(a, b, preferred_element_type=F32)


def fill_base(ref):
    for c in range(0, BASE, 8 * 28):
        n = min(8 * 28, BASE - c)
        rows = lax.broadcasted_iota(jnp.int32, (n, HALF), 0)
        cols = lax.broadcasted_iota(jnp.int32, (n, HALF), 1)
        dist = (rows - cols + (c - 384)).astype(F32) / S
        ref[c : c + n] = jnp.exp(-dist * dist / EPS)


def window(ref, start):
    base = pl.multiple_of(start // 8 * 8, 8)
    rest = start - base
    tiles = ref[pl.ds(base, REACH + 8), :].reshape(REACH // 8 + 1, 8, HALF)
    tiles = pltpu.roll(tiles, jnp.where(rest == 0, 0, 8 - rest), 1)
    row = lax.broadcasted_iota(jnp.int32, (REACH // 8, 8, HALF), 1)
    return jnp.where(row < 8 - rest, tiles[:-1], tiles[1:]).reshape(REACH, HALF).astype(BF16)


def fill_tables(o_r, o_c, w_r, w_c, base_ref, refs):
    back_r, back_c, fwd_r, fwd_c = refs
    tall_r = window(base_ref, o_r + S)
    tall_c = window(base_ref, o_c + S)
    wide_r = window(base_ref, -o_r)
    wide_c = window(base_ref, -o_c)
    none = jnp.zeros((), BF16)
    lane = lax.broadcasted_iota(jnp.int32, (S, HALF), 1)
    deep = lax.broadcasted_iota(jnp.int32, (BOX, HALF), 0)
    for k in range(BOX // HALF):
        at = slice(k * HALF, (k + 1) * HALF)
        rows = slice(384 - HALF * k, 640 - HALF * k)
        back_c[:, at] = wide_c[rows]
        fwd_r[:, at] = jnp.where(lane + k * HALF < w_r, wide_r[rows], none)
    for k in range(S // HALF):
        at = slice(k * HALF, (k + 1) * HALF)
        rows = slice(HALF - HALF * k, REACH - HALF * k)
        back_r[:, at] = tall_r[rows]
        fwd_c[:, at] = jnp.where(deep < w_c, tall_c[rows], none)


def table_scratch():
    return [
        pltpu.VMEM((BOX, S), BF16),
        pltpu.VMEM((S, BOX), BF16),
        pltpu.VMEM((S, BOX), BF16),
        pltpu.VMEM((BOX, S), BF16),
    ]


def forward(mass, tables, vb_ref):
    inner = dot(tables[2][...], vb_ref[...]).astype(BF16)
    return mass / dot(inner, tables[3][...])


def fetch(boxes, cells, ref, sems):
    copies = [
        pltpu.make_async_copy(boxes.at[0, j], ref.at[i], sems.at[i]) for i, j in enumerate(cells)
    ]
    for copy in copies:
        copy.start()
    return copies


def aligned_kernel(cells, later, shifts, widths, source, boxes, later_boxes, *refs):
    n = len(cells)
    if 0 in cells:
        outs, base_ref, later_ref, box_ref, refs = refs[:4], refs[4], refs[5], refs[6], refs[7:]
    else:
        base_ref, outs, later_ref, refs = refs[0], refs[1:3], refs[3], refs[4:]
        box_ref = boxes
    mass_ref, vb_ref, tables, sems, later_sems = refs
    copies = []
    for i, j in enumerate(cells):
        copies.append([
            pltpu.make_async_copy(
                source.at[:, pl.ds(j * S, S)], mass_ref.at[:, pl.ds(i * S, S)], sems.at[i, 1]),
        ])
        if 0 in cells:
            copies[i].append(pltpu.make_async_copy(boxes.at[0, j], box_ref.at[i], sems.at[i, 0]))
    for pair in copies:
        for copy in reversed(pair):
            copy.start()
    if 0 in cells:
        fill_base(base_ref)
    for i, j in enumerate(cells):
        fill_tables(
            shifts[0, 0, j], shifts[0, 1, j], widths[0, 0, j], widths[0, 1, j], base_ref, tables[i])
    scales = []
    for i in range(n):
        down = dot(tables[i][0][...], jnp.ones((S, HALF), BF16)).astype(BF16).astype(F32)
        across = dot(jnp.ones((8, S), BF16), tables[i][1][...])
        scales.append(((1.0 / down)[:, :1], (1.0 / across)[:1]))
    u = [None] * n
    for step in range(ITERS):
        for i in range(n):
            if step == 0:
                for copy in copies[i]:
                    copy.wait()
                if i == n - 1:
                    later_copies = fetch(later_boxes, later, later_ref, later_sems)
                down, across = scales[i]
                for c in range(0, BOX, HALF):
                    v = box_ref[i, c : c + HALF] * down[c : c + HALF] * across
                    vb_ref[i, c : c + HALF] = v.astype(BF16)
            else:
                inner = dot(tables[i][0][...], u[i].astype(BF16)).astype(BF16)
                vb_ref[i] = (box_ref[i] / dot(inner, tables[i][1][...])).astype(BF16)
        for i in range(n):
            u[i] = forward(mass_ref[:, i * S : (i + 1) * S], tables[i], vb_ref.at[i])
    for i, j in enumerate(cells):
        outs[0][:HALF, i * S : (i + 1) * S] = u[i][:HALF]
        outs[0][HALF:, i * S : (i + 1) * S] = mass_ref[:HALF, i * S : (i + 1) * S]
        outs[1][:, i * S : (i + 1) * S] = u[i][HALF:]
        if j == 0:
            for k in range(2):
                outs[2 + k][:HALF] = u[i][k * HALF : (k + 1) * HALF, :HALF]
                outs[2 + k][HALF:] = mass_ref[k * HALF : (k + 1) * HALF, i * S : i * S + HALF]
    for copy in later_copies:
        copy.wait()


def cost(cells, applies):
    return pl.CostEstimate(
        flops=cells * applies * 804_000_000, bytes_accessed=cells << 20, transcendentals=0)


def aligned(cells, later, source, boxes, later_boxes, shifts, widths, *base):
    n = len(cells)
    corner = jax.ShapeDtypeStruct((S, HALF), F32)
    shapes = [jax.ShapeDtypeStruct((S, n * S), F32), jax.ShapeDtypeStruct((HALF, n * S), F32)]
    scratch = []
    if 0 in cells:
        shapes += [corner, corner, jax.ShapeDtypeStruct((BASE, HALF), F32)]
        scratch.append(pltpu.VMEM((n, BOX, BOX), F32))
    shapes.append(jax.ShapeDtypeStruct((len(later), BOX, BOX), F32))
    return pl.pallas_call(
        functools.partial(aligned_kernel, cells, later),
        in_specs=[SMEM, SMEM, HBM, HBM if 0 in cells else VMEM, HBM] + [VMEM] * len(base),
        out_specs=[VMEM] * len(shapes),
        out_shape=shapes,
        scratch_shapes=scratch + [
            pltpu.VMEM((S, n * S), F32),
            pltpu.VMEM((n, BOX, BOX), BF16),
            [table_scratch() for _ in cells],
            pltpu.SemaphoreType.DMA((n, 2)),
            pltpu.SemaphoreType.DMA((len(later),)),
        ],
        compiler_params=PARAMS,
        cost_estimate=cost(n, 5),
        name="aligned",
    )(shifts, widths, source, boxes, later_boxes, *base)


def place(plan_ref, top, left, canvas_ref, first):
    base = pl.multiple_of(top // 8 * 8, 8)
    rest = top - base
    row = lax.broadcasted_iota(jnp.int32, (HALF // 8 + 1, 8, BOX), 1)
    column = lax.broadcasted_iota(jnp.int32, (HALF + 8, HALF), 1)
    none = jnp.zeros((1, 8, BOX), F32)
    for c in range(0, BOX, HALF):
        turned = pltpu.roll(plan_ref[c : c + HALF].reshape(HALF // 8, 8, BOX), rest, 1)
        rows = jnp.where(
            row < rest,
            jnp.concatenate([none, turned], 0),
            jnp.concatenate([turned, none], 0),
        ).reshape(HALF + 8, BOX)
        before = jnp.zeros((HALF + 8, HALF), F32)
        for k in range(BOX // HALF + 1):
            now = jnp.zeros((HALF + 8, HALF), F32)
            if k < BOX // HALF:
                now = pltpu.roll(rows[:, k * HALF : (k + 1) * HALF], left, 1)
            at = (pl.ds(base + c, HALF + 8), slice(first + k * HALF, first + (k + 1) * HALF))
            canvas_ref[at] = canvas_ref[at] + jnp.where(column < left, before, now)
            before = now


def shifted_kernel(cells, later, origin, carried, finals, kept, quads, count, shifts, widths,
                   box_ref, base_ref, *refs):
    n = len(cells)
    arrays, refs = refs[:count], refs[count:]
    upper_ref = None
    if carried:
        carry_ref, refs = refs[0], refs[1:]
        if kept:
            upper_ref, refs = refs[0], refs[1:]
    if later:
        later_boxes, refs = refs[0], refs[1:]
    outs, refs = refs[:4], refs[4:]
    if kept:
        keep_ref, refs = refs[0], refs[1:]
    if later:
        later_ref, refs = refs[0], refs[1:]
    mass_ref, ub_ref, vb_ref, v_ref, canvas_ref, tables, sems, out_sems = refs
    later_copies = fetch(later_boxes, later, later_ref, sems) if later else []
    canvas_ref[...] = jnp.zeros_like(canvas_ref)
    if carried:
        first, last = carried[0] - origin, carried[1] - origin
        canvas_ref[:REACH, first:last] = carry_ref[...]
    for i, j in enumerate(cells):
        fill_tables(
            shifts[0, 0, j], shifts[0, 1, j], widths[0, 0, j], widths[0, 1, j], base_ref, tables[i])
        for k in range(4):
            rows = slice(k // 2 * HALF, (k // 2 + 1) * HALF)
            cols = slice(k % 2 * HALF, (k % 2 + 1) * HALF)
            for ref, (array, down, across) in (
                (ub_ref, quads[i][k]), (mass_ref, quads[i][4 + k])
            ):
                part = arrays[array][
                    down * HALF : (down + 1) * HALF, across * HALF : (across + 1) * HALF]
                ref[i, rows, cols] = part.astype(ref.dtype)
    u = [ub_ref[i] for i in range(n)]
    for step in range(ITERS):
        for i in range(n):
            inner = dot(tables[i][0][...], u[i]).astype(BF16)
            den = dot(inner, tables[i][1][...])
            v = box_ref[i] / den
            if step == ITERS - 1:
                v_ref[i] = v
            vb_ref[i] = v.astype(BF16)
        for i in range(n):
            u[i] = forward(mass_ref[i], tables[i], vb_ref.at[i]).astype(BF16)
    deep = lax.broadcasted_iota(jnp.int32, (BOX, S), 0)
    lane = lax.broadcasted_iota(jnp.int32, (S, BOX), 1)
    for i, j in enumerate(cells):
        inner = jnp.where(deep < widths[0, 0, j], dot(tables[i][0][...], u[i]), 0.0).astype(BF16)
        used = jnp.where(lane < widths[0, 1, j], tables[i][1][...], jnp.zeros((), BF16))
        v_ref[i] = v_ref[i] * dot(inner, used)
    for i, j in enumerate(cells):
        place(v_ref.at[i], shifts[0, 0, j] + HALF, shifts[0, 1, j] + HALF, canvas_ref,
              j * S - origin)
    writes = []
    at = 0
    for first, last in finals:
        size = last - first
        for ref, row in zip(outs, (0, S - RADIUS, 2 * S - RADIUS, 0)):
            writes.append(pltpu.make_async_copy(
                canvas_ref.at[pl.ds(row, ref.shape[0]), pl.ds(first - origin, size)],
                ref.at[:, pl.ds(at, size)],
                out_sems.at[len(writes)]))
        at += size
    if upper_ref is not None:
        writes.append(pltpu.make_async_copy(
            upper_ref, outs[3].at[:, pl.ds(at, upper_ref.shape[1])], out_sems.at[len(writes)]))
    if kept:
        size = kept[1] - kept[0]
        writes.append(pltpu.make_async_copy(
            canvas_ref.at[pl.ds(0, REACH), pl.ds(kept[0] - origin, size)], keep_ref,
            out_sems.at[len(writes)]))
    for copy in writes:
        copy.start()
    for copy in writes + later_copies:
        copy.wait()


def shifted(cells, later, boxes, later_boxes, shifts, widths, base, quads, carried=None,
            carry=(), finals=(), kept=None):
    n = len(cells)
    origin = min(j * S for j in cells)
    width = max(j * S + REACH for j in cells) - origin
    total = sum(last - first for first, last in finals)
    shapes = [jax.ShapeDtypeStruct((rows, total), F32) for rows in (OWN, NEXT, FAR, RADIUS)]
    if kept:
        if carried:
            shapes[3] = jax.ShapeDtypeStruct((RADIUS, total + carry[1].shape[1]), F32)
        shapes.append(jax.ShapeDtypeStruct((REACH, kept[1] - kept[0]), F32))
    outs = [ANY] * len(shapes)
    if later:
        shapes.append(jax.ShapeDtypeStruct((len(later), BOX, BOX), F32))
        outs.append(VMEM)
    arrays, where = [], []
    for j in cells:
        where.append([])
        for array, (down, across) in quads[j]:
            known = [k for k, other in enumerate(arrays) if other is array]
            if not known:
                known = [len(arrays)]
                arrays.append(array)
            where[-1].append((known[0], down, across))
    count = len(arrays)
    arrays += carry
    return pl.pallas_call(
        functools.partial(
            shifted_kernel, cells, later, origin, carried, finals, kept, where, count),
        in_specs=[SMEM, SMEM, VMEM, VMEM] + [VMEM] * len(arrays) + [HBM] * bool(later),
        out_specs=outs,
        out_shape=shapes,
        scratch_shapes=[
            pltpu.VMEM((n, S, S), F32),
            pltpu.VMEM((n, S, S), BF16),
            pltpu.VMEM((n, BOX, BOX), BF16),
            pltpu.VMEM((n, BOX, BOX), F32),
            pltpu.VMEM((REACH + 8, width), F32),
            [table_scratch() for _ in cells],
            pltpu.SemaphoreType.DMA((max(1, len(later)),)),
            pltpu.SemaphoreType.DMA((4 * len(finals) + 2,)),
        ],
        compiler_params=PARAMS,
        cost_estimate=cost(n, 7),
        name="shifted",
    )(shifts, widths, boxes, base, *arrays, *([later_boxes] if later else []))


def blur_weights():
    raw = [math.exp(-(d * d) / (2.0 * SIGMA * SIGMA)) for d in range(-RADIUS, RADIUS + 1)]
    total = sum(raw)
    return [w / total for w in raw]


def blurred_rows(own_ref, next_ref, far_ref, back_ref, win_ref, width, put):
    win_ref[:, :width] = next_ref[...]
    win_ref[RADIUS:, :width] = win_ref[RADIUS:, :width] + own_ref[...]
    win_ref[:FAR, :width] = win_ref[:FAR, :width] + far_ref[...]
    win_ref[NEXT - RADIUS :, :width] = win_ref[NEXT - RADIUS :, :width] + back_ref[...]
    weights = blur_weights()
    for c in range(0, width, HALF):
        col = win_ref[:, c : c + HALF]
        out = weights[RADIUS] * col[RADIUS : RADIUS + S]
        for d in range(1, RADIUS + 1):
            out = out + weights[RADIUS + d] * (
                col[RADIUS + d : RADIUS + d + S] + col[RADIUS - d : RADIUS - d + S])
        put(c, out)


def edges_kernel(*refs):
    (own3, next3, far3, own2, next2, far2, back2, main_ref, right_ref, east_ref, west_ref,
     win_ref) = refs

    def outer(c, out):
        east_ref[:S, HALF + c : 2 * HALF + c] = out

    def inner(c, out):
        if c < 3 * HALF:
            main_ref[:, c : c + HALF] = out
        else:
            east_ref[:S, :HALF] = out
            right_ref[...] = out
        if c == 0:
            west_ref[...] = out.T[:RADIUS]
        if c == 2 * HALF:
            east_ref[S:, :S] = out.T[HALF - RADIUS :]
            east_ref[S:, S:] = jnp.zeros((RADIUS, HALF), F32)

    blurred_rows(own3, next3, far3, back2.at[:, 2 * S :], win_ref, S, outer)
    blurred_rows(own2, next2, far2, back2.at[:, : 2 * S], win_ref, 2 * S, inner)


def edges(*arrays):
    return pl.pallas_call(
        edges_kernel,
        in_specs=[VMEM] * 7,
        out_specs=[VMEM] * 4,
        out_shape=[
            jax.ShapeDtypeStruct((S, 3 * HALF), F32),
            jax.ShapeDtypeStruct((S, HALF), F32),
            jax.ShapeDtypeStruct((S + RADIUS, 3 * HALF), F32),
            jax.ShapeDtypeStruct((RADIUS, S), F32),
        ],
        scratch_shapes=[pltpu.VMEM((NEXT, 2 * S), F32)],
        compiler_params=PARAMS,
        name="edges",
    )(*arrays)


def band():
    full = np.zeros((2 * S, S), np.float64)
    for j in range(S):
        for d, w in zip(range(-RADIUS, RADIUS + 1), blur_weights()):
            full[j + HALF + d, j] = w
    high = full.astype(jnp.bfloat16)
    return high, (full - high.astype(np.float64)).astype(jnp.bfloat16)


def final_kernel(own1, next1, far1, back1, main_ref, right_ref, east_ref, west_ref, high_ref,
                 low_ref, out_ref, rows_ref, win_ref):
    span = out_ref.shape[1]
    none = jnp.zeros((HALF - RADIUS, S), F32)
    win_ref[:, :HALF] = jnp.concatenate([none, east_ref[S:, :S]], 0).T
    win_ref[:, HALF : HALF + S] = main_ref[:, :S] + east_ref[:S, :S]
    win_ref[:, HALF + 7 * HALF : HALF + span] = main_ref[:, S:]
    win_ref[:, HALF + span :] = right_ref[...] + jnp.concatenate([west_ref[...], none], 0).T

    def middle(c, out):
        if c == 0:
            out = out + east_ref[:S, S:]
        win_ref[:, HALF + S + c : 2 * HALF + S + c] = out

    blurred_rows(own1, next1, far1, back1, rows_ref, REACH, middle)
    for c in range(0, span, S):
        strip = win_ref[:, c : c + 2 * S]
        high = strip.astype(BF16)
        low = (strip - high.astype(F32)).astype(BF16)
        out_ref[:, c : c + S] = (
            dot(high, high_ref[...]) + dot(high, low_ref[...]) + dot(low, high_ref[...]))


def final(span, *arrays):
    high, low = band()
    return pl.pallas_call(
        final_kernel,
        in_specs=[VMEM] * 10,
        out_specs=VMEM,
        out_shape=jax.ShapeDtypeStruct((S, span), F32),
        scratch_shapes=[
            pltpu.VMEM((NEXT, REACH), F32),
            pltpu.VMEM((S, span + 2 * HALF), F32),
        ],
        compiler_params=PARAMS,
        name="final",
    )(*arrays, jnp.asarray(high), jnp.asarray(low))


def moved(array, by_row, by_col):
    n_row, n_col = lax.axis_size("row"), lax.axis_size("col")
    if by_col == 0:
        return lax.ppermute(array, "row", [(i, (i + by_row) % n_row) for i in range(n_row)])
    if by_row == 0:
        return lax.ppermute(array, "col", [(i, (i + by_col) % n_col) for i in range(n_col)])
    pairs = [
        (r * n_col + c, (r + by_row) % n_row * n_col + (c + by_col) % n_col)
        for r in range(n_row)
        for c in range(n_col)
    ]
    return lax.ppermute(array, ("row", "col"), pairs)


def spilled(parts):
    own, after, far, back = parts
    return own, moved(after, 1, 0), moved(far, 2, 0), moved(back, -1, 0)


def behind(array, *others):
    return lax.optimization_barrier((array, *others))[0]


def on_device(source, boxes_a, shifts_a, widths_a, boxes_b, shifts_b, widths_b):
    shifts_a, widths_a, shifts_b, widths_b = (
        jnp.swapaxes(array, 1, 2) for array in (shifts_a, widths_a, shifts_b, widths_b))
    boxes_a = pltpu.with_memory_space_constraint(boxes_a, pltpu.HBM)
    boxes_b = pltpu.with_memory_space_constraint(boxes_b, pltpu.HBM)
    masses = pltpu.with_memory_space_constraint(source, pltpu.HBM)
    shifts_a = pltpu.with_memory_space_constraint(shifts_a, pltpu.HBM)
    widths_a = pltpu.with_memory_space_constraint(widths_a, pltpu.HBM)
    top03, bot03, left_top, left_bot, base, boxes12 = aligned(
        (0, 3), (1, 2), masses, boxes_a, boxes_a, shifts_a, widths_a)
    rtop03 = moved(top03, -1, 0)
    east = moved(left_bot, 0, -1)
    diag = moved(left_top, -1, -1)
    top12, bot12, boxes3 = aligned(
        (1, 2), (3,), masses, boxes12, boxes_b, shifts_a, widths_a, base)
    rtop12 = moved(top12, -1, 0)
    own = [(bot03, 0), (bot03, 1), (bot12, 0), (bot12, 1), (bot12, 2), (bot12, 3), (bot03, 2),
           (bot03, 3), (east, 0)]
    below = [(rtop03, 0), (rtop03, 1), (rtop12, 0), (rtop12, 1), (rtop12, 2), (rtop12, 3),
             (rtop03, 2), (rtop03, 3), (diag, 0)]
    quads = {}
    for j in range(4):
        a, b = 2 * j + 1, 2 * j + 2
        quads[j] = [(array, (0, at)) for array, at in (own[a], own[b], below[a], below[b])]
        quads[j] += [
            (source, (1, a)),
            (source, (1, b)) if j < 3 else (east, (1, 0)),
        ]
        quads[j] += [(array, (1, at)) for array, at in (below[a], below[b])]
    own3, next3, far3, back3, carry, boxes02 = shifted(
        (3,), (0, 2), boxes3, boxes_b, shifts_b, widths_b, base, quads,
        finals=((1152, 1408),), kept=(768, 1152))
    next3 = moved(next3, 1, 0)
    far3 = moved(far3, 2, 0)
    own2, next2, far2, back2, carry, boxes1 = shifted(
        (0, 2), (1,), boxes02, boxes_b, shifts_b, widths_b, base, quads,
        carried=(768, 1152), carry=(carry, back3), finals=((0, 256), (896, 1152)),
        kept=(256, 896))
    next2 = moved(next2, 1, 0)
    far2 = moved(far2, 2, 0)
    rback2 = moved(back2, -1, 0)
    own1, next1, far1, back1 = shifted(
        (1,), (), boxes1, None, shifts_b, widths_b, base, quads,
        carried=(256, 896), carry=(behind(carry, next3, far3),),
        finals=((256, 896),))
    n_row = lax.axis_size("row")
    joined = lax.ppermute(
        behind(far1, far2, rback2), "row", [(i, i + 1) for i in range(0, n_row, 2)])
    far1 = lax.ppermute(far1, "row", [(i, (i + 2) % n_row) for i in range(1, n_row, 2)])
    back1 = moved(back1, -1, 0)
    next1 = moved(next1.at[:FAR].add(behind(joined, next2)), 1, 0)
    main, right, east, west = edges(own3, next3, far3, own2, next2, far2, rback2)
    return final(
        source.shape[1], own1, next1, far1, back1, main, right, moved(east, 0, 1),
        moved(west, 0, -1))


def solution(mesh):
    cells = P("row", "col", None)
    boxes = P("row", "col", None, None)
    return jax.shard_map(
        on_device,
        mesh=mesh,
        in_specs=(P("row", "col"), boxes, cells, cells, boxes, cells, cells),
        out_specs=P("row", "col"),
        check_vma=False,
    )
```

```python
import functools
import math

import jax
import jax.numpy as jnp
import numpy as np
from jax import lax
from jax.experimental import pallas as pl
from jax.experimental.pallas import tpu as pltpu
from jax.sharding import PartitionSpec as P

S = 256
HALF = 128
BOX = 512
ITERS = 3
RADIUS = 8
REACH = BOX + HALF
EPS = 0.05
SIGMA = 2.0
F32 = jnp.float32
BF16 = jnp.bfloat16
OWN = S + RADIUS
NEXT = S + 2 * RADIUS
FAR = REACH - 2 * S + RADIUS
BASE = 904
VMEM = pl.BlockSpec(memory_space=pltpu.VMEM)
SMEM = pl.BlockSpec(memory_space=pltpu.SMEM)
ANY = pl.BlockSpec(memory_space=pl.ANY)
HBM = pl.BlockSpec(memory_space=pltpu.HBM)
PARAMS = pltpu.CompilerParams(vmem_limit_bytes=24 << 20)


def dot(a, b):
    return jnp.dot(a, b, preferred_element_type=F32)


def fill_base(ref):
    for c in range(0, BASE, 8 * 28):
        n = min(8 * 28, BASE - c)
        rows = lax.broadcasted_iota(jnp.int32, (n, HALF), 0)
        cols = lax.broadcasted_iota(jnp.int32, (n, HALF), 1)
        dist = (rows - cols + (c - 384)).astype(F32) / S
        ref[c : c + n] = jnp.exp(-dist * dist / EPS)


def window(ref, start):
    base = pl.multiple_of(start // 8 * 8, 8)
    rest = start - base
    tiles = ref[pl.ds(base, REACH + 8), :].reshape(REACH // 8 + 1, 8, HALF)
    tiles = pltpu.roll(tiles, jnp.where(rest == 0, 0, 8 - rest), 1)
    row = lax.broadcasted_iota(jnp.int32, (REACH // 8, 8, HALF), 1)
    return jnp.where(row < 8 - rest, tiles[:-1], tiles[1:]).reshape(REACH, HALF).astype(BF16)


def fill_tables(o_r, o_c, w_r, w_c, base_ref, refs):
    back_r, back_c, fwd_r, fwd_c = refs
    tall_r = window(base_ref, o_r + S)
    tall_c = window(base_ref, o_c + S)
    wide_r = window(base_ref, -o_r)
    wide_c = window(base_ref, -o_c)
    none = jnp.zeros((), BF16)
    lane = lax.broadcasted_iota(jnp.int32, (S, HALF), 1)
    deep = lax.broadcasted_iota(jnp.int32, (BOX, HALF), 0)
    for k in range(BOX // HALF):
        at = slice(k * HALF, (k + 1) * HALF)
        rows = slice(384 - HALF * k, 640 - HALF * k)
        back_c[:, at] = wide_c[rows]
        fwd_r[:, at] = jnp.where(lane + k * HALF < w_r, wide_r[rows], none)
    for k in range(S // HALF):
        at = slice(k * HALF, (k + 1) * HALF)
        rows = slice(HALF - HALF * k, REACH - HALF * k)
        back_r[:, at] = tall_r[rows]
        fwd_c[:, at] = jnp.where(deep < w_c, tall_c[rows], none)


def table_scratch():
    return [
        pltpu.VMEM((BOX, S), BF16),
        pltpu.VMEM((S, BOX), BF16),
        pltpu.VMEM((S, BOX), BF16),
        pltpu.VMEM((BOX, S), BF16),
    ]


def forward(mass, tables, vb_ref):
    inner = dot(tables[2][...], vb_ref[...]).astype(BF16)
    return mass / dot(inner, tables[3][...])


def fetch(boxes, cells, ref, sems):
    copies = [
        pltpu.make_async_copy(boxes.at[0, j], ref.at[i], sems.at[i]) for i, j in enumerate(cells)
    ]
    for copy in copies:
        copy.start()
    return copies


def aligned_kernel(cells, later, shifts, widths, source, boxes, later_boxes, *refs):
    n = len(cells)
    if 0 in cells:
        outs, base_ref, later_ref, box_ref, refs = refs[:4], refs[4], refs[5], refs[6], refs[7:]
    else:
        base_ref, outs, later_ref, refs = refs[0], refs[1:3], refs[3], refs[4:]
        box_ref = boxes
    copies = [[] for _ in cells]
    if 0 in cells:
        mass_ref, vb_ref, tables, sems, later_sems = refs
        masses = [mass_ref.at[:, pl.ds(i * S, S)] for i in range(n)]
        for i, j in enumerate(cells):
            copies[i] += [
                pltpu.make_async_copy(source.at[:, pl.ds(j * S, S)], masses[i], sems.at[i, 1]),
                pltpu.make_async_copy(boxes.at[0, j], box_ref.at[i], sems.at[i, 0]),
            ]
    else:
        vb_ref, tables, later_sems = refs
        masses = [source.at[:, pl.ds(j * S, S)] for j in cells]
    for pair in copies:
        for copy in reversed(pair):
            copy.start()
    if 0 in cells:
        fill_base(base_ref)
    for i, j in enumerate(cells):
        fill_tables(
            shifts[0, 0, j], shifts[0, 1, j], widths[0, 0, j], widths[0, 1, j], base_ref, tables[i])
    scales = []
    for i in range(n):
        down = dot(tables[i][0][...], jnp.ones((S, HALF), BF16)).astype(BF16).astype(F32)
        across = dot(jnp.ones((8, S), BF16), tables[i][1][...])
        scales.append(((1.0 / down)[:, :1], (1.0 / across)[:1]))
    u = [None] * n
    for step in range(ITERS):
        for i in range(n):
            if step == 0:
                for copy in copies[i]:
                    copy.wait()
                if i == n - 1:
                    later_copies = fetch(later_boxes, later, later_ref, later_sems)
                down, across = scales[i]
                for c in range(0, BOX, HALF):
                    v = box_ref[i, c : c + HALF] * down[c : c + HALF] * across
                    vb_ref[i, c : c + HALF] = v.astype(BF16)
            else:
                inner = dot(tables[i][0][...], u[i].astype(BF16)).astype(BF16)
                vb_ref[i] = (box_ref[i] / dot(inner, tables[i][1][...])).astype(BF16)
        for i in range(n):
            u[i] = forward(masses[i][...], tables[i], vb_ref.at[i])
    for i, j in enumerate(cells):
        outs[0][:HALF, i * S : (i + 1) * S] = u[i][:HALF]
        outs[0][HALF:, i * S : (i + 1) * S] = masses[i][:HALF]
        outs[1][:, i * S : (i + 1) * S] = u[i][HALF:]
        if j == 0:
            for k in range(2):
                outs[2 + k][:HALF] = u[i][k * HALF : (k + 1) * HALF, :HALF]
                outs[2 + k][HALF:] = masses[i][k * HALF : (k + 1) * HALF, :HALF]
    for copy in later_copies:
        copy.wait()


def cost(cells, applies):
    return pl.CostEstimate(
        flops=cells * applies * 804_000_000, bytes_accessed=cells << 20, transcendentals=0)


def aligned(cells, later, source, boxes, later_boxes, shifts, widths, *base):
    n = len(cells)
    corner = jax.ShapeDtypeStruct((S, HALF), F32)
    shapes = [jax.ShapeDtypeStruct((S, n * S), F32), jax.ShapeDtypeStruct((HALF, n * S), F32)]
    scratch = []
    if 0 in cells:
        shapes += [corner, corner, jax.ShapeDtypeStruct((BASE, HALF), F32)]
        scratch += [pltpu.VMEM((n, BOX, BOX), F32), pltpu.VMEM((S, n * S), F32)]
    shapes.append(jax.ShapeDtypeStruct((len(later), BOX, BOX), F32))
    return pl.pallas_call(
        functools.partial(aligned_kernel, cells, later),
        in_specs=[SMEM, SMEM] + ([HBM, HBM] if 0 in cells else [VMEM, VMEM]) + [HBM] + [VMEM] * len(base),
        out_specs=[VMEM] * len(shapes),
        out_shape=shapes,
        scratch_shapes=scratch + [
            pltpu.VMEM((n, BOX, BOX), BF16),
            [table_scratch() for _ in cells],
        ] + [pltpu.SemaphoreType.DMA((n, 2))] * (0 in cells) + [
            pltpu.SemaphoreType.DMA((len(later),)),
        ],
        compiler_params=PARAMS,
        cost_estimate=cost(n, 5),
        name="aligned",
    )(shifts, widths, source, boxes, later_boxes, *base)


def place(plan_ref, top, left, canvas_ref, first):
    base = pl.multiple_of(top // 8 * 8, 8)
    rest = top - base
    row = lax.broadcasted_iota(jnp.int32, (HALF // 8 + 1, 8, BOX), 1)
    column = lax.broadcasted_iota(jnp.int32, (HALF + 8, HALF), 1)
    none = jnp.zeros((1, 8, BOX), F32)
    for c in range(0, BOX, HALF):
        turned = pltpu.roll(plan_ref[c : c + HALF].reshape(HALF // 8, 8, BOX), rest, 1)
        rows = jnp.where(
            row < rest,
            jnp.concatenate([none, turned], 0),
            jnp.concatenate([turned, none], 0),
        ).reshape(HALF + 8, BOX)
        before = jnp.zeros((HALF + 8, HALF), F32)
        for k in range(BOX // HALF + 1):
            now = jnp.zeros((HALF + 8, HALF), F32)
            if k < BOX // HALF:
                now = pltpu.roll(rows[:, k * HALF : (k + 1) * HALF], left, 1)
            at = (pl.ds(base + c, HALF + 8), slice(first + k * HALF, first + (k + 1) * HALF))
            canvas_ref[at] = canvas_ref[at] + jnp.where(column < left, before, now)
            before = now


def shifted_kernel(cells, later, origin, carried, finals, quads, count, shifts, widths, box_ref,
                   base_ref, *refs):
    n = len(cells)
    arrays, refs = refs[:count], refs[count:]
    if carried:
        carry_ref, upper_ref, refs = refs[0], refs[1], refs[2:]
    if later:
        later_boxes, refs = refs[0], refs[1:]
    canvas_ref, outs, refs = refs[0], refs[1:4], refs[4:]
    if later:
        later_ref, refs = refs[0], refs[1:]
    mass_ref, ub_ref, vb_ref, v_ref, tables, sems = refs
    later_copies = fetch(later_boxes, later, later_ref, sems) if later else []
    canvas_ref[...] = jnp.zeros_like(canvas_ref)
    if carried:
        first, last, start = carried
        canvas_ref[:, first - origin : last - origin] = carry_ref[
            :, first - start : last - start]
    for i, j in enumerate(cells):
        fill_tables(
            shifts[0, 0, j], shifts[0, 1, j], widths[0, 0, j], widths[0, 1, j], base_ref, tables[i])
        for k in range(4):
            rows = slice(k // 2 * HALF, (k // 2 + 1) * HALF)
            cols = slice(k % 2 * HALF, (k % 2 + 1) * HALF)
            for ref, (array, down, across) in (
                (ub_ref, quads[i][k]), (mass_ref, quads[i][4 + k])
            ):
                part = arrays[array][
                    down * HALF : (down + 1) * HALF, across * HALF : (across + 1) * HALF]
                ref[i, rows, cols] = part.astype(ref.dtype)
    u = [ub_ref[i] for i in range(n)]
    for step in range(ITERS):
        for i in range(n):
            inner = dot(tables[i][0][...], u[i]).astype(BF16)
            den = dot(inner, tables[i][1][...])
            v = box_ref[i] / den
            if step == ITERS - 1:
                v_ref[i] = v
            vb_ref[i] = v.astype(BF16)
        for i in range(n):
            u[i] = forward(mass_ref[i], tables[i], vb_ref.at[i]).astype(BF16)
    deep = lax.broadcasted_iota(jnp.int32, (BOX, S), 0)
    lane = lax.broadcasted_iota(jnp.int32, (S, BOX), 1)
    for i, j in enumerate(cells):
        inner = jnp.where(deep < widths[0, 0, j], dot(tables[i][0][...], u[i]), 0.0).astype(BF16)
        used = jnp.where(lane < widths[0, 1, j], tables[i][1][...], jnp.zeros((), BF16))
        v_ref[i] = v_ref[i] * dot(inner, used)
    for i, j in enumerate(cells):
        place(v_ref.at[i], shifts[0, 0, j] + HALF, shifts[0, 1, j] + HALF, canvas_ref,
              j * S - origin)
    at = 0
    for first, last in finals:
        for ref, row in zip(outs, (S - RADIUS, 2 * S - RADIUS, 0)):
            ref[:, at : at + last - first] = canvas_ref[
                row : row + ref.shape[0], first - origin : last - origin]
        at += last - first
    if carried and later:
        outs[2][:, at:] = upper_ref[...]
    for copy in later_copies:
        copy.wait()


def shifted(cells, later, boxes, later_boxes, shifts, widths, base, quads, carried=None,
            carry=(), finals=()):
    n = len(cells)
    origin = min(j * S for j in cells)
    width = max(j * S + REACH for j in cells) - origin
    total = sum(last - first for first, last in finals)
    upper = carry[1].shape[1] if carried and later else 0
    shapes = [
        jax.ShapeDtypeStruct((REACH + 8, width), F32),
        jax.ShapeDtypeStruct((NEXT, total), F32),
        jax.ShapeDtypeStruct((FAR, total), F32),
        jax.ShapeDtypeStruct((RADIUS, total + upper), F32),
    ]
    if later:
        shapes.append(jax.ShapeDtypeStruct((len(later), BOX, BOX), F32))
    arrays, where = [], []
    for j in cells:
        where.append([])
        for array, (down, across) in quads[j]:
            known = [k for k, other in enumerate(arrays) if other is array]
            if not known:
                known = [len(arrays)]
                arrays.append(array)
            where[-1].append((known[0], down, across))
    count = len(arrays)
    arrays += carry
    return pl.pallas_call(
        functools.partial(
            shifted_kernel, cells, later, origin, carried, finals, where, count),
        in_specs=[SMEM, SMEM, VMEM, VMEM] + [VMEM] * len(arrays) + [HBM] * bool(later),
        out_specs=[VMEM] * len(shapes),
        out_shape=shapes,
        scratch_shapes=[
            pltpu.VMEM((n, S, S), F32),
            pltpu.VMEM((n, S, S), BF16),
            pltpu.VMEM((n, BOX, BOX), BF16),
            pltpu.VMEM((n, BOX, BOX), F32),
            [table_scratch() for _ in cells],
            pltpu.SemaphoreType.DMA((max(1, len(later)),)),
        ],
        compiler_params=PARAMS,
        cost_estimate=cost(n, 7),
        name="shifted",
    )(shifts, widths, boxes, base, *arrays, *([later_boxes] if later else []))


def blur_weights():
    raw = [math.exp(-(d * d) / (2.0 * SIGMA * SIGMA)) for d in range(-RADIUS, RADIUS + 1)]
    total = sum(raw)
    return [w / total for w in raw]


def blurred_rows(own, next_ref, far_ref, back_ref, win_ref, width, put):
    win_ref[:, :width] = next_ref[...]
    at = 0
    for part in own:
        cols = slice(at, at + part.shape[1])
        win_ref[RADIUS:, cols] = win_ref[RADIUS:, cols] + part[...]
        at += part.shape[1]
    win_ref[:FAR, :width] = win_ref[:FAR, :width] + far_ref[...]
    win_ref[NEXT - RADIUS :, :width] = win_ref[NEXT - RADIUS :, :width] + back_ref[...]
    weights = blur_weights()
    for c in range(0, width, HALF):
        col = win_ref[:, c : c + HALF]
        out = weights[RADIUS] * col[RADIUS : RADIUS + S]
        for d in range(1, RADIUS + 1):
            out = out + weights[RADIUS + d] * (
                col[RADIUS + d : RADIUS + d + S] + col[RADIUS - d : RADIUS - d + S])
        put(c, out)


def edges_kernel(*refs):
    (canvas3, next3, far3, canvas2, next2, far2, back2, main_ref, right_ref, east_ref, west_ref,
     win_ref) = refs

    def outer(c, out):
        east_ref[:S, HALF + c : 2 * HALF + c] = out

    def inner(c, out):
        if c < 3 * HALF:
            main_ref[:, c : c + HALF] = out
        else:
            east_ref[:S, :HALF] = out
            right_ref[...] = out
        if c == 0:
            west_ref[...] = out.T[:RADIUS]
        if c == 2 * HALF:
            east_ref[S:, :S] = out.T[HALF - RADIUS :]
            east_ref[S:, S:] = jnp.zeros((RADIUS, HALF), F32)

    own3 = [canvas3.at[:OWN, 3 * HALF :]]
    own2 = [canvas2.at[:OWN, :S], canvas2.at[:OWN, 7 * HALF :]]
    blurred_rows(own3, next3, far3, back2.at[:, 2 * S :], win_ref, S, outer)
    blurred_rows(own2, next2, far2, back2.at[:, : 2 * S], win_ref, 2 * S, inner)


def edges(*arrays):
    return pl.pallas_call(
        edges_kernel,
        in_specs=[VMEM] * 7,
        out_specs=[VMEM] * 4,
        out_shape=[
            jax.ShapeDtypeStruct((S, 3 * HALF), F32),
            jax.ShapeDtypeStruct((S, HALF), F32),
            jax.ShapeDtypeStruct((S + RADIUS, 3 * HALF), F32),
            jax.ShapeDtypeStruct((RADIUS, S), F32),
        ],
        scratch_shapes=[pltpu.VMEM((NEXT, 2 * S), F32)],
        compiler_params=PARAMS,
        name="edges",
    )(*arrays)


def band():
    full = np.zeros((2 * S, S), np.float64)
    for j in range(S):
        for d, w in zip(range(-RADIUS, RADIUS + 1), blur_weights()):
            full[j + HALF + d, j] = w
    high = full.astype(jnp.bfloat16)
    return high, (full - high.astype(np.float64)).astype(jnp.bfloat16)


def final_kernel(canvas1, next1, far1, back1, main_ref, right_ref, east_ref, west_ref, high_ref,
                 low_ref, out_ref, rows_ref, win_ref, done_ref, sems):
    span = out_ref.shape[1]
    none = jnp.zeros((HALF - RADIUS, S), F32)
    win_ref[:, :HALF] = jnp.concatenate([none, east_ref[S:, :S]], 0).T
    win_ref[:, HALF : HALF + S] = main_ref[:, :S] + east_ref[:S, :S]
    win_ref[:, HALF + 7 * HALF : HALF + span] = main_ref[:, S:]
    win_ref[:, HALF + span :] = right_ref[...] + jnp.concatenate([west_ref[...], none], 0).T

    def middle(c, out):
        if c == 0:
            out = out + east_ref[:S, S:]
        win_ref[:, HALF + S + c : 2 * HALF + S + c] = out

    blurred_rows([canvas1.at[:OWN]], next1, far1, back1, rows_ref, REACH, middle)
    copies = []
    for c in range(0, span, S):
        strip = win_ref[:, c : c + 2 * S]
        high = strip.astype(BF16)
        low = (strip - high.astype(F32)).astype(BF16)
        done_ref[:, c : c + S] = (
            dot(high, high_ref[...]) + dot(high, low_ref[...]) + dot(low, high_ref[...]))
        copies.append(pltpu.make_async_copy(
            done_ref.at[:, pl.ds(c, S)], out_ref.at[:, pl.ds(c, S)], sems.at[c // S]))
        copies[-1].start()
    for copy in copies:
        copy.wait()


def final(span, *arrays):
    high, low = band()
    return pl.pallas_call(
        final_kernel,
        in_specs=[VMEM] * 10,
        out_specs=ANY,
        out_shape=jax.ShapeDtypeStruct((S, span), F32),
        scratch_shapes=[
            pltpu.VMEM((NEXT, REACH), F32),
            pltpu.VMEM((S, span + 2 * HALF), F32),
            pltpu.VMEM((S, span), F32),
            pltpu.SemaphoreType.DMA((span // S,)),
        ],
        compiler_params=PARAMS,
        name="final",
    )(*arrays, jnp.asarray(high), jnp.asarray(low))


def moved(array, by_row, by_col):
    n_row, n_col = lax.axis_size("row"), lax.axis_size("col")
    if by_col == 0:
        return lax.ppermute(array, "row", [(i, (i + by_row) % n_row) for i in range(n_row)])
    if by_row == 0:
        return lax.ppermute(array, "col", [(i, (i + by_col) % n_col) for i in range(n_col)])
    pairs = [
        (r * n_col + c, (r + by_row) % n_row * n_col + (c + by_col) % n_col)
        for r in range(n_row)
        for c in range(n_col)
    ]
    return lax.ppermute(array, ("row", "col"), pairs)


def spilled(parts):
    own, after, far, back = parts
    return own, moved(after, 1, 0), moved(far, 2, 0), moved(back, -1, 0)


def behind(array, *others):
    return lax.optimization_barrier((array, *others))[0]


def on_device(source, boxes_a, shifts_a, widths_a, boxes_b, shifts_b, widths_b):
    shifts_a, widths_a, shifts_b, widths_b = (
        jnp.swapaxes(array, 1, 2) for array in (shifts_a, widths_a, shifts_b, widths_b))
    boxes_a = pltpu.with_memory_space_constraint(boxes_a, pltpu.HBM)
    boxes_b = pltpu.with_memory_space_constraint(boxes_b, pltpu.HBM)
    masses = pltpu.with_memory_space_constraint(source, pltpu.HBM)
    shifts_a = pltpu.with_memory_space_constraint(shifts_a, pltpu.HBM)
    widths_a = pltpu.with_memory_space_constraint(widths_a, pltpu.HBM)
    top03, bot03, left_top, left_bot, base, boxes12 = aligned(
        (0, 3), (1, 2), masses, boxes_a, boxes_a, shifts_a, widths_a)
    rtop03 = moved(top03, -1, 0)
    east = moved(left_bot, 0, -1)
    diag = moved(left_top, -1, -1)
    top12, bot12, boxes3 = aligned(
        (1, 2), (3,), source, boxes12, boxes_b, shifts_a, widths_a, base)
    rtop12 = moved(top12, -1, 0)
    own = [(bot03, 0), (bot03, 1), (bot12, 0), (bot12, 1), (bot12, 2), (bot12, 3), (bot03, 2),
           (bot03, 3), (east, 0)]
    below = [(rtop03, 0), (rtop03, 1), (rtop12, 0), (rtop12, 1), (rtop12, 2), (rtop12, 3),
             (rtop03, 2), (rtop03, 3), (diag, 0)]
    quads = {}
    for j in range(4):
        a, b = 2 * j + 1, 2 * j + 2
        quads[j] = [(array, (0, at)) for array, at in (own[a], own[b], below[a], below[b])]
        quads[j] += [
            (source, (1, a)),
            (source, (1, b)) if j < 3 else (east, (1, 0)),
        ]
        quads[j] += [(array, (1, at)) for array, at in (below[a], below[b])]
    canvas3, next3, far3, back3, boxes02 = shifted(
        (3,), (0, 2), boxes3, boxes_b, shifts_b, widths_b, base, quads,
        finals=((1152, 1408),))
    next3 = moved(next3, 1, 0)
    far3 = moved(far3, 2, 0)
    canvas2, next2, far2, back2, boxes1 = shifted(
        (0, 2), (1,), boxes02, boxes_b, shifts_b, widths_b, base, quads,
        carried=(768, 1152, 768), carry=(canvas3, back3), finals=((0, 256), (896, 1152)))
    next2 = moved(next2, 1, 0)
    far2 = moved(far2, 2, 0)
    rback2 = moved(back2, -1, 0)
    canvas1, next1, far1, back1 = shifted(
        (1,), (), boxes1, None, shifts_b, widths_b, base, quads,
        carried=(256, 896, 0), carry=(canvas2, behind(back3, next3, far3)),
        finals=((256, 896),))
    n_row = lax.axis_size("row")
    joined = lax.ppermute(
        behind(far1, far2, rback2), "row", [(i, i + 1) for i in range(0, n_row, 2)])
    far1 = lax.ppermute(far1, "row", [(i, (i + 2) % n_row) for i in range(1, n_row, 2)])
    back1 = moved(back1, -1, 0)
    next1 = moved(next1.at[:FAR].add(behind(joined, next2)), 1, 0)
    main, right, east, west = edges(canvas3, next3, far3, canvas2, next2, far2, rback2)
    return final(
        source.shape[1], canvas1, next1, far1, back1, main, right, moved(east, 0, 1),
        moved(west, 0, -1))


def solution(mesh):
    cells = P("row", "col", None)
    boxes = P("row", "col", None, None)
    return jax.shard_map(
        on_device,
        mesh=mesh,
        in_specs=(P("row", "col"), boxes, cells, cells, boxes, cells, cells),
        out_specs=P("row", "col"),
        check_vma=False,
    )
```

```python
import functools
import math

import jax
import jax.numpy as jnp
import numpy as np
from jax import lax
from jax.experimental import pallas as pl
from jax.experimental.pallas import tpu as pltpu
from jax.sharding import PartitionSpec as P

S = 256
HALF = 128
BOX = 512
ITERS = 3
RADIUS = 8
REACH = BOX + HALF
EPS = 0.05
SIGMA = 2.0
F32 = jnp.float32
BF16 = jnp.bfloat16
OWN = S + RADIUS
NEXT = S + 2 * RADIUS
FAR = REACH - 2 * S + RADIUS
BASE = 904
VMEM = pl.BlockSpec(memory_space=pltpu.VMEM)
SMEM = pl.BlockSpec(memory_space=pltpu.SMEM)
ANY = pl.BlockSpec(memory_space=pl.ANY)
HBM = pl.BlockSpec(memory_space=pltpu.HBM)
PARAMS = pltpu.CompilerParams(vmem_limit_bytes=24 << 20)


def dot(a, b):
    return jnp.dot(a, b, preferred_element_type=F32)


def fill_base(ref):
    for c in range(0, BASE, 8 * 28):
        n = min(8 * 28, BASE - c)
        rows = lax.broadcasted_iota(jnp.int32, (n, HALF), 0)
        cols = lax.broadcasted_iota(jnp.int32, (n, HALF), 1)
        dist = (rows - cols + (c - 384)).astype(F32) / S
        ref[c : c + n] = jnp.exp(-dist * dist / EPS)


def window(ref, start):
    base = pl.multiple_of(start // 8 * 8, 8)
    rest = start - base
    tiles = ref[pl.ds(base, REACH + 8), :].reshape(REACH // 8 + 1, 8, HALF)
    tiles = pltpu.roll(tiles, jnp.where(rest == 0, 0, 8 - rest), 1)
    row = lax.broadcasted_iota(jnp.int32, (REACH // 8, 8, HALF), 1)
    return jnp.where(row < 8 - rest, tiles[:-1], tiles[1:]).reshape(REACH, HALF).astype(BF16)


def fill_tables(o_r, o_c, w_r, w_c, base_ref, refs):
    back_r, back_c, fwd_r, fwd_c = refs
    tall_r = window(base_ref, o_r + S)
    tall_c = window(base_ref, o_c + S)
    wide_r = window(base_ref, -o_r)
    wide_c = window(base_ref, -o_c)
    none = jnp.zeros((), BF16)
    lane = lax.broadcasted_iota(jnp.int32, (S, HALF), 1)
    deep = lax.broadcasted_iota(jnp.int32, (BOX, HALF), 0)
    for k in range(BOX // HALF):
        at = slice(k * HALF, (k + 1) * HALF)
        rows = slice(384 - HALF * k, 640 - HALF * k)
        back_c[:, at] = wide_c[rows]
        fwd_r[:, at] = jnp.where(lane + k * HALF < w_r, wide_r[rows], none)
    for k in range(S // HALF):
        at = slice(k * HALF, (k + 1) * HALF)
        rows = slice(HALF - HALF * k, REACH - HALF * k)
        back_r[:, at] = tall_r[rows]
        fwd_c[:, at] = jnp.where(deep < w_c, tall_c[rows], none)


def table_scratch():
    return [
        pltpu.VMEM((BOX, S), BF16),
        pltpu.VMEM((S, BOX), BF16),
        pltpu.VMEM((S, BOX), BF16),
        pltpu.VMEM((BOX, S), BF16),
    ]


def forward(mass, tables, vb_ref):
    inner = dot(tables[2][...], vb_ref[...]).astype(BF16)
    return mass / dot(inner, tables[3][...])


def fetch(boxes, cells, ref, sems):
    copies = [
        pltpu.make_async_copy(boxes.at[0, j], ref.at[i], sems.at[i]) for i, j in enumerate(cells)
    ]
    for copy in copies:
        copy.start()
    return copies


def aligned_kernel(cells, later, shifts, widths, source, boxes, later_boxes, *refs):
    n = len(cells)
    if 0 in cells:
        tops, outs, refs = refs[:n], refs[n - 1 : n + 3], refs[n + 3 :]
        base_ref, later_ref, box_ref, refs = refs[0], refs[1], refs[2], refs[3:]
    else:
        base_ref, outs, later_ref, refs = refs[0], refs[1:3], refs[3], refs[4:]
        tops = [outs[0].at[:, pl.ds(i * S, S)] for i in range(n)]
        box_ref = boxes
    copies = [[] for _ in cells]
    if 0 in cells:
        mass_ref, vb_ref, tables, sems, later_sems = refs
        masses = [mass_ref.at[:, pl.ds(i * S, S)] for i in range(n)]
        for i, j in enumerate(cells):
            copies[i] += [
                pltpu.make_async_copy(source.at[:, pl.ds(j * S, S)], masses[i], sems.at[i, 1]),
                pltpu.make_async_copy(boxes.at[0, j], box_ref.at[i], sems.at[i, 0]),
            ]
    else:
        vb_ref, tables, later_sems = refs
        masses = [source.at[:, pl.ds(j * S, S)] for j in cells]
    for pair in copies:
        for copy in reversed(pair):
            copy.start()
    if 0 in cells:
        fill_base(base_ref)
    for i, j in enumerate(cells):
        fill_tables(
            shifts[0, 0, j], shifts[0, 1, j], widths[0, 0, j], widths[0, 1, j], base_ref, tables[i])
    scales = []
    for i in range(n):
        down = dot(tables[i][0][...], jnp.ones((S, HALF), BF16)).astype(BF16).astype(F32)
        across = dot(jnp.ones((8, S), BF16), tables[i][1][...])
        scales.append(((1.0 / down)[:, :1], (1.0 / across)[:1]))
    u = [None] * n
    for step in range(ITERS):
        for i in range(n):
            if step == 0:
                for copy in copies[i]:
                    copy.wait()
                if i == n - 1:
                    later_copies = fetch(later_boxes, later, later_ref, later_sems)
                down, across = scales[i]
                for c in range(0, BOX, HALF):
                    v = box_ref[i, c : c + HALF] * down[c : c + HALF] * across
                    vb_ref[i, c : c + HALF] = v.astype(BF16)
            else:
                inner = dot(tables[i][0][...], u[i].astype(BF16)).astype(BF16)
                vb_ref[i] = (box_ref[i] / dot(inner, tables[i][1][...])).astype(BF16)
        for i in range(n):
            u[i] = forward(masses[i][...], tables[i], vb_ref.at[i])
    for i, j in enumerate(cells):
        tops[i][:HALF] = u[i][:HALF]
        tops[i][HALF:] = masses[i][:HALF]
        outs[1][:, i * S : (i + 1) * S] = u[i][HALF:]
        if j == 0:
            for k in range(2):
                outs[2 + k][:HALF] = u[i][k * HALF : (k + 1) * HALF, :HALF]
                outs[2 + k][HALF:] = masses[i][k * HALF : (k + 1) * HALF, :HALF]
    for copy in later_copies:
        copy.wait()


def cost(cells, applies):
    return pl.CostEstimate(
        flops=cells * applies * 804_000_000, bytes_accessed=cells << 20, transcendentals=0)


def aligned(cells, later, source, boxes, later_boxes, shifts, widths, *base):
    n = len(cells)
    corner = jax.ShapeDtypeStruct((S, HALF), F32)
    apart = n if 0 in cells else 1
    shapes = [jax.ShapeDtypeStruct((S, n * S // apart), F32)] * apart
    shapes.append(jax.ShapeDtypeStruct((HALF, n * S), F32))
    scratch = []
    if 0 in cells:
        shapes += [corner, corner, jax.ShapeDtypeStruct((BASE, HALF), F32)]
        scratch += [pltpu.VMEM((n, BOX, BOX), F32), pltpu.VMEM((S, n * S), F32)]
    shapes.append(jax.ShapeDtypeStruct((len(later), BOX, BOX), F32))
    return pl.pallas_call(
        functools.partial(aligned_kernel, cells, later),
        in_specs=[SMEM, SMEM] + ([HBM, HBM] if 0 in cells else [VMEM, VMEM]) + [HBM] + [VMEM] * len(base),
        out_specs=[VMEM] * len(shapes),
        out_shape=shapes,
        scratch_shapes=scratch + [
            pltpu.VMEM((n, BOX, BOX), BF16),
            [table_scratch() for _ in cells],
        ] + [pltpu.SemaphoreType.DMA((n, 2))] * (0 in cells) + [
            pltpu.SemaphoreType.DMA((len(later),)),
        ],
        compiler_params=PARAMS,
        cost_estimate=cost(n, 5),
        name="aligned",
    )(shifts, widths, source, boxes, later_boxes, *base)


def place(plan_ref, top, left, canvas_ref, first):
    base = pl.multiple_of(top // 8 * 8, 8)
    rest = top - base
    row = lax.broadcasted_iota(jnp.int32, (HALF // 8 + 1, 8, BOX), 1)
    column = lax.broadcasted_iota(jnp.int32, (HALF + 8, HALF), 1)
    none = jnp.zeros((1, 8, BOX), F32)
    for c in range(0, BOX, HALF):
        turned = pltpu.roll(plan_ref[c : c + HALF].reshape(HALF // 8, 8, BOX), rest, 1)
        rows = jnp.where(
            row < rest,
            jnp.concatenate([none, turned], 0),
            jnp.concatenate([turned, none], 0),
        ).reshape(HALF + 8, BOX)
        before = jnp.zeros((HALF + 8, HALF), F32)
        for k in range(BOX // HALF + 1):
            now = jnp.zeros((HALF + 8, HALF), F32)
            if k < BOX // HALF:
                now = pltpu.roll(rows[:, k * HALF : (k + 1) * HALF], left, 1)
            at = (pl.ds(base + c, HALF + 8), slice(first + k * HALF, first + (k + 1) * HALF))
            canvas_ref[at] = canvas_ref[at] + jnp.where(column < left, before, now)
            before = now


def shifted_kernel(cells, later, origin, carried, finals, quads, count, shifts, widths, box_ref,
                   base_ref, *refs):
    n = len(cells)
    arrays, refs = refs[:count], refs[count:]
    if carried:
        carry_ref, upper_ref, refs = refs[0], refs[1], refs[2:]
    if later:
        later_boxes, refs = refs[0], refs[1:]
    canvas_ref, outs, refs = refs[0], refs[1:4], refs[4:]
    if later:
        later_ref, refs = refs[0], refs[1:]
    mass_ref, ub_ref, vb_ref, v_ref, tables, sems = refs
    later_copies = fetch(later_boxes, later, later_ref, sems) if later else []
    canvas_ref[...] = jnp.zeros_like(canvas_ref)
    if carried:
        first, last, start = carried
        canvas_ref[:, first - origin : last - origin] = carry_ref[
            :, first - start : last - start]
    for i, j in enumerate(cells):
        fill_tables(
            shifts[0, 0, j], shifts[0, 1, j], widths[0, 0, j], widths[0, 1, j], base_ref, tables[i])
        for k in range(4):
            rows = slice(k // 2 * HALF, (k // 2 + 1) * HALF)
            cols = slice(k % 2 * HALF, (k % 2 + 1) * HALF)
            for ref, (array, down, across) in (
                (ub_ref, quads[i][k]), (mass_ref, quads[i][4 + k])
            ):
                part = arrays[array][
                    down * HALF : (down + 1) * HALF, across * HALF : (across + 1) * HALF]
                ref[i, rows, cols] = part.astype(ref.dtype)
    u = [ub_ref[i] for i in range(n)]
    for step in range(ITERS):
        for i in range(n):
            inner = dot(tables[i][0][...], u[i]).astype(BF16)
            den = dot(inner, tables[i][1][...])
            v = box_ref[i] / den
            if step == ITERS - 1:
                v_ref[i] = v
            vb_ref[i] = v.astype(BF16)
        for i in range(n):
            u[i] = forward(mass_ref[i], tables[i], vb_ref.at[i]).astype(BF16)
    deep = lax.broadcasted_iota(jnp.int32, (BOX, S), 0)
    lane = lax.broadcasted_iota(jnp.int32, (S, BOX), 1)
    for i, j in enumerate(cells):
        inner = jnp.where(deep < widths[0, 0, j], dot(tables[i][0][...], u[i]), 0.0).astype(BF16)
        used = jnp.where(lane < widths[0, 1, j], tables[i][1][...], jnp.zeros((), BF16))
        v_ref[i] = v_ref[i] * dot(inner, used)
    for i, j in enumerate(cells):
        place(v_ref.at[i], shifts[0, 0, j] + HALF, shifts[0, 1, j] + HALF, canvas_ref,
              j * S - origin)
    at = 0
    for first, last in finals:
        for ref, row in zip(outs, (S - RADIUS, 2 * S - RADIUS, 0)):
            ref[:, at : at + last - first] = canvas_ref[
                row : row + ref.shape[0], first - origin : last - origin]
        at += last - first
    if carried and later:
        outs[2][:, at:] = upper_ref[...]
    for copy in later_copies:
        copy.wait()


def shifted(cells, later, boxes, later_boxes, shifts, widths, base, quads, carried=None,
            carry=(), finals=()):
    n = len(cells)
    origin = min(j * S for j in cells)
    width = max(j * S + REACH for j in cells) - origin
    total = sum(last - first for first, last in finals)
    upper = carry[1].shape[1] if carried and later else 0
    shapes = [
        jax.ShapeDtypeStruct((REACH + 8, width), F32),
        jax.ShapeDtypeStruct((NEXT, total), F32),
        jax.ShapeDtypeStruct((FAR, total), F32),
        jax.ShapeDtypeStruct((RADIUS, total + upper), F32),
    ]
    if later:
        shapes.append(jax.ShapeDtypeStruct((len(later), BOX, BOX), F32))
    arrays, where = [], []
    for j in cells:
        where.append([])
        for array, (down, across) in quads[j]:
            known = [k for k, other in enumerate(arrays) if other is array]
            if not known:
                known = [len(arrays)]
                arrays.append(array)
            where[-1].append((known[0], down, across))
    count = len(arrays)
    arrays += carry
    return pl.pallas_call(
        functools.partial(
            shifted_kernel, cells, later, origin, carried, finals, where, count),
        in_specs=[SMEM, SMEM, VMEM, VMEM] + [VMEM] * len(arrays) + [HBM] * bool(later),
        out_specs=[VMEM] * len(shapes),
        out_shape=shapes,
        scratch_shapes=[
            pltpu.VMEM((n, S, S), F32),
            pltpu.VMEM((n, S, S), BF16),
            pltpu.VMEM((n, BOX, BOX), BF16),
            pltpu.VMEM((n, BOX, BOX), F32),
            [table_scratch() for _ in cells],
            pltpu.SemaphoreType.DMA((max(1, len(later)),)),
        ],
        compiler_params=PARAMS,
        cost_estimate=cost(n, 7),
        name="shifted",
    )(shifts, widths, boxes, base, *arrays, *([later_boxes] if later else []))


def blur_weights():
    raw = [math.exp(-(d * d) / (2.0 * SIGMA * SIGMA)) for d in range(-RADIUS, RADIUS + 1)]
    total = sum(raw)
    return [w / total for w in raw]


def blurred_rows(own, next_ref, far_ref, back_ref, win_ref, width, put):
    win_ref[:, :width] = next_ref[...]
    at = 0
    for part in own:
        cols = slice(at, at + part.shape[1])
        win_ref[RADIUS:, cols] = win_ref[RADIUS:, cols] + part[...]
        at += part.shape[1]
    win_ref[:FAR, :width] = win_ref[:FAR, :width] + far_ref[...]
    win_ref[NEXT - RADIUS :, :width] = win_ref[NEXT - RADIUS :, :width] + back_ref[...]
    weights = blur_weights()
    for c in range(0, width, HALF):
        col = win_ref[:, c : c + HALF]
        out = weights[RADIUS] * col[RADIUS : RADIUS + S]
        for d in range(1, RADIUS + 1):
            out = out + weights[RADIUS + d] * (
                col[RADIUS + d : RADIUS + d + S] + col[RADIUS - d : RADIUS - d + S])
        put(c, out)


def edges_kernel(*refs):
    (canvas3, next3, far3, canvas2, next2, far2, back2, main_ref, right_ref, east_ref, west_ref,
     win_ref) = refs

    def outer(c, out):
        east_ref[:S, HALF + c : 2 * HALF + c] = out

    def inner(c, out):
        if c < 3 * HALF:
            main_ref[:, c : c + HALF] = out
        else:
            east_ref[:S, :HALF] = out
            right_ref[...] = out
        if c == 0:
            west_ref[...] = out.T[:RADIUS]
        if c == 2 * HALF:
            east_ref[S:, :S] = out.T[HALF - RADIUS :]
            east_ref[S:, S:] = jnp.zeros((RADIUS, HALF), F32)

    own3 = [canvas3.at[:OWN, 3 * HALF :]]
    own2 = [canvas2.at[:OWN, :S], canvas2.at[:OWN, 7 * HALF :]]
    blurred_rows(own3, next3, far3, back2.at[:, 2 * S :], win_ref, S, outer)
    blurred_rows(own2, next2, far2, back2.at[:, : 2 * S], win_ref, 2 * S, inner)


def edges(*arrays):
    return pl.pallas_call(
        edges_kernel,
        in_specs=[VMEM] * 7,
        out_specs=[VMEM] * 4,
        out_shape=[
            jax.ShapeDtypeStruct((S, 3 * HALF), F32),
            jax.ShapeDtypeStruct((S, HALF), F32),
            jax.ShapeDtypeStruct((S + RADIUS, 3 * HALF), F32),
            jax.ShapeDtypeStruct((RADIUS, S), F32),
        ],
        scratch_shapes=[pltpu.VMEM((NEXT, 2 * S), F32)],
        compiler_params=PARAMS,
        name="edges",
    )(*arrays)


def band():
    full = np.zeros((2 * S, S), np.float64)
    for j in range(S):
        for d, w in zip(range(-RADIUS, RADIUS + 1), blur_weights()):
            full[j + HALF + d, j] = w
    high = full.astype(jnp.bfloat16)
    return high, (full - high.astype(np.float64)).astype(jnp.bfloat16)


def final_kernel(canvas1, next1, far1, back1, main_ref, right_ref, east_ref, west_ref, high_ref,
                 low_ref, out_ref, rows_ref, win_ref, done_ref, sems):
    span = out_ref.shape[1]
    none = jnp.zeros((HALF - RADIUS, S), F32)
    win_ref[:, :HALF] = jnp.concatenate([none, east_ref[S:, :S]], 0).T
    win_ref[:, HALF : HALF + S] = main_ref[:, :S] + east_ref[:S, :S]
    win_ref[:, HALF + 7 * HALF : HALF + span] = main_ref[:, S:]
    win_ref[:, HALF + span :] = right_ref[...] + jnp.concatenate([west_ref[...], none], 0).T

    def middle(c, out):
        if c == 0:
            out = out + east_ref[:S, S:]
        win_ref[:, HALF + S + c : 2 * HALF + S + c] = out

    blurred_rows([canvas1.at[:OWN]], next1, far1, back1, rows_ref, REACH, middle)
    copies = []
    for c in range(0, span, S):
        strip = win_ref[:, c : c + 2 * S]
        high = strip.astype(BF16)
        low = (strip - high.astype(F32)).astype(BF16)
        done_ref[:, c : c + S] = (
            dot(high, high_ref[...]) + dot(high, low_ref[...]) + dot(low, high_ref[...]))
        copies.append(pltpu.make_async_copy(
            done_ref.at[:, pl.ds(c, S)], out_ref.at[:, pl.ds(c, S)], sems.at[c // S]))
        copies[-1].start()
    for copy in copies:
        copy.wait()


def final(span, *arrays):
    high, low = band()
    return pl.pallas_call(
        final_kernel,
        in_specs=[VMEM] * 10,
        out_specs=ANY,
        out_shape=jax.ShapeDtypeStruct((S, span), F32),
        scratch_shapes=[
            pltpu.VMEM((NEXT, REACH), F32),
            pltpu.VMEM((S, span + 2 * HALF), F32),
            pltpu.VMEM((S, span), F32),
            pltpu.SemaphoreType.DMA((span // S,)),
        ],
        compiler_params=PARAMS,
        name="final",
    )(*arrays, jnp.asarray(high), jnp.asarray(low))


def moved(array, by_row, by_col):
    n_row, n_col = lax.axis_size("row"), lax.axis_size("col")
    if by_col == 0:
        return lax.ppermute(array, "row", [(i, (i + by_row) % n_row) for i in range(n_row)])
    if by_row == 0:
        return lax.ppermute(array, "col", [(i, (i + by_col) % n_col) for i in range(n_col)])
    pairs = [
        (r * n_col + c, (r + by_row) % n_row * n_col + (c + by_col) % n_col)
        for r in range(n_row)
        for c in range(n_col)
    ]
    return lax.ppermute(array, ("row", "col"), pairs)


def spilled(parts):
    own, after, far, back = parts
    return own, moved(after, 1, 0), moved(far, 2, 0), moved(back, -1, 0)


def behind(array, *others):
    return lax.optimization_barrier((array, *others))[0]


def on_device(source, boxes_a, shifts_a, widths_a, boxes_b, shifts_b, widths_b):
    shifts_a, widths_a, shifts_b, widths_b = (
        jnp.swapaxes(array, 1, 2) for array in (shifts_a, widths_a, shifts_b, widths_b))
    boxes_a = pltpu.with_memory_space_constraint(boxes_a, pltpu.HBM)
    boxes_b = pltpu.with_memory_space_constraint(boxes_b, pltpu.HBM)
    masses = pltpu.with_memory_space_constraint(source, pltpu.HBM)
    shifts_a = pltpu.with_memory_space_constraint(shifts_a, pltpu.HBM)
    widths_a = pltpu.with_memory_space_constraint(widths_a, pltpu.HBM)
    top0, top3, bot03, left_top, left_bot, base, boxes12 = aligned(
        (0, 3), (1, 2), masses, boxes_a, boxes_a, shifts_a, widths_a)
    rtop3 = moved(top3, -1, 0)
    rtop0 = moved(top0, -1, 0)
    east = moved(left_bot, 0, -1)
    diag = moved(left_top, -1, -1)
    top12, bot12, boxes3 = aligned(
        (1, 2), (3,), source, boxes12, boxes_b, shifts_a, widths_a, base)
    rtop12 = moved(top12, -1, 0)
    own = [(bot03, 0), (bot03, 1), (bot12, 0), (bot12, 1), (bot12, 2), (bot12, 3), (bot03, 2),
           (bot03, 3), (east, 0)]
    below = [(rtop0, 0), (rtop0, 1), (rtop12, 0), (rtop12, 1), (rtop12, 2), (rtop12, 3),
             (rtop3, 0), (rtop3, 1), (diag, 0)]
    quads = {}
    for j in range(4):
        a, b = 2 * j + 1, 2 * j + 2
        quads[j] = [(array, (0, at)) for array, at in (own[a], own[b], below[a], below[b])]
        quads[j] += [
            (source, (1, a)),
            (source, (1, b)) if j < 3 else (east, (1, 0)),
        ]
        quads[j] += [(array, (1, at)) for array, at in (below[a], below[b])]
    canvas3, next3, far3, back3, boxes02 = shifted(
        (3,), (0, 2), boxes3, boxes_b, shifts_b, widths_b, base, quads,
        finals=((1152, 1408),))
    next3 = moved(next3, 1, 0)
    far3 = moved(far3, 2, 0)
    canvas2, next2, far2, back2, boxes1 = shifted(
        (0, 2), (1,), boxes02, boxes_b, shifts_b, widths_b, base, quads,
        carried=(768, 1152, 768), carry=(canvas3, back3), finals=((0, 256), (896, 1152)))
    next2 = moved(next2, 1, 0)
    far2 = moved(far2, 2, 0)
    rback2 = moved(back2, -1, 0)
    canvas1, next1, far1, back1 = shifted(
        (1,), (), boxes1, None, shifts_b, widths_b, base, quads,
        carried=(256, 896, 0), carry=(canvas2, behind(back3, next3, far3)),
        finals=((256, 896),))
    n_row = lax.axis_size("row")
    joined = lax.ppermute(
        behind(far1, far2), "row", [(i, i + 1) for i in range(0, n_row, 2)])
    far1 = lax.ppermute(far1, "row", [(i, (i + 2) % n_row) for i in range(1, n_row, 2)])
    back1 = moved(back1, -1, 0)
    next1 = moved(next1.at[:FAR].add(behind(joined, next2, rback2)), 1, 0)
    main, right, east, west = edges(canvas3, next3, far3, canvas2, next2, far2, rback2)
    return final(
        source.shape[1], canvas1, next1, far1, back1, main, right, moved(east, 0, 1),
        moved(west, 0, -1))


def solution(mesh):
    cells = P("row", "col", None)
    boxes = P("row", "col", None, None)
    return jax.shard_map(
        on_device,
        mesh=mesh,
        in_specs=(P("row", "col"), boxes, cells, cells, boxes, cells, cells),
        out_specs=P("row", "col"),
        check_vma=False,
    )
```

```python
import functools
import math

import jax
import jax.numpy as jnp
import numpy as np
from jax import lax
from jax.experimental import pallas as pl
from jax.experimental.pallas import tpu as pltpu
from jax.sharding import PartitionSpec as P

S = 256
HALF = 128
BOX = 512
ITERS = 3
RADIUS = 8
REACH = BOX + HALF
EPS = 0.05
SIGMA = 2.0
F32 = jnp.float32
BF16 = jnp.bfloat16
OWN = S + RADIUS
NEXT = S + 2 * RADIUS
NC_CELLS = 4
FAR = REACH - 2 * S + RADIUS
BASE = 904
VMEM = pl.BlockSpec(memory_space=pltpu.VMEM)
SMEM = pl.BlockSpec(memory_space=pltpu.SMEM)
ANY = pl.BlockSpec(memory_space=pl.ANY)
HBM = pl.BlockSpec(memory_space=pltpu.HBM)
PARAMS = pltpu.CompilerParams(vmem_limit_bytes=24 << 20)


def dot(a, b):
    return jnp.dot(a, b, preferred_element_type=F32)


def fill_base(ref):
    for c in range(0, BASE, 8 * 28):
        n = min(8 * 28, BASE - c)
        rows = lax.broadcasted_iota(jnp.int32, (n, HALF), 0)
        cols = lax.broadcasted_iota(jnp.int32, (n, HALF), 1)
        dist = (rows - cols + (c - 384)).astype(F32) / S
        ref[c : c + n] = jnp.exp(-dist * dist / EPS)


def window(ref, start):
    base = pl.multiple_of(start // 8 * 8, 8)
    rest = start - base
    tiles = ref[pl.ds(base, REACH + 8), :].reshape(REACH // 8 + 1, 8, HALF)
    tiles = pltpu.roll(tiles, jnp.where(rest == 0, 0, 8 - rest), 1)
    row = lax.broadcasted_iota(jnp.int32, (REACH // 8, 8, HALF), 1)
    return jnp.where(row < 8 - rest, tiles[:-1], tiles[1:]).reshape(REACH, HALF).astype(BF16)


def fill_tables(o_r, o_c, w_r, w_c, base_ref, refs):
    back_r, back_c, fwd_r, fwd_c = refs
    tall_r = window(base_ref, o_r + S)
    tall_c = window(base_ref, o_c + S)
    wide_r = window(base_ref, -o_r)
    wide_c = window(base_ref, -o_c)
    none = jnp.zeros((), BF16)
    lane = lax.broadcasted_iota(jnp.int32, (S, HALF), 1)
    deep = lax.broadcasted_iota(jnp.int32, (BOX, HALF), 0)
    for k in range(BOX // HALF):
        at = slice(k * HALF, (k + 1) * HALF)
        rows = slice(384 - HALF * k, 640 - HALF * k)
        back_c[:, at] = wide_c[rows]
        fwd_r[:, at] = jnp.where(lane + k * HALF < w_r, wide_r[rows], none)
    for k in range(S // HALF):
        at = slice(k * HALF, (k + 1) * HALF)
        rows = slice(HALF - HALF * k, REACH - HALF * k)
        back_r[:, at] = tall_r[rows]
        fwd_c[:, at] = jnp.where(deep < w_c, tall_c[rows], none)


def table_scratch():
    return [
        pltpu.VMEM((BOX, S), BF16),
        pltpu.VMEM((S, BOX), BF16),
        pltpu.VMEM((S, BOX), BF16),
        pltpu.VMEM((BOX, S), BF16),
    ]


def forward(mass, tables, vb_ref):
    inner = dot(tables[2][...], vb_ref[...]).astype(BF16)
    return mass / dot(inner, tables[3][...])


def fetch(boxes, cells, ref, sems):
    copies = [
        pltpu.make_async_copy(boxes.at[0, j], ref.at[i], sems.at[i]) for i, j in enumerate(cells)
    ]
    for copy in copies:
        copy.start()
    return copies


def aligned_kernel(cells, later, shifts, widths, source, boxes, later_boxes, *refs):
    n = len(cells)
    if 0 in cells:
        tops, outs, refs = refs[:n], refs[n - 1 : n + 3], refs[n + 3 :]
        base_ref, later_ref, box_ref, refs = refs[0], refs[1], refs[2], refs[3:]
    else:
        base_ref, first_ref, outs, later_ref, refs = refs[0], refs[1], refs[2:4], refs[4], refs[5:]
        tops = [outs[0].at[:, pl.ds(S + i * S, S)] for i in range(n)]
        outs[0][:, :S] = first_ref[...]
        box_ref = boxes
    copies = [[] for _ in cells]
    if 0 in cells:
        mass_ref, vb_ref, tables, sems, later_sems = refs
        masses = [mass_ref.at[:, pl.ds(i * S, S)] for i in range(n)]
        for i, j in enumerate(cells):
            copies[i] += [
                pltpu.make_async_copy(source.at[:, pl.ds(j * S, S)], masses[i], sems.at[i, 1]),
                pltpu.make_async_copy(boxes.at[0, j], box_ref.at[i], sems.at[i, 0]),
            ]
    else:
        vb_ref, tables, later_sems = refs
        masses = [source.at[:, pl.ds(j * S, S)] for j in cells]
    for pair in copies:
        for copy in reversed(pair):
            copy.start()
    if 0 in cells:
        fill_base(base_ref)
    for i, j in enumerate(cells):
        fill_tables(
            shifts[0, 0, j], shifts[0, 1, j], widths[0, 0, j], widths[0, 1, j], base_ref, tables[i])
    scales = []
    for i in range(n):
        down = dot(tables[i][0][...], jnp.ones((S, HALF), BF16)).astype(BF16).astype(F32)
        across = dot(jnp.ones((8, S), BF16), tables[i][1][...])
        scales.append(((1.0 / down)[:, :1], (1.0 / across)[:1]))
    u = [None] * n
    for step in range(ITERS):
        for i in range(n):
            if step == 0:
                for copy in copies[i]:
                    copy.wait()
                if i == n - 1:
                    later_copies = fetch(later_boxes, later, later_ref, later_sems)
                down, across = scales[i]
                for c in range(0, BOX, HALF):
                    v = box_ref[i, c : c + HALF] * down[c : c + HALF] * across
                    vb_ref[i, c : c + HALF] = v.astype(BF16)
            else:
                inner = dot(tables[i][0][...], u[i].astype(BF16)).astype(BF16)
                vb_ref[i] = (box_ref[i] / dot(inner, tables[i][1][...])).astype(BF16)
        for i in range(n):
            u[i] = forward(masses[i][...], tables[i], vb_ref.at[i])
    for i, j in enumerate(cells):
        tops[i][:HALF, :S] = u[i][:HALF]
        if j == NC_CELLS - 1:
            tops[i][HALF:] = masses[i][:HALF]
        outs[1][:, i * S : (i + 1) * S] = u[i][HALF:]
        if j == 0:
            for k in range(2):
                outs[2 + k][:HALF] = u[i][k * HALF : (k + 1) * HALF, :HALF]
                outs[2 + k][HALF:] = masses[i][k * HALF : (k + 1) * HALF, :HALF]
    for copy in later_copies:
        copy.wait()


def cost(cells, applies):
    return pl.CostEstimate(
        flops=cells * applies * 804_000_000, bytes_accessed=cells << 20, transcendentals=0)


def aligned(cells, later, source, boxes, later_boxes, shifts, widths, *base):
    n = len(cells)
    corner = jax.ShapeDtypeStruct((S, HALF), F32)
    if 0 in cells:
        shapes = [jax.ShapeDtypeStruct((HALF, S), F32), jax.ShapeDtypeStruct((S, S), F32)]
    else:
        shapes = [jax.ShapeDtypeStruct((HALF, (n + 1) * S), F32)]
    shapes.append(jax.ShapeDtypeStruct((HALF, n * S), F32))
    scratch = []
    if 0 in cells:
        shapes += [corner, corner, jax.ShapeDtypeStruct((BASE, HALF), F32)]
        scratch += [pltpu.VMEM((n, BOX, BOX), F32), pltpu.VMEM((S, n * S), F32)]
    shapes.append(jax.ShapeDtypeStruct((len(later), BOX, BOX), F32))
    return pl.pallas_call(
        functools.partial(aligned_kernel, cells, later),
        in_specs=[SMEM, SMEM] + ([HBM, HBM] if 0 in cells else [VMEM, VMEM]) + [HBM] + [VMEM] * len(base),
        out_specs=[VMEM] * len(shapes),
        out_shape=shapes,
        scratch_shapes=scratch + [
            pltpu.VMEM((n, BOX, BOX), BF16),
            [table_scratch() for _ in cells],
        ] + [pltpu.SemaphoreType.DMA((n, 2))] * (0 in cells) + [
            pltpu.SemaphoreType.DMA((len(later),)),
        ],
        compiler_params=PARAMS,
        cost_estimate=cost(n, 5),
        name="aligned",
    )(shifts, widths, source, boxes, later_boxes, *base)


def place(plan_ref, top, left, canvas_ref, first):
    base = pl.multiple_of(top // 8 * 8, 8)
    rest = top - base
    row = lax.broadcasted_iota(jnp.int32, (HALF // 8 + 1, 8, BOX), 1)
    column = lax.broadcasted_iota(jnp.int32, (HALF + 8, HALF), 1)
    none = jnp.zeros((1, 8, BOX), F32)
    for c in range(0, BOX, HALF):
        turned = pltpu.roll(plan_ref[c : c + HALF].reshape(HALF // 8, 8, BOX), rest, 1)
        rows = jnp.where(
            row < rest,
            jnp.concatenate([none, turned], 0),
            jnp.concatenate([turned, none], 0),
        ).reshape(HALF + 8, BOX)
        before = jnp.zeros((HALF + 8, HALF), F32)
        for k in range(BOX // HALF + 1):
            now = jnp.zeros((HALF + 8, HALF), F32)
            if k < BOX // HALF:
                now = pltpu.roll(rows[:, k * HALF : (k + 1) * HALF], left, 1)
            at = (pl.ds(base + c, HALF + 8), slice(first + k * HALF, first + (k + 1) * HALF))
            canvas_ref[at] = canvas_ref[at] + jnp.where(column < left, before, now)
            before = now


def shifted_kernel(cells, later, origin, carried, finals, quads, count, shifts, widths, box_ref,
                   base_ref, *refs):
    n = len(cells)
    arrays, refs = refs[:count], refs[count:]
    if carried:
        carry_ref, upper_ref, refs = refs[0], refs[1], refs[2:]
    if later:
        later_boxes, refs = refs[0], refs[1:]
    canvas_ref, outs, refs = refs[0], refs[1:4], refs[4:]
    if later:
        later_ref, refs = refs[0], refs[1:]
    mass_ref, ub_ref, vb_ref, v_ref, tables, sems = refs
    later_copies = fetch(later_boxes, later, later_ref, sems) if later else []
    canvas_ref[...] = jnp.zeros_like(canvas_ref)
    if carried:
        first, last, start = carried
        canvas_ref[:, first - origin : last - origin] = carry_ref[
            :, first - start : last - start]
    for i, j in enumerate(cells):
        fill_tables(
            shifts[0, 0, j], shifts[0, 1, j], widths[0, 0, j], widths[0, 1, j], base_ref, tables[i])
        for k in range(4):
            rows = slice(k // 2 * HALF, (k // 2 + 1) * HALF)
            cols = slice(k % 2 * HALF, (k % 2 + 1) * HALF)
            for ref, (array, down, across) in (
                (ub_ref, quads[i][k]), (mass_ref, quads[i][4 + k])
            ):
                part = arrays[array][
                    down * HALF : (down + 1) * HALF, across * HALF : (across + 1) * HALF]
                ref[i, rows, cols] = part.astype(ref.dtype)
    u = [ub_ref[i] for i in range(n)]
    for step in range(ITERS):
        for i in range(n):
            inner = dot(tables[i][0][...], u[i]).astype(BF16)
            den = dot(inner, tables[i][1][...])
            v = box_ref[i] / den
            if step == ITERS - 1:
                v_ref[i] = v
            vb_ref[i] = v.astype(BF16)
        for i in range(n):
            u[i] = forward(mass_ref[i], tables[i], vb_ref.at[i]).astype(BF16)
    deep = lax.broadcasted_iota(jnp.int32, (BOX, S), 0)
    lane = lax.broadcasted_iota(jnp.int32, (S, BOX), 1)
    for i, j in enumerate(cells):
        inner = jnp.where(deep < widths[0, 0, j], dot(tables[i][0][...], u[i]), 0.0).astype(BF16)
        used = jnp.where(lane < widths[0, 1, j], tables[i][1][...], jnp.zeros((), BF16))
        v_ref[i] = v_ref[i] * dot(inner, used)
    for i, j in enumerate(cells):
        place(v_ref.at[i], shifts[0, 0, j] + HALF, shifts[0, 1, j] + HALF, canvas_ref,
              j * S - origin)
    at = 0
    for first, last in finals:
        for ref, row in zip(outs, (S - RADIUS, 2 * S - RADIUS, 0)):
            ref[:, at : at + last - first] = canvas_ref[
                row : row + ref.shape[0], first - origin : last - origin]
        at += last - first
    if carried and later:
        outs[2][:, at:] = upper_ref[...]
    for copy in later_copies:
        copy.wait()


def shifted(cells, later, boxes, later_boxes, shifts, widths, base, quads, carried=None,
            carry=(), finals=()):
    n = len(cells)
    origin = min(j * S for j in cells)
    width = max(j * S + REACH for j in cells) - origin
    total = sum(last - first for first, last in finals)
    upper = carry[1].shape[1] if carried and later else 0
    shapes = [
        jax.ShapeDtypeStruct((REACH + 8, width), F32),
        jax.ShapeDtypeStruct((NEXT, total), F32),
        jax.ShapeDtypeStruct((FAR, total), F32),
        jax.ShapeDtypeStruct((RADIUS, total + upper), F32),
    ]
    if later:
        shapes.append(jax.ShapeDtypeStruct((len(later), BOX, BOX), F32))
    arrays, where = [], []
    for j in cells:
        where.append([])
        for array, (down, across) in quads[j]:
            known = [k for k, other in enumerate(arrays) if other is array]
            if not known:
                known = [len(arrays)]
                arrays.append(array)
            where[-1].append((known[0], down, across))
    count = len(arrays)
    arrays += carry
    return pl.pallas_call(
        functools.partial(
            shifted_kernel, cells, later, origin, carried, finals, where, count),
        in_specs=[SMEM, SMEM, VMEM, VMEM] + [VMEM] * len(arrays) + [HBM] * bool(later),
        out_specs=[VMEM] * len(shapes),
        out_shape=shapes,
        scratch_shapes=[
            pltpu.VMEM((n, S, S), F32),
            pltpu.VMEM((n, S, S), BF16),
            pltpu.VMEM((n, BOX, BOX), BF16),
            pltpu.VMEM((n, BOX, BOX), F32),
            [table_scratch() for _ in cells],
            pltpu.SemaphoreType.DMA((max(1, len(later)),)),
        ],
        compiler_params=PARAMS,
        cost_estimate=cost(n, 7),
        name="shifted",
    )(shifts, widths, boxes, base, *arrays, *([later_boxes] if later else []))


def blur_weights():
    raw = [math.exp(-(d * d) / (2.0 * SIGMA * SIGMA)) for d in range(-RADIUS, RADIUS + 1)]
    total = sum(raw)
    return [w / total for w in raw]


def blurred_rows(own, next_ref, far_ref, back_ref, win_ref, width, put):
    win_ref[:, :width] = next_ref[...]
    at = 0
    for part in own:
        cols = slice(at, at + part.shape[1])
        win_ref[RADIUS:, cols] = win_ref[RADIUS:, cols] + part[...]
        at += part.shape[1]
    win_ref[:FAR, :width] = win_ref[:FAR, :width] + far_ref[...]
    win_ref[NEXT - RADIUS :, :width] = win_ref[NEXT - RADIUS :, :width] + back_ref[...]
    weights = blur_weights()
    for c in range(0, width, HALF):
        col = win_ref[:, c : c + HALF]
        out = weights[RADIUS] * col[RADIUS : RADIUS + S]
        for d in range(1, RADIUS + 1):
            out = out + weights[RADIUS + d] * (
                col[RADIUS + d : RADIUS + d + S] + col[RADIUS - d : RADIUS - d + S])
        put(c, out)


def edges_kernel(*refs):
    (canvas3, next3, far3, canvas2, next2, far2, back2, main_ref, right_ref, east_ref, west_ref,
     win_ref) = refs

    def outer(c, out):
        east_ref[:S, HALF + c : 2 * HALF + c] = out

    def inner(c, out):
        if c < 3 * HALF:
            main_ref[:, c : c + HALF] = out
        else:
            east_ref[:S, :HALF] = out
            right_ref[...] = out
        if c == 0:
            west_ref[...] = out.T[:RADIUS]
        if c == 2 * HALF:
            east_ref[S:, :S] = out.T[HALF - RADIUS :]
            east_ref[S:, S:] = jnp.zeros((RADIUS, HALF), F32)

    own3 = [canvas3.at[:OWN, 3 * HALF :]]
    own2 = [canvas2.at[:OWN, :S], canvas2.at[:OWN, 7 * HALF :]]
    blurred_rows(own3, next3, far3, back2.at[:, 2 * S :], win_ref, S, outer)
    blurred_rows(own2, next2, far2, back2.at[:, : 2 * S], win_ref, 2 * S, inner)


def edges(*arrays):
    return pl.pallas_call(
        edges_kernel,
        in_specs=[VMEM] * 7,
        out_specs=[VMEM] * 4,
        out_shape=[
            jax.ShapeDtypeStruct((S, 3 * HALF), F32),
            jax.ShapeDtypeStruct((S, HALF), F32),
            jax.ShapeDtypeStruct((S + RADIUS, 3 * HALF), F32),
            jax.ShapeDtypeStruct((RADIUS, S), F32),
        ],
        scratch_shapes=[pltpu.VMEM((NEXT, 2 * S), F32)],
        compiler_params=PARAMS,
        name="edges",
    )(*arrays)


def band():
    full = np.zeros((2 * S, S), np.float64)
    for j in range(S):
        for d, w in zip(range(-RADIUS, RADIUS + 1), blur_weights()):
            full[j + HALF + d, j] = w
    high = full.astype(jnp.bfloat16)
    return high, (full - high.astype(np.float64)).astype(jnp.bfloat16)


def final_kernel(canvas1, next1, far1, back1, main_ref, right_ref, east_ref, west_ref, high_ref,
                 low_ref, out_ref, rows_ref, win_ref, done_ref, sems):
    span = out_ref.shape[1]
    none = jnp.zeros((HALF - RADIUS, S), F32)
    win_ref[:, :HALF] = jnp.concatenate([none, east_ref[S:, :S]], 0).T
    win_ref[:, HALF : HALF + S] = main_ref[:, :S] + east_ref[:S, :S]
    win_ref[:, HALF + 7 * HALF : HALF + span] = main_ref[:, S:]
    win_ref[:, HALF + span :] = right_ref[...] + jnp.concatenate([west_ref[...], none], 0).T

    def middle(c, out):
        if c == 0:
            out = out + east_ref[:S, S:]
        win_ref[:, HALF + S + c : 2 * HALF + S + c] = out

    blurred_rows([canvas1.at[:OWN]], next1, far1, back1, rows_ref, REACH, middle)
    copies = []
    for c in range(0, span, S):
        strip = win_ref[:, c : c + 2 * S]
        high = strip.astype(BF16)
        low = (strip - high.astype(F32)).astype(BF16)
        done_ref[:, c : c + S] = (
            dot(high, high_ref[...]) + dot(high, low_ref[...]) + dot(low, high_ref[...]))
        copies.append(pltpu.make_async_copy(
            done_ref.at[:, pl.ds(c, S)], out_ref.at[:, pl.ds(c, S)], sems.at[c // S]))
        copies[-1].start()
    for copy in copies:
        copy.wait()


def final(span, *arrays):
    high, low = band()
    return pl.pallas_call(
        final_kernel,
        in_specs=[VMEM] * 10,
        out_specs=ANY,
        out_shape=jax.ShapeDtypeStruct((S, span), F32),
        scratch_shapes=[
            pltpu.VMEM((NEXT, REACH), F32),
            pltpu.VMEM((S, span + 2 * HALF), F32),
            pltpu.VMEM((S, span), F32),
            pltpu.SemaphoreType.DMA((span // S,)),
        ],
        compiler_params=PARAMS,
        name="final",
    )(*arrays, jnp.asarray(high), jnp.asarray(low))


def moved(array, by_row, by_col):
    n_row, n_col = lax.axis_size("row"), lax.axis_size("col")
    if by_col == 0:
        return lax.ppermute(array, "row", [(i, (i + by_row) % n_row) for i in range(n_row)])
    if by_row == 0:
        return lax.ppermute(array, "col", [(i, (i + by_col) % n_col) for i in range(n_col)])
    pairs = [
        (r * n_col + c, (r + by_row) % n_row * n_col + (c + by_col) % n_col)
        for r in range(n_row)
        for c in range(n_col)
    ]
    return lax.ppermute(array, ("row", "col"), pairs)


def spilled(parts):
    own, after, far, back = parts
    return own, moved(after, 1, 0), moved(far, 2, 0), moved(back, -1, 0)


def behind(array, *others):
    return lax.optimization_barrier((array, *others))[0]


def on_device(source, boxes_a, shifts_a, widths_a, boxes_b, shifts_b, widths_b):
    shifts_a, widths_a, shifts_b, widths_b = (
        jnp.swapaxes(array, 1, 2) for array in (shifts_a, widths_a, shifts_b, widths_b))
    boxes_a = pltpu.with_memory_space_constraint(boxes_a, pltpu.HBM)
    boxes_b = pltpu.with_memory_space_constraint(boxes_b, pltpu.HBM)
    masses = pltpu.with_memory_space_constraint(source, pltpu.HBM)
    shifts_a = pltpu.with_memory_space_constraint(shifts_a, pltpu.HBM)
    widths_a = pltpu.with_memory_space_constraint(widths_a, pltpu.HBM)
    rmass = moved(source[:HALF, : (NC_CELLS - 1) * S], -1, 0)
    top0, top3, bot03, left_top, left_bot, base, boxes12 = aligned(
        (0, 3), (1, 2), masses, boxes_a, boxes_a, shifts_a, widths_a)
    rtop3 = moved(top3, -1, 0)
    east = moved(left_bot, 0, -1)
    diag = moved(left_top, -1, -1)
    top012, bot12, boxes3 = aligned(
        (1, 2), (3,), source, boxes12, boxes_b, shifts_a, widths_a, behind(base, rmass), top0)
    rtop012 = moved(top012, -1, 0)
    own = [(bot03, 0), (bot03, 1), (bot12, 0), (bot12, 1), (bot12, 2), (bot12, 3), (bot03, 2),
           (bot03, 3), (east, 0)]
    below = [(rtop012, k) for k in range(6)] + [(rtop3, 0), (rtop3, 1), (diag, 0)]
    mass = [(rmass, (0, k)) for k in range(6)] + [
        (rtop3, (1, 0)), (rtop3, (1, 1)), (diag, (1, 0))]
    quads = {}
    for j in range(NC_CELLS):
        a, b = 2 * j + 1, 2 * j + 2
        quads[j] = [(array, (0, at)) for array, at in (own[a], own[b], below[a], below[b])]
        quads[j] += [
            (source, (1, a)),
            (source, (1, b)) if j < NC_CELLS - 1 else (east, (1, 0)),
            mass[a],
            mass[b],
        ]
    canvas3, next3, far3, back3, boxes02 = shifted(
        (3,), (0, 2), boxes3, boxes_b, shifts_b, widths_b, base, quads,
        finals=((1152, 1408),))
    next3 = moved(next3, 1, 0)
    far3 = moved(far3, 2, 0)
    canvas2, next2, far2, back2, boxes1 = shifted(
        (0, 2), (1,), boxes02, boxes_b, shifts_b, widths_b, base, quads,
        carried=(768, 1152, 768), carry=(canvas3, back3), finals=((0, 256), (896, 1152)))
    next2 = moved(next2, 1, 0)
    far2 = moved(far2, 2, 0)
    rback2 = moved(back2, -1, 0)
    canvas1, next1, far1, back1 = shifted(
        (1,), (), boxes1, None, shifts_b, widths_b, base, quads,
        carried=(256, 896, 0), carry=(behind(canvas2, next3, far3), back3),
        finals=((256, 896),))
    n_row = lax.axis_size("row")
    joined = lax.ppermute(
        behind(far1, far2), "row", [(i, i + 1) for i in range(0, n_row, 2)])
    far1 = lax.ppermute(far1, "row", [(i, (i + 2) % n_row) for i in range(1, n_row, 2)])
    back1 = moved(back1, -1, 0)
    next1 = moved(next1.at[:FAR].add(behind(joined, next2, rback2)), 1, 0)
    main, right, east, west = edges(canvas3, next3, far3, canvas2, next2, far2, rback2)
    return final(
        source.shape[1], canvas1, next1, far1, back1, main, right, moved(east, 0, 1),
        moved(west, 0, -1))


def solution(mesh):
    cells = P("row", "col", None)
    boxes = P("row", "col", None, None)
    return jax.shard_map(
        on_device,
        mesh=mesh,
        in_specs=(P("row", "col"), boxes, cells, cells, boxes, cells, cells),
        out_specs=P("row", "col"),
        check_vma=False,
    )
```

```python
import functools
import math

import jax
import jax.numpy as jnp
import numpy as np
from jax import lax
from jax.experimental import pallas as pl
from jax.experimental.pallas import tpu as pltpu
from jax.sharding import PartitionSpec as P

S = 256
HALF = 128
BOX = 512
ITERS = 3
RADIUS = 8
REACH = BOX + HALF
EPS = 0.05
SIGMA = 2.0
F32 = jnp.float32
BF16 = jnp.bfloat16
OWN = S + RADIUS
NEXT = S + 2 * RADIUS
NC_CELLS = 4
FAR = REACH - 2 * S + RADIUS
BASE = 904
VMEM = pl.BlockSpec(memory_space=pltpu.VMEM)
SMEM = pl.BlockSpec(memory_space=pltpu.SMEM)
ANY = pl.BlockSpec(memory_space=pl.ANY)
HBM = pl.BlockSpec(memory_space=pltpu.HBM)
PARAMS = pltpu.CompilerParams(vmem_limit_bytes=24 << 20)


def dot(a, b):
    return jnp.dot(a, b, preferred_element_type=F32)


def fill_base(ref):
    for c in range(0, BASE, 8 * 28):
        n = min(8 * 28, BASE - c)
        rows = lax.broadcasted_iota(jnp.int32, (n, HALF), 0)
        cols = lax.broadcasted_iota(jnp.int32, (n, HALF), 1)
        dist = (rows - cols + (c - 384)).astype(F32) / S
        ref[c : c + n] = jnp.exp(-dist * dist / EPS)


def window(ref, start):
    base = pl.multiple_of(start // 8 * 8, 8)
    rest = start - base
    tiles = ref[pl.ds(base, REACH + 8), :].reshape(REACH // 8 + 1, 8, HALF)
    tiles = pltpu.roll(tiles, jnp.where(rest == 0, 0, 8 - rest), 1)
    row = lax.broadcasted_iota(jnp.int32, (REACH // 8, 8, HALF), 1)
    return jnp.where(row < 8 - rest, tiles[:-1], tiles[1:]).reshape(REACH, HALF).astype(BF16)


def fill_tables(o_r, o_c, w_r, w_c, base_ref, refs):
    back_r, back_c, fwd_r, fwd_c = refs
    tall_r = window(base_ref, o_r + S)
    tall_c = window(base_ref, o_c + S)
    wide_r = window(base_ref, -o_r)
    wide_c = window(base_ref, -o_c)
    none = jnp.zeros((), BF16)
    lane = lax.broadcasted_iota(jnp.int32, (S, HALF), 1)
    deep = lax.broadcasted_iota(jnp.int32, (BOX, HALF), 0)
    for k in range(BOX // HALF):
        at = slice(k * HALF, (k + 1) * HALF)
        rows = slice(384 - HALF * k, 640 - HALF * k)
        back_c[:, at] = wide_c[rows]
        fwd_r[:, at] = jnp.where(lane + k * HALF < w_r, wide_r[rows], none)
    for k in range(S // HALF):
        at = slice(k * HALF, (k + 1) * HALF)
        rows = slice(HALF - HALF * k, REACH - HALF * k)
        back_r[:, at] = tall_r[rows]
        fwd_c[:, at] = jnp.where(deep < w_c, tall_c[rows], none)


def table_scratch():
    return [
        pltpu.VMEM((BOX, S), BF16),
        pltpu.VMEM((S, BOX), BF16),
        pltpu.VMEM((S, BOX), BF16),
        pltpu.VMEM((BOX, S), BF16),
    ]


def forward(mass, tables, vb_ref):
    inner = dot(tables[2][...], vb_ref[...]).astype(BF16)
    return mass / dot(inner, tables[3][...])


def fetch(boxes, cells, ref, sems):
    copies = [
        pltpu.make_async_copy(boxes.at[0, j], ref.at[i], sems.at[i]) for i, j in enumerate(cells)
    ]
    for copy in copies:
        copy.start()
    return copies


def aligned_kernel(cells, later, shifts, widths, source, boxes, later_boxes, *refs):
    n = len(cells)
    if 0 in cells:
        tops, outs, refs = refs[:n], refs[n - 1 : n + 3], refs[n + 3 :]
        base_ref, later_ref, box_ref, refs = refs[0], refs[1], refs[2], refs[3:]
    else:
        base_ref, first_ref, outs, later_ref, refs = refs[0], refs[1], refs[2:4], refs[4], refs[5:]
        tops = [outs[0].at[:, pl.ds(S + i * S, S)] for i in range(n)]
        outs[0][:, :S] = first_ref[...]
        box_ref = boxes
    copies = [[] for _ in cells]
    if 0 in cells:
        mass_ref, vb_ref, tables, sems, later_sems = refs
        masses = [mass_ref.at[:, pl.ds(i * S, S)] for i in range(n)]
        for i, j in enumerate(cells):
            copies[i] += [
                pltpu.make_async_copy(source.at[:, pl.ds(j * S, S)], masses[i], sems.at[i, 1]),
                pltpu.make_async_copy(boxes.at[0, j], box_ref.at[i], sems.at[i, 0]),
            ]
    else:
        vb_ref, tables, later_sems = refs
        masses = [source.at[:, pl.ds(j * S, S)] for j in cells]
    for pair in copies:
        for copy in reversed(pair):
            copy.start()
    if 0 in cells:
        fill_base(base_ref)
    for i, j in enumerate(cells):
        fill_tables(
            shifts[0, 0, j], shifts[0, 1, j], widths[0, 0, j], widths[0, 1, j], base_ref, tables[i])
    scales = []
    for i in range(n):
        down = dot(tables[i][0][...], jnp.ones((S, HALF), BF16)).astype(BF16).astype(F32)
        across = dot(jnp.ones((8, S), BF16), tables[i][1][...])
        scales.append(((1.0 / down)[:, :1], (1.0 / across)[:1]))
    u = [None] * n
    for step in range(ITERS):
        for i in range(n):
            if step == 0:
                for copy in copies[i]:
                    copy.wait()
                if i == n - 1:
                    later_copies = fetch(later_boxes, later, later_ref, later_sems)
                down, across = scales[i]
                for c in range(0, BOX, HALF):
                    v = box_ref[i, c : c + HALF] * down[c : c + HALF] * across
                    vb_ref[i, c : c + HALF] = v.astype(BF16)
            else:
                inner = dot(tables[i][0][...], u[i].astype(BF16)).astype(BF16)
                vb_ref[i] = (box_ref[i] / dot(inner, tables[i][1][...])).astype(BF16)
        for i in range(n):
            u[i] = forward(masses[i][...], tables[i], vb_ref.at[i])
    for i, j in enumerate(cells):
        tops[i][:HALF, :S] = u[i][:HALF]
        if j == NC_CELLS - 1:
            tops[i][HALF:] = masses[i][:HALF]
        outs[1][:, i * S : (i + 1) * S] = u[i][HALF:]
        if j == 0:
            for k in range(2):
                outs[2 + k][:HALF] = u[i][k * HALF : (k + 1) * HALF, :HALF]
                outs[2 + k][HALF:] = masses[i][k * HALF : (k + 1) * HALF, :HALF]
    for copy in later_copies:
        copy.wait()


def cost(cells, applies):
    return pl.CostEstimate(
        flops=cells * applies * 804_000_000, bytes_accessed=cells << 20, transcendentals=0)


def aligned(cells, later, source, boxes, later_boxes, shifts, widths, *base):
    n = len(cells)
    corner = jax.ShapeDtypeStruct((S, HALF), F32)
    if 0 in cells:
        shapes = [jax.ShapeDtypeStruct((HALF, S), F32), jax.ShapeDtypeStruct((S, S), F32)]
    else:
        shapes = [jax.ShapeDtypeStruct((HALF, (n + 1) * S), F32)]
    shapes.append(jax.ShapeDtypeStruct((HALF, n * S), F32))
    scratch = []
    if 0 in cells:
        shapes += [corner, corner, jax.ShapeDtypeStruct((BASE, HALF), F32)]
        scratch += [pltpu.VMEM((n, BOX, BOX), F32), pltpu.VMEM((S, n * S), F32)]
    shapes.append(jax.ShapeDtypeStruct((len(later), BOX, BOX), F32))
    return pl.pallas_call(
        functools.partial(aligned_kernel, cells, later),
        in_specs=[SMEM, SMEM] + ([HBM, HBM] if 0 in cells else [VMEM, VMEM]) + [HBM] + [VMEM] * len(base),
        out_specs=[VMEM] * len(shapes),
        out_shape=shapes,
        scratch_shapes=scratch + [
            pltpu.VMEM((n, BOX, BOX), BF16),
            [table_scratch() for _ in cells],
        ] + [pltpu.SemaphoreType.DMA((n, 2))] * (0 in cells) + [
            pltpu.SemaphoreType.DMA((len(later),)),
        ],
        compiler_params=PARAMS,
        cost_estimate=cost(n, 5),
        name="aligned",
    )(shifts, widths, source, boxes, later_boxes, *base)


def place(plan_ref, top, left, canvas_ref, first):
    base = pl.multiple_of(top // 8 * 8, 8)
    rest = top - base
    row = lax.broadcasted_iota(jnp.int32, (HALF // 8 + 1, 8, BOX), 1)
    column = lax.broadcasted_iota(jnp.int32, (HALF + 8, HALF), 1)
    none = jnp.zeros((1, 8, BOX), F32)
    for c in range(0, BOX, HALF):
        turned = pltpu.roll(plan_ref[c : c + HALF].reshape(HALF // 8, 8, BOX), rest, 1)
        rows = jnp.where(
            row < rest,
            jnp.concatenate([none, turned], 0),
            jnp.concatenate([turned, none], 0),
        ).reshape(HALF + 8, BOX)
        before = jnp.zeros((HALF + 8, HALF), F32)
        for k in range(BOX // HALF + 1):
            now = jnp.zeros((HALF + 8, HALF), F32)
            if k < BOX // HALF:
                now = pltpu.roll(rows[:, k * HALF : (k + 1) * HALF], left, 1)
            at = (pl.ds(base + c, HALF + 8), slice(first + k * HALF, first + (k + 1) * HALF))
            canvas_ref[at] = canvas_ref[at] + jnp.where(column < left, before, now)
            before = now


def shifted_kernel(cells, later, origin, carried, finals, quads, count, shifts, widths, box_ref,
                   base_ref, *refs):
    n = len(cells)
    arrays, refs = refs[:count], refs[count:]
    if carried:
        carry_ref, upper_ref, refs = refs[0], refs[1], refs[2:]
    if later:
        later_boxes, refs = refs[0], refs[1:]
    canvas_ref, outs, refs = refs[0], refs[1:4], refs[4:]
    if later:
        later_ref, refs = refs[0], refs[1:]
    mass_ref, ub_ref, vb_ref, v_ref, tables, sems = refs
    later_copies = fetch(later_boxes, later, later_ref, sems) if later else []
    canvas_ref[...] = jnp.zeros_like(canvas_ref)
    if carried:
        first, last, start = carried
        canvas_ref[:, first - origin : last - origin] = carry_ref[
            :, first - start : last - start]
    for i, j in enumerate(cells):
        fill_tables(
            shifts[0, 0, j], shifts[0, 1, j], widths[0, 0, j], widths[0, 1, j], base_ref, tables[i])
        for k in range(4):
            rows = slice(k // 2 * HALF, (k // 2 + 1) * HALF)
            cols = slice(k % 2 * HALF, (k % 2 + 1) * HALF)
            for ref, (array, down, across) in (
                (ub_ref, quads[i][k]), (mass_ref, quads[i][4 + k])
            ):
                part = arrays[array][
                    down * HALF : (down + 1) * HALF, across * HALF : (across + 1) * HALF]
                ref[i, rows, cols] = part.astype(ref.dtype)
    u = [ub_ref[i] for i in range(n)]
    for step in range(ITERS):
        for i in range(n):
            inner = dot(tables[i][0][...], u[i]).astype(BF16)
            den = dot(inner, tables[i][1][...])
            v = box_ref[i] / den
            if step == ITERS - 1:
                v_ref[i] = v
            vb_ref[i] = v.astype(BF16)
        for i in range(n):
            u[i] = forward(mass_ref[i], tables[i], vb_ref.at[i]).astype(BF16)
    deep = lax.broadcasted_iota(jnp.int32, (BOX, S), 0)
    lane = lax.broadcasted_iota(jnp.int32, (S, BOX), 1)
    for i, j in enumerate(cells):
        inner = jnp.where(deep < widths[0, 0, j], dot(tables[i][0][...], u[i]), 0.0).astype(BF16)
        used = jnp.where(lane < widths[0, 1, j], tables[i][1][...], jnp.zeros((), BF16))
        v_ref[i] = v_ref[i] * dot(inner, used)
    for i, j in enumerate(cells):
        place(v_ref.at[i], shifts[0, 0, j] + HALF, shifts[0, 1, j] + HALF, canvas_ref,
              j * S - origin)
    at = 0
    for first, last in finals:
        for ref, row in zip(outs, (S - RADIUS, 2 * S - RADIUS, 0)):
            ref[:, at : at + last - first] = canvas_ref[
                row : row + ref.shape[0], first - origin : last - origin]
        at += last - first
    if carried and later:
        outs[2][:, at:] = upper_ref[...]
    for copy in later_copies:
        copy.wait()


def shifted(cells, later, boxes, later_boxes, shifts, widths, base, quads, carried=None,
            carry=(), finals=()):
    n = len(cells)
    origin = min(j * S for j in cells)
    width = max(j * S + REACH for j in cells) - origin
    total = sum(last - first for first, last in finals)
    upper = carry[1].shape[1] if carried and later else 0
    shapes = [
        jax.ShapeDtypeStruct((REACH + 8, width), F32),
        jax.ShapeDtypeStruct((NEXT, total), F32),
        jax.ShapeDtypeStruct((FAR, total), F32),
        jax.ShapeDtypeStruct((RADIUS, total + upper), F32),
    ]
    if later:
        shapes.append(jax.ShapeDtypeStruct((len(later), BOX, BOX), F32))
    arrays, where = [], []
    for j in cells:
        where.append([])
        for array, (down, across) in quads[j]:
            known = [k for k, other in enumerate(arrays) if other is array]
            if not known:
                known = [len(arrays)]
                arrays.append(array)
            where[-1].append((known[0], down, across))
    count = len(arrays)
    arrays += carry
    return pl.pallas_call(
        functools.partial(
            shifted_kernel, cells, later, origin, carried, finals, where, count),
        in_specs=[SMEM, SMEM, VMEM, VMEM] + [VMEM] * len(arrays) + [HBM] * bool(later),
        out_specs=[VMEM] * len(shapes),
        out_shape=shapes,
        scratch_shapes=[
            pltpu.VMEM((n, S, S), F32),
            pltpu.VMEM((n, S, S), BF16),
            pltpu.VMEM((n, BOX, BOX), BF16),
            pltpu.VMEM((n, BOX, BOX), F32),
            [table_scratch() for _ in cells],
            pltpu.SemaphoreType.DMA((max(1, len(later)),)),
        ],
        compiler_params=PARAMS,
        cost_estimate=cost(n, 7),
        name="shifted",
    )(shifts, widths, boxes, base, *arrays, *([later_boxes] if later else []))


def blur_weights():
    raw = [math.exp(-(d * d) / (2.0 * SIGMA * SIGMA)) for d in range(-RADIUS, RADIUS + 1)]
    total = sum(raw)
    return [w / total for w in raw]


def blurred_rows(own, next_ref, far_ref, back_ref, win_ref, width, put):
    win_ref[:, :width] = next_ref[...]
    at = 0
    for part in own:
        cols = slice(at, at + part.shape[1])
        win_ref[RADIUS:, cols] = win_ref[RADIUS:, cols] + part[...]
        at += part.shape[1]
    win_ref[:FAR, :width] = win_ref[:FAR, :width] + far_ref[...]
    win_ref[NEXT - RADIUS :, :width] = win_ref[NEXT - RADIUS :, :width] + back_ref[...]
    weights = blur_weights()
    for c in range(0, width, HALF):
        col = win_ref[:, c : c + HALF]
        out = weights[RADIUS] * col[RADIUS : RADIUS + S]
        for d in range(1, RADIUS + 1):
            out = out + weights[RADIUS + d] * (
                col[RADIUS + d : RADIUS + d + S] + col[RADIUS - d : RADIUS - d + S])
        put(c, out)


def edges_kernel(*refs):
    (canvas3, next3, far3, canvas2, next2, far2, back2, main_ref, right_ref, east_ref, west_ref,
     win_ref) = refs

    def outer(c, out):
        east_ref[:S, HALF + c : 2 * HALF + c] = out

    def inner(c, out):
        if c < 3 * HALF:
            main_ref[:, c : c + HALF] = out
        else:
            east_ref[:S, :HALF] = out
            right_ref[...] = out
        if c == 0:
            west_ref[...] = out.T[:RADIUS]
        if c == 2 * HALF:
            east_ref[S:, :S] = out.T[HALF - RADIUS :]
            east_ref[S:, S:] = jnp.zeros((RADIUS, HALF), F32)

    own3 = [canvas3.at[:OWN, 3 * HALF :]]
    own2 = [canvas2.at[:OWN, :S], canvas2.at[:OWN, 7 * HALF :]]
    blurred_rows(own3, next3, far3, back2.at[:, 2 * S :], win_ref, S, outer)
    blurred_rows(own2, next2, far2, back2.at[:, : 2 * S], win_ref, 2 * S, inner)


def edges(*arrays):
    return pl.pallas_call(
        edges_kernel,
        in_specs=[VMEM] * 7,
        out_specs=[VMEM] * 4,
        out_shape=[
            jax.ShapeDtypeStruct((S, 3 * HALF), F32),
            jax.ShapeDtypeStruct((S, HALF), F32),
            jax.ShapeDtypeStruct((S + RADIUS, 3 * HALF), F32),
            jax.ShapeDtypeStruct((RADIUS, S), F32),
        ],
        scratch_shapes=[pltpu.VMEM((NEXT, 2 * S), F32)],
        compiler_params=PARAMS,
        name="edges",
    )(*arrays)


def band():
    full = np.zeros((2 * S, S), np.float64)
    for j in range(S):
        for d, w in zip(range(-RADIUS, RADIUS + 1), blur_weights()):
            full[j + HALF + d, j] = w
    high = full.astype(jnp.bfloat16)
    return high, (full - high.astype(np.float64)).astype(jnp.bfloat16)


def final_kernel(canvas1, next1, far1, back1, main_ref, right_ref, east_ref, west_ref, high_ref,
                 low_ref, out_ref, rows_ref, win_ref, done_ref, sems):
    span = out_ref.shape[1]
    none = jnp.zeros((HALF - RADIUS, S), F32)
    win_ref[:, :HALF] = jnp.concatenate([none, east_ref[S:, :S]], 0).T
    win_ref[:, HALF : HALF + S] = main_ref[:, :S] + east_ref[:S, :S]
    win_ref[:, HALF + 7 * HALF : HALF + span] = main_ref[:, S:]
    win_ref[:, HALF + span :] = right_ref[...] + jnp.concatenate([west_ref[...], none], 0).T

    def middle(c, out):
        if c == 0:
            out = out + east_ref[:S, S:]
        win_ref[:, HALF + S + c : 2 * HALF + S + c] = out

    blurred_rows([canvas1.at[:OWN]], next1, far1, back1, rows_ref, REACH, middle)
    copies = []
    for c in range(0, span, S):
        strip = win_ref[:, c : c + 2 * S]
        high = strip.astype(BF16)
        low = (strip - high.astype(F32)).astype(BF16)
        done_ref[:, c : c + S] = (
            dot(high, high_ref[...]) + dot(high, low_ref[...]) + dot(low, high_ref[...]))
        copies.append(pltpu.make_async_copy(
            done_ref.at[:, pl.ds(c, S)], out_ref.at[:, pl.ds(c, S)], sems.at[c // S]))
        copies[-1].start()
    for copy in copies:
        copy.wait()


def final(span, *arrays):
    high, low = band()
    return pl.pallas_call(
        final_kernel,
        in_specs=[VMEM] * 10,
        out_specs=ANY,
        out_shape=jax.ShapeDtypeStruct((S, span), F32),
        scratch_shapes=[
            pltpu.VMEM((NEXT, REACH), F32),
            pltpu.VMEM((S, span + 2 * HALF), F32),
            pltpu.VMEM((S, span), F32),
            pltpu.SemaphoreType.DMA((span // S,)),
        ],
        compiler_params=PARAMS,
        name="final",
    )(*arrays, jnp.asarray(high), jnp.asarray(low))


def moved(array, by_row, by_col):
    n_row, n_col = lax.axis_size("row"), lax.axis_size("col")
    if by_col == 0:
        return lax.ppermute(array, "row", [(i, (i + by_row) % n_row) for i in range(n_row)])
    if by_row == 0:
        return lax.ppermute(array, "col", [(i, (i + by_col) % n_col) for i in range(n_col)])
    pairs = [
        (r * n_col + c, (r + by_row) % n_row * n_col + (c + by_col) % n_col)
        for r in range(n_row)
        for c in range(n_col)
    ]
    return lax.ppermute(array, ("row", "col"), pairs)


def spilled(parts):
    own, after, far, back = parts
    return own, moved(after, 1, 0), moved(far, 2, 0), moved(back, -1, 0)


def behind(array, *others):
    return lax.optimization_barrier((array, *others))[0]


def on_device(source, boxes_a, shifts_a, widths_a, boxes_b, shifts_b, widths_b):
    shifts_a, widths_a, shifts_b, widths_b = (
        jnp.swapaxes(array, 1, 2) for array in (shifts_a, widths_a, shifts_b, widths_b))
    boxes_a = pltpu.with_memory_space_constraint(boxes_a, pltpu.HBM)
    boxes_b = pltpu.with_memory_space_constraint(boxes_b, pltpu.HBM)
    masses = pltpu.with_memory_space_constraint(source, pltpu.HBM)
    shifts_a = pltpu.with_memory_space_constraint(shifts_a, pltpu.HBM)
    widths_a = pltpu.with_memory_space_constraint(widths_a, pltpu.HBM)
    rmass = moved(source[:HALF, : (NC_CELLS - 1) * S], -1, 0)
    top0, top3, bot03, left_top, left_bot, base, boxes12 = aligned(
        (0, 3), (1, 2), masses, boxes_a, boxes_a, shifts_a, widths_a)
    rtop3 = moved(top3, -1, 0)
    east = moved(left_bot, 0, -1)
    diag = moved(left_top, -1, -1)
    top012, bot12, boxes3 = aligned(
        (1, 2), (3,), source, boxes12, boxes_b, shifts_a, widths_a, behind(base, rmass), top0)
    rtop012 = moved(top012, -1, 0)
    own = [(bot03, 0), (bot03, 1), (bot12, 0), (bot12, 1), (bot12, 2), (bot12, 3), (bot03, 2),
           (bot03, 3), (east, 0)]
    below = [(rtop012, k) for k in range(6)] + [(rtop3, 0), (rtop3, 1), (diag, 0)]
    mass = [(rmass, (0, k)) for k in range(6)] + [
        (rtop3, (1, 0)), (rtop3, (1, 1)), (diag, (1, 0))]
    quads = {}
    for j in range(NC_CELLS):
        a, b = 2 * j + 1, 2 * j + 2
        quads[j] = [(array, (0, at)) for array, at in (own[a], own[b], below[a], below[b])]
        quads[j] += [
            (source, (1, a)),
            (source, (1, b)) if j < NC_CELLS - 1 else (east, (1, 0)),
            mass[a],
            mass[b],
        ]
    canvas3, next3, far3, back3, boxes02 = shifted(
        (3,), (0, 2), boxes3, boxes_b, shifts_b, widths_b, base, quads,
        finals=((1152, 1408),))
    next3 = moved(next3, 1, 0)
    far3 = moved(far3, 2, 0)
    canvas2, next2, far2, back2, boxes1 = shifted(
        (0, 2), (1,), boxes02, boxes_b, shifts_b, widths_b, base, quads,
        carried=(768, 1152, 768), carry=(canvas3, back3), finals=((0, 256), (896, 1152)))
    next2 = moved(next2, 1, 0)
    far2 = moved(far2, 2, 0)
    rback2 = moved(back2, -1, 0)
    canvas1, next1, far1, back1 = shifted(
        (1,), (), boxes1, None, shifts_b, widths_b, base, quads,
        carried=(256, 896, 0), carry=(behind(canvas2, next3, far3), back3),
        finals=((256, 896),))
    n_row = lax.axis_size("row")
    joined = lax.ppermute(
        behind(far1, rback2), "row", [(i, i + 1) for i in range(0, n_row, 2)])
    far1 = lax.ppermute(far1, "row", [(i, (i + 2) % n_row) for i in range(1, n_row, 2)])
    back1 = moved(back1, -1, 0)
    next1 = moved(next1.at[:FAR].add(behind(joined, next2, far2)), 1, 0)
    main, right, east, west = edges(canvas3, next3, far3, canvas2, next2, far2, rback2)
    return final(
        source.shape[1], canvas1, next1, far1, back1, main, right, moved(east, 0, 1),
        moved(west, 0, -1))


def solution(mesh):
    cells = P("row", "col", None)
    boxes = P("row", "col", None, None)
    return jax.shard_map(
        on_device,
        mesh=mesh,
        in_specs=(P("row", "col"), boxes, cells, cells, boxes, cells, cells),
        out_specs=P("row", "col"),
        check_vma=False,
    )
```

```python
import functools
import math

import jax
import jax.numpy as jnp
import numpy as np
from jax import lax
from jax.experimental import pallas as pl
from jax.experimental.pallas import tpu as pltpu
from jax.sharding import PartitionSpec as P

S = 256
HALF = 128
BOX = 512
ITERS = 3
RADIUS = 8
REACH = BOX + HALF
EPS = 0.05
SIGMA = 2.0
F32 = jnp.float32
BF16 = jnp.bfloat16
OWN = S + RADIUS
NEXT = S + 2 * RADIUS
NC_CELLS = 4
FAR = REACH - 2 * S + RADIUS
BASE = 904
VMEM = pl.BlockSpec(memory_space=pltpu.VMEM)
SMEM = pl.BlockSpec(memory_space=pltpu.SMEM)
ANY = pl.BlockSpec(memory_space=pl.ANY)
HBM = pl.BlockSpec(memory_space=pltpu.HBM)
PARAMS = pltpu.CompilerParams(vmem_limit_bytes=24 << 20)


def dot(a, b):
    return jnp.dot(a, b, preferred_element_type=F32)


def fill_base(ref):
    for c in range(0, BASE, 8 * 28):
        n = min(8 * 28, BASE - c)
        rows = lax.broadcasted_iota(jnp.int32, (n, HALF), 0)
        cols = lax.broadcasted_iota(jnp.int32, (n, HALF), 1)
        dist = (rows - cols + (c - 384)).astype(F32) / S
        ref[c : c + n] = jnp.exp(-dist * dist / EPS)


def window(ref, start):
    base = pl.multiple_of(start // 8 * 8, 8)
    rest = start - base
    tiles = ref[pl.ds(base, REACH + 8), :].reshape(REACH // 8 + 1, 8, HALF)
    tiles = pltpu.roll(tiles, jnp.where(rest == 0, 0, 8 - rest), 1)
    row = lax.broadcasted_iota(jnp.int32, (REACH // 8, 8, HALF), 1)
    return jnp.where(row < 8 - rest, tiles[:-1], tiles[1:]).reshape(REACH, HALF).astype(BF16)


def fill_tables(o_r, o_c, w_r, w_c, base_ref, refs):
    back_r, back_c, fwd_r, fwd_c = refs
    tall_r = window(base_ref, o_r + S)
    tall_c = window(base_ref, o_c + S)
    wide_r = window(base_ref, -o_r)
    wide_c = window(base_ref, -o_c)
    none = jnp.zeros((), BF16)
    lane = lax.broadcasted_iota(jnp.int32, (S, HALF), 1)
    deep = lax.broadcasted_iota(jnp.int32, (BOX, HALF), 0)
    for k in range(BOX // HALF):
        at = slice(k * HALF, (k + 1) * HALF)
        rows = slice(384 - HALF * k, 640 - HALF * k)
        back_c[:, at] = wide_c[rows]
        fwd_r[:, at] = jnp.where(lane + k * HALF < w_r, wide_r[rows], none)
    for k in range(S // HALF):
        at = slice(k * HALF, (k + 1) * HALF)
        rows = slice(HALF - HALF * k, REACH - HALF * k)
        back_r[:, at] = tall_r[rows]
        fwd_c[:, at] = jnp.where(deep < w_c, tall_c[rows], none)


def table_scratch():
    return [
        pltpu.VMEM((BOX, S), BF16),
        pltpu.VMEM((S, BOX), BF16),
        pltpu.VMEM((S, BOX), BF16),
        pltpu.VMEM((BOX, S), BF16),
    ]


def forward(mass, tables, vb_ref):
    inner = dot(tables[2][...], vb_ref[...]).astype(BF16)
    return mass / dot(inner, tables[3][...])


def fetch(boxes, cells, ref, sems):
    copies = [
        pltpu.make_async_copy(boxes.at[0, j], ref.at[i], sems.at[i]) for i, j in enumerate(cells)
    ]
    for copy in copies:
        copy.start()
    return copies


def aligned_kernel(cells, later, shifts, widths, source, boxes, later_boxes, *refs):
    n = len(cells)
    if 0 in cells:
        tops, outs, refs = refs[:n], refs[n - 1 : n + 3], refs[n + 3 :]
        base_ref, later_ref, box_ref, refs = refs[0], refs[1], refs[2], refs[3:]
    else:
        base_ref, first_ref, outs, later_ref, refs = refs[0], refs[1], refs[2:4], refs[4], refs[5:]
        tops = [outs[0].at[:, pl.ds(S + i * S, S)] for i in range(n)]
        outs[0][:, :S] = first_ref[...]
        box_ref = boxes
    copies = [[] for _ in cells]
    if 0 in cells:
        mass_ref, vb_ref, tables, sems, later_sems = refs
        masses = [mass_ref.at[:, pl.ds(i * S, S)] for i in range(n)]
        for i, j in enumerate(cells):
            copies[i] += [
                pltpu.make_async_copy(source.at[:, pl.ds(j * S, S)], masses[i], sems.at[i, 1]),
                pltpu.make_async_copy(boxes.at[0, j], box_ref.at[i], sems.at[i, 0]),
            ]
    else:
        vb_ref, tables, later_sems = refs
        masses = [source.at[:, pl.ds(j * S, S)] for j in cells]
    for pair in copies:
        for copy in reversed(pair):
            copy.start()
    if 0 in cells:
        fill_base(base_ref)
    for i, j in enumerate(cells):
        fill_tables(
            shifts[0, 0, j], shifts[0, 1, j], widths[0, 0, j], widths[0, 1, j], base_ref, tables[i])
    scales = []
    for i in range(n):
        down = dot(tables[i][0][...], jnp.ones((S, HALF), BF16)).astype(BF16).astype(F32)
        across = dot(jnp.ones((8, S), BF16), tables[i][1][...])
        scales.append(((1.0 / down)[:, :1], (1.0 / across)[:1]))
    u = [None] * n
    for step in range(ITERS):
        for i in range(n):
            if step == 0:
                for copy in copies[i]:
                    copy.wait()
                if i == n - 1:
                    later_copies = fetch(later_boxes, later, later_ref, later_sems)
                down, across = scales[i]
                for c in range(0, BOX, HALF):
                    v = box_ref[i, c : c + HALF] * down[c : c + HALF] * across
                    vb_ref[i, c : c + HALF] = v.astype(BF16)
            else:
                inner = dot(tables[i][0][...], u[i].astype(BF16)).astype(BF16)
                vb_ref[i] = (box_ref[i] / dot(inner, tables[i][1][...])).astype(BF16)
        for i in range(n):
            u[i] = forward(masses[i][...], tables[i], vb_ref.at[i])
    for i, j in enumerate(cells):
        tops[i][:HALF, :S] = u[i][:HALF]
        if j == NC_CELLS - 1:
            tops[i][HALF:] = masses[i][:HALF]
        outs[1][:, i * S : (i + 1) * S] = u[i][HALF:]
        if j == 0:
            for k in range(2):
                outs[2 + k][:HALF] = u[i][k * HALF : (k + 1) * HALF, :HALF]
                outs[2 + k][HALF:] = masses[i][k * HALF : (k + 1) * HALF, :HALF]
    for copy in later_copies:
        copy.wait()


def cost(cells, applies):
    return pl.CostEstimate(
        flops=cells * applies * 300_000_000, bytes_accessed=cells << 20, transcendentals=0)


def aligned(cells, later, source, boxes, later_boxes, shifts, widths, *base):
    n = len(cells)
    corner = jax.ShapeDtypeStruct((S, HALF), F32)
    if 0 in cells:
        shapes = [jax.ShapeDtypeStruct((HALF, S), F32), jax.ShapeDtypeStruct((S, S), F32)]
    else:
        shapes = [jax.ShapeDtypeStruct((HALF, (n + 1) * S), F32)]
    shapes.append(jax.ShapeDtypeStruct((HALF, n * S), F32))
    scratch = []
    if 0 in cells:
        shapes += [corner, corner, jax.ShapeDtypeStruct((BASE, HALF), F32)]
        scratch += [pltpu.VMEM((n, BOX, BOX), F32), pltpu.VMEM((S, n * S), F32)]
    shapes.append(jax.ShapeDtypeStruct((len(later), BOX, BOX), F32))
    return pl.pallas_call(
        functools.partial(aligned_kernel, cells, later),
        in_specs=[SMEM, SMEM] + ([HBM, HBM] if 0 in cells else [VMEM, VMEM]) + [HBM] + [VMEM] * len(base),
        out_specs=[VMEM] * len(shapes),
        out_shape=shapes,
        scratch_shapes=scratch + [
            pltpu.VMEM((n, BOX, BOX), BF16),
            [table_scratch() for _ in cells],
        ] + [pltpu.SemaphoreType.DMA((n, 2))] * (0 in cells) + [
            pltpu.SemaphoreType.DMA((len(later),)),
        ],
        compiler_params=PARAMS,
        cost_estimate=cost(n, 13),
        name="aligned",
    )(shifts, widths, source, boxes, later_boxes, *base)


def place(plan_ref, top, left, canvas_ref, first):
    base = pl.multiple_of(top // 8 * 8, 8)
    rest = top - base
    row = lax.broadcasted_iota(jnp.int32, (HALF // 8 + 1, 8, BOX), 1)
    column = lax.broadcasted_iota(jnp.int32, (HALF + 8, HALF), 1)
    none = jnp.zeros((1, 8, BOX), F32)
    for c in range(0, BOX, HALF):
        turned = pltpu.roll(plan_ref[c : c + HALF].reshape(HALF // 8, 8, BOX), rest, 1)
        rows = jnp.where(
            row < rest,
            jnp.concatenate([none, turned], 0),
            jnp.concatenate([turned, none], 0),
        ).reshape(HALF + 8, BOX)
        before = jnp.zeros((HALF + 8, HALF), F32)
        for k in range(BOX // HALF + 1):
            now = jnp.zeros((HALF + 8, HALF), F32)
            if k < BOX // HALF:
                now = pltpu.roll(rows[:, k * HALF : (k + 1) * HALF], left, 1)
            at = (pl.ds(base + c, HALF + 8), slice(first + k * HALF, first + (k + 1) * HALF))
            canvas_ref[at] = canvas_ref[at] + jnp.where(column < left, before, now)
            before = now


def shifted_kernel(cells, later, origin, carried, finals, quads, count, shifts, widths, box_ref,
                   base_ref, *refs):
    n = len(cells)
    arrays, refs = refs[:count], refs[count:]
    if carried:
        carry_ref, upper_ref, refs = refs[0], refs[1], refs[2:]
    if later:
        later_boxes, refs = refs[0], refs[1:]
    canvas_ref, outs, refs = refs[0], refs[1:4], refs[4:]
    if later:
        later_ref, refs = refs[0], refs[1:]
    mass_ref, ub_ref, vb_ref, v_ref, tables, sems = refs
    later_copies = fetch(later_boxes, later, later_ref, sems) if later else []
    canvas_ref[...] = jnp.zeros_like(canvas_ref)
    if carried:
        first, last, start = carried
        canvas_ref[:, first - origin : last - origin] = carry_ref[
            :, first - start : last - start]
    for i, j in enumerate(cells):
        fill_tables(
            shifts[0, 0, j], shifts[0, 1, j], widths[0, 0, j], widths[0, 1, j], base_ref, tables[i])
        for k in range(4):
            rows = slice(k // 2 * HALF, (k // 2 + 1) * HALF)
            cols = slice(k % 2 * HALF, (k % 2 + 1) * HALF)
            for ref, (array, down, across) in (
                (ub_ref, quads[i][k]), (mass_ref, quads[i][4 + k])
            ):
                part = arrays[array][
                    down * HALF : (down + 1) * HALF, across * HALF : (across + 1) * HALF]
                ref[i, rows, cols] = part.astype(ref.dtype)
    u = [ub_ref[i] for i in range(n)]
    for step in range(ITERS):
        for i in range(n):
            inner = dot(tables[i][0][...], u[i]).astype(BF16)
            den = dot(inner, tables[i][1][...])
            v = box_ref[i] / den
            if step == ITERS - 1:
                v_ref[i] = v
            vb_ref[i] = v.astype(BF16)
        for i in range(n):
            u[i] = forward(mass_ref[i], tables[i], vb_ref.at[i]).astype(BF16)
    deep = lax.broadcasted_iota(jnp.int32, (BOX, S), 0)
    lane = lax.broadcasted_iota(jnp.int32, (S, BOX), 1)
    for i, j in enumerate(cells):
        inner = jnp.where(deep < widths[0, 0, j], dot(tables[i][0][...], u[i]), 0.0).astype(BF16)
        used = jnp.where(lane < widths[0, 1, j], tables[i][1][...], jnp.zeros((), BF16))
        v_ref[i] = v_ref[i] * dot(inner, used)
    for i, j in enumerate(cells):
        place(v_ref.at[i], shifts[0, 0, j] + HALF, shifts[0, 1, j] + HALF, canvas_ref,
              j * S - origin)
    at = 0
    for first, last in finals:
        for ref, row in zip(outs, (S - RADIUS, 2 * S - RADIUS, 0)):
            ref[:, at : at + last - first] = canvas_ref[
                row : row + ref.shape[0], first - origin : last - origin]
        at += last - first
    if carried and later:
        outs[2][:, at:] = upper_ref[...]
    for copy in later_copies:
        copy.wait()


def shifted(cells, later, boxes, later_boxes, shifts, widths, base, quads, carried=None,
            carry=(), finals=()):
    n = len(cells)
    origin = min(j * S for j in cells)
    width = max(j * S + REACH for j in cells) - origin
    total = sum(last - first for first, last in finals)
    upper = carry[1].shape[1] if carried and later else 0
    shapes = [
        jax.ShapeDtypeStruct((REACH + 8, width), F32),
        jax.ShapeDtypeStruct((NEXT, total), F32),
        jax.ShapeDtypeStruct((FAR, total), F32),
        jax.ShapeDtypeStruct((RADIUS, total + upper), F32),
    ]
    if later:
        shapes.append(jax.ShapeDtypeStruct((len(later), BOX, BOX), F32))
    arrays, where = [], []
    for j in cells:
        where.append([])
        for array, (down, across) in quads[j]:
            known = [k for k, other in enumerate(arrays) if other is array]
            if not known:
                known = [len(arrays)]
                arrays.append(array)
            where[-1].append((known[0], down, across))
    count = len(arrays)
    arrays += carry
    return pl.pallas_call(
        functools.partial(
            shifted_kernel, cells, later, origin, carried, finals, where, count),
        in_specs=[SMEM, SMEM, VMEM, VMEM] + [VMEM] * len(arrays) + [HBM] * bool(later),
        out_specs=[VMEM] * len(shapes),
        out_shape=shapes,
        scratch_shapes=[
            pltpu.VMEM((n, S, S), F32),
            pltpu.VMEM((n, S, S), BF16),
            pltpu.VMEM((n, BOX, BOX), BF16),
            pltpu.VMEM((n, BOX, BOX), F32),
            [table_scratch() for _ in cells],
            pltpu.SemaphoreType.DMA((max(1, len(later)),)),
        ],
        compiler_params=PARAMS,
        cost_estimate=cost(n, 19 if later else 7),
        name="shifted",
    )(shifts, widths, boxes, base, *arrays, *([later_boxes] if later else []))


def blur_weights():
    raw = [math.exp(-(d * d) / (2.0 * SIGMA * SIGMA)) for d in range(-RADIUS, RADIUS + 1)]
    total = sum(raw)
    return [w / total for w in raw]


def blurred_rows(own, next_ref, far_ref, back_ref, win_ref, width, put):
    win_ref[:, :width] = next_ref[...]
    at = 0
    for part in own:
        cols = slice(at, at + part.shape[1])
        win_ref[RADIUS:, cols] = win_ref[RADIUS:, cols] + part[...]
        at += part.shape[1]
    win_ref[:FAR, :width] = win_ref[:FAR, :width] + far_ref[...]
    win_ref[NEXT - RADIUS :, :width] = win_ref[NEXT - RADIUS :, :width] + back_ref[...]
    weights = blur_weights()
    for c in range(0, width, HALF):
        col = win_ref[:, c : c + HALF]
        out = weights[RADIUS] * col[RADIUS : RADIUS + S]
        for d in range(1, RADIUS + 1):
            out = out + weights[RADIUS + d] * (
                col[RADIUS + d : RADIUS + d + S] + col[RADIUS - d : RADIUS - d + S])
        put(c, out)


def edges_kernel(*refs):
    (canvas3, next3, far3, canvas2, next2, far2, back2, main_ref, right_ref, east_ref, west_ref,
     win_ref) = refs

    def outer(c, out):
        east_ref[:S, HALF + c : 2 * HALF + c] = out

    def inner(c, out):
        if c < 3 * HALF:
            main_ref[:, c : c + HALF] = out
        else:
            east_ref[:S, :HALF] = out
            right_ref[...] = out
        if c == 0:
            west_ref[...] = out.T[:RADIUS]
        if c == 2 * HALF:
            east_ref[S:, :S] = out.T[HALF - RADIUS :]
            east_ref[S:, S:] = jnp.zeros((RADIUS, HALF), F32)

    own3 = [canvas3.at[:OWN, 3 * HALF :]]
    own2 = [canvas2.at[:OWN, :S], canvas2.at[:OWN, 7 * HALF :]]
    blurred_rows(own3, next3, far3, back2.at[:, 2 * S :], win_ref, S, outer)
    blurred_rows(own2, next2, far2, back2.at[:, : 2 * S], win_ref, 2 * S, inner)


def edges(*arrays):
    return pl.pallas_call(
        edges_kernel,
        in_specs=[VMEM] * 7,
        out_specs=[VMEM] * 4,
        out_shape=[
            jax.ShapeDtypeStruct((S, 3 * HALF), F32),
            jax.ShapeDtypeStruct((S, HALF), F32),
            jax.ShapeDtypeStruct((S + RADIUS, 3 * HALF), F32),
            jax.ShapeDtypeStruct((RADIUS, S), F32),
        ],
        scratch_shapes=[pltpu.VMEM((NEXT, 2 * S), F32)],
        compiler_params=PARAMS,
        name="edges",
    )(*arrays)


def band():
    full = np.zeros((2 * S, S), np.float64)
    for j in range(S):
        for d, w in zip(range(-RADIUS, RADIUS + 1), blur_weights()):
            full[j + HALF + d, j] = w
    high = full.astype(jnp.bfloat16)
    return high, (full - high.astype(np.float64)).astype(jnp.bfloat16)


def final_kernel(canvas1, next1, far1, back1, main_ref, right_ref, east_ref, west_ref, high_ref,
                 low_ref, out_ref, rows_ref, win_ref, done_ref, sems):
    span = out_ref.shape[1]
    none = jnp.zeros((HALF - RADIUS, S), F32)
    win_ref[:, :HALF] = jnp.concatenate([none, east_ref[S:, :S]], 0).T
    win_ref[:, HALF : HALF + S] = main_ref[:, :S] + east_ref[:S, :S]
    win_ref[:, HALF + 7 * HALF : HALF + span] = main_ref[:, S:]
    win_ref[:, HALF + span :] = right_ref[...] + jnp.concatenate([west_ref[...], none], 0).T

    def middle(c, out):
        if c == 0:
            out = out + east_ref[:S, S:]
        win_ref[:, HALF + S + c : 2 * HALF + S + c] = out

    blurred_rows([canvas1.at[:OWN]], next1, far1, back1, rows_ref, REACH, middle)
    copies = []
    for c in range(0, span, S):
        strip = win_ref[:, c : c + 2 * S]
        high = strip.astype(BF16)
        low = (strip - high.astype(F32)).astype(BF16)
        done_ref[:, c : c + S] = (
            dot(high, high_ref[...]) + dot(high, low_ref[...]) + dot(low, high_ref[...]))
        copies.append(pltpu.make_async_copy(
            done_ref.at[:, pl.ds(c, S)], out_ref.at[:, pl.ds(c, S)], sems.at[c // S]))
        copies[-1].start()
    for copy in copies:
        copy.wait()


def final(span, *arrays):
    high, low = band()
    return pl.pallas_call(
        final_kernel,
        in_specs=[VMEM] * 10,
        out_specs=ANY,
        out_shape=jax.ShapeDtypeStruct((S, span), F32),
        scratch_shapes=[
            pltpu.VMEM((NEXT, REACH), F32),
            pltpu.VMEM((S, span + 2 * HALF), F32),
            pltpu.VMEM((S, span), F32),
            pltpu.SemaphoreType.DMA((span // S,)),
        ],
        compiler_params=PARAMS,
        name="final",
    )(*arrays, jnp.asarray(high), jnp.asarray(low))


def moved(array, by_row, by_col):
    n_row, n_col = lax.axis_size("row"), lax.axis_size("col")
    if by_col == 0:
        return lax.ppermute(array, "row", [(i, (i + by_row) % n_row) for i in range(n_row)])
    if by_row == 0:
        return lax.ppermute(array, "col", [(i, (i + by_col) % n_col) for i in range(n_col)])
    pairs = [
        (r * n_col + c, (r + by_row) % n_row * n_col + (c + by_col) % n_col)
        for r in range(n_row)
        for c in range(n_col)
    ]
    return lax.ppermute(array, ("row", "col"), pairs)


def spilled(parts):
    own, after, far, back = parts
    return own, moved(after, 1, 0), moved(far, 2, 0), moved(back, -1, 0)


def behind(array, *others):
    return lax.optimization_barrier((array, *others))[0]


def on_device(source, boxes_a, shifts_a, widths_a, boxes_b, shifts_b, widths_b):
    shifts_a, widths_a, shifts_b, widths_b = (
        jnp.swapaxes(array, 1, 2) for array in (shifts_a, widths_a, shifts_b, widths_b))
    boxes_a = pltpu.with_memory_space_constraint(boxes_a, pltpu.HBM)
    boxes_b = pltpu.with_memory_space_constraint(boxes_b, pltpu.HBM)
    masses = pltpu.with_memory_space_constraint(source, pltpu.HBM)
    shifts_a = pltpu.with_memory_space_constraint(shifts_a, pltpu.HBM)
    widths_a = pltpu.with_memory_space_constraint(widths_a, pltpu.HBM)
    rmass = moved(source[:HALF, : (NC_CELLS - 1) * S], -1, 0)
    top0, top3, bot03, left_top, left_bot, base, boxes12 = aligned(
        (0, 3), (1, 2), masses, boxes_a, boxes_a, shifts_a, widths_a)
    rtop3 = moved(top3, -1, 0)
    east = moved(left_bot, 0, -1)
    diag = moved(left_top, -1, -1)
    top012, bot12, boxes3 = aligned(
        (1, 2), (3,), source, boxes12, boxes_b, shifts_a, widths_a, behind(base, rmass), top0)
    rtop012 = moved(top012, -1, 0)
    own = [(bot03, 0), (bot03, 1), (bot12, 0), (bot12, 1), (bot12, 2), (bot12, 3), (bot03, 2),
           (bot03, 3), (east, 0)]
    below = [(rtop012, k) for k in range(6)] + [(rtop3, 0), (rtop3, 1), (diag, 0)]
    mass = [(rmass, (0, k)) for k in range(6)] + [
        (rtop3, (1, 0)), (rtop3, (1, 1)), (diag, (1, 0))]
    quads = {}
    for j in range(NC_CELLS):
        a, b = 2 * j + 1, 2 * j + 2
        quads[j] = [(array, (0, at)) for array, at in (own[a], own[b], below[a], below[b])]
        quads[j] += [
            (source, (1, a)),
            (source, (1, b)) if j < NC_CELLS - 1 else (east, (1, 0)),
            mass[a],
            mass[b],
        ]
    canvas3, next3, far3, back3, boxes02 = shifted(
        (3,), (0, 2), boxes3, boxes_b, shifts_b, widths_b, base, quads,
        finals=((1152, 1408),))
    next3 = moved(next3, 1, 0)
    far3 = moved(far3, 2, 0)
    canvas2, next2, far2, back2, boxes1 = shifted(
        (0, 2), (1,), boxes02, boxes_b, shifts_b, widths_b, base, quads,
        carried=(768, 1152, 768), carry=(canvas3, back3), finals=((0, 256), (896, 1152)))
    next2 = moved(next2, 1, 0)
    far2 = moved(far2, 2, 0)
    rback2 = moved(back2, -1, 0)
    canvas1, next1, far1, back1 = shifted(
        (1,), (), boxes1, None, shifts_b, widths_b, base, quads,
        carried=(256, 896, 0), carry=(behind(canvas2, next3, far3), back3),
        finals=((256, 896),))
    n_row = lax.axis_size("row")
    joined = lax.ppermute(
        behind(far1, far2), "row", [(i, i + 1) for i in range(0, n_row, 2)])
    far1 = lax.ppermute(far1, "row", [(i, (i + 2) % n_row) for i in range(1, n_row, 2)])
    back1 = moved(back1, -1, 0)
    next1 = moved(next1.at[:FAR].add(behind(joined, next2, rback2)), 1, 0)
    main, right, east, west = edges(canvas3, next3, far3, canvas2, next2, far2, rback2)
    return final(
        source.shape[1], canvas1, next1, far1, back1, main, right, moved(east, 0, 1),
        moved(west, 0, -1))


def solution(mesh):
    cells = P("row", "col", None)
    boxes = P("row", "col", None, None)
    return jax.shard_map(
        on_device,
        mesh=mesh,
        in_specs=(P("row", "col"), boxes, cells, cells, boxes, cells, cells),
        out_specs=P("row", "col"),
        check_vma=False,
    )
```
